256 devices in a mesh: row: 8 (over z_hi, x), col: 32 (over z_lo, y, core).
Axes of the slice: x: 4, y: 4, z: 8 (z_hi: 2, z_lo: 4; z = z_hi * 4 + z_lo), core: 2. Of those that a mesh axis runs over, the one named last changes fastest.
Arguments:
- features: float32 [65536, 128], P(('row', 'col')), may hold values from -6 to 6
- weight: float32 [128, 256], replicated, may hold values from -0.5 to 0.5
- out_bias: float32 [256], replicated, may hold values from -3 to 3
- cotangent: float32 [65536, 256], P(('row', 'col')), may hold values from -6 to 6
- drop_keep: int32 [65536, 256], P(('row', 'col')), may hold values 0 or 1
- tile_cols: int32 [8, 32, 64, 4], P('row', 'col'), may hold values from 0 to 15, as said below
- tile_edge_counts: int32 [8, 32, 64, 4], P('row', 'col'), may hold values from 1 to 64, as said below
- edge_pos: int32 [8, 32, 64, 256], P('row', 'col'), may hold values from 0 to 16383
- edge_keep_bits: int32 [8, 32, 64, 256], P('row', 'col'), may hold values 0 or 1
Outputs:
- hidden_out: float32 [65536, 256], P(('row', 'col'))
- grad_features: float32 [65536, 128], P(('row', 'col'))
- grad_weight: float32 [128, 256], replicated
The draws below stay inside these ranges and needn't reach their ends.
Inputs may be any that keep to these rules, and one draw needn't show every extreme that they name: `tile_cols`: the 4 source tile columns of one tile-row of a device block are distinct. A tile's edges are its first tile_edge_counts slots; the slots at and after the count are unused.
All inputs are finite; a program needn't handle non-finite values. No bound on the sum of `drop_keep` or of `edge_keep_bits` on one device may be relied on, other than what follows from the above.
Results may differ from the reference program's by a relative error of at most 0.000071.
Values sent between devices are 32-bit elements; how exact they have to be, the bound alone decides.
A program may use at most 64 MiB of HBM per device.

```python
import jax
import jax.numpy as jnp
from jax import lax

FIN = 128
FH = 256
TILE_SIDE = 128
TPR = 4
EPT = 64
ND = 256
GRID_ROWS = 8
GRID_COLS = 32
NODES = 65536
DST_TILES = 64
SRC_TILES = 16
EDGE_SLOTS = 256


def draw_tile_cols(key, part):
    row_total = GRID_ROWS * GRID_COLS * DST_TILES
    scores = jax.random.randint(key, (row_total, SRC_TILES), 0, 1 << 20) * SRC_TILES + jnp.arange(SRC_TILES, dtype=jnp.int32)[None, :]
    ranked = jnp.argsort(scores, axis=1)
    return ranked[:, :TPR].astype(jnp.int32).reshape(GRID_ROWS, GRID_COLS, DST_TILES, TPR)


def draw_tile_edge_counts(key, part):
    counts = jax.random.randint(key, (GRID_ROWS, GRID_COLS, DST_TILES, TPR), 1, EPT + 1)
    return counts.at[:, :, 0, 0].set(EPT).astype(jnp.int32)


def place_ends(drawn, key, low, high):
    longest = drawn.shape.index(max(drawn.shape))
    spots = []
    for shift in (0, 1):
        where = [jax.random.randint(jax.random.fold_in(key, axis), (), 0, length) for axis, length in enumerate(drawn.shape)]
        where[longest] = (where[longest] + shift) % drawn.shape[longest]
        spots.append(tuple(where))
    return drawn.at[spots[0]].set(low).at[spots[1]].set(high)


def block_scale(rng, extent, pieces, low, high):
    def one(dim, blocks):
        draws = jax.random.uniform(jax.random.fold_in(jax.random.fold_in(rng, 6), dim), (blocks,), jnp.float32, low / len(pieces), high / len(pieces))
        return jnp.repeat(jnp.exp(draws), extent[dim] // blocks).reshape((-1,) + (1,) * (len(extent) - dim - 1))

    level = one(*pieces[0])
    for cut in pieces[1:]:
        level = level * one(*cut)
    return level


def centred(stream_key, dims, width, limit, cuts=(), held_as=jnp.bfloat16):
    array = jax.random.normal(stream_key, dims, jnp.float32) * width
    if len(cuts) > 0:
        array = block_scale(stream_key, dims, cuts, -0.22, 0.18) * array
    return jnp.clip(array, min=-limit, max=limit).astype(held_as)


def setup_inputs(seed: int = 0) -> dict:
    seeds = jax.random.split(jax.random.key(seed), 10)
    features = centred(seeds[0], (NODES, FIN), 1.0, 6.0, ((0, 256),), jnp.float32)
    weight = centred(seeds[1], (FIN, FH), FIN ** -0.5, 0.5, (), jnp.float32)
    out_bias = centred(seeds[2], (FH,), 0.5, 3.0, (), jnp.float32)
    cotangent = centred(seeds[3], (NODES, FH), 1.0, 6.0, ((0, 256),), jnp.float32)
    drop_keep = place_ends((jax.random.randint(seeds[4], (NODES, FH), 0, 10) < 9).astype(jnp.int32), jax.random.fold_in(seeds[4], 1), 0, 1)
    tile_cols = draw_tile_cols(jax.random.fold_in(seeds[9], 71), 0)
    tile_edge_counts = draw_tile_edge_counts(jax.random.fold_in(seeds[9], 71), 0)
    edge_pos = place_ends(jax.random.randint(seeds[7], (GRID_ROWS, GRID_COLS, DST_TILES, EDGE_SLOTS), 0, TILE_SIDE * TILE_SIDE), jax.random.fold_in(seeds[7], 1), 0, (TILE_SIDE * TILE_SIDE) - 1).astype(jnp.int32)
    edge_keep_bits = place_ends((jax.random.randint(seeds[8], (GRID_ROWS, GRID_COLS, DST_TILES, EDGE_SLOTS), 0, 5) < 4).astype(jnp.int32), jax.random.fold_in(seeds[8], 1), 0, 1)
    return {"features": features, "weight": weight, "out_bias": out_bias, "cotangent": cotangent, "drop_keep": drop_keep, "tile_cols": tile_cols, "tile_edge_counts": tile_edge_counts, "edge_pos": edge_pos, "edge_keep_bits": edge_keep_bits}


keep_rate = 0.9

def gelu_exact(values):
    return 0.5 * values * (1.0 + lax.erf(values * 0.7071067811865476))

def gelu_slope(values):
    return 0.5 * (1.0 + lax.erf(values * 0.7071067811865476)) + values * jnp.exp(-0.5 * values * values) * 0.3989422804014327

def edge_lists(tile_cols, tile_edge_counts, edge_pos, edge_keep_bits):
    slot_ids = jnp.arange(EDGE_SLOTS, dtype=jnp.int32)
    tile_of = slot_ids // EPT
    slot_place = slot_ids % EPT
    count_slot = tile_edge_counts[:, :, :, tile_of]
    column_slot = tile_cols[:, :, :, tile_of]
    live_mask = jnp.where((slot_place[None, None, None, :] < count_slot) & (edge_keep_bits == 1), 1.0, 0.0).astype(jnp.float32)
    tile_row = jnp.arange(DST_TILES, dtype=jnp.int32)[None, None, :, None]
    grid_row = jnp.arange(GRID_ROWS, dtype=jnp.int32)[:, None, None, None]
    grid_col = jnp.arange(GRID_COLS, dtype=jnp.int32)[None, :, None, None]
    target = grid_row * (GRID_COLS * ND) + tile_row * TILE_SIDE + edge_pos // TILE_SIDE
    source_local = column_slot * TILE_SIDE + edge_pos % TILE_SIDE
    source = (source_local // ND * GRID_COLS + grid_col) * ND + source_local % ND
    flat_count = GRID_ROWS * GRID_COLS
    return (target.reshape(flat_count, -1).astype(jnp.int32), source.reshape(flat_count, -1).astype(jnp.int32), live_mask.reshape(flat_count, -1))

def reference(features, weight, out_bias, cotangent, drop_keep, tile_cols, tile_edge_counts, edge_pos, edge_keep_bits):
    highest = lax.Precision.HIGHEST
    target, source, live_mask = edge_lists(tile_cols, tile_edge_counts, edge_pos, edge_keep_bits)
    degree = 1.0 + jax.ops.segment_sum(live_mask.ravel(), target.ravel(), num_segments=NODES)
    inv_root = lax.rsqrt(degree)[:, None]
    transformed = jnp.dot(features, weight, precision=highest, preferred_element_type=jnp.float32)
    scaled_rows = inv_root * transformed

    def forward_step(running_total, single_edge):
        target_nodes, source_nodes, surviving_mask = single_edge
        return (running_total.at[target_nodes].add(surviving_mask[:, None] * scaled_rows[source_nodes]), None)
    summed, _ = lax.scan(forward_step, jnp.zeros((NODES, FH), jnp.float32), (target, source, live_mask))
    pre_act = inv_root * (summed + scaled_rows) + out_bias[None, :]
    dropout = drop_keep.astype(jnp.float32) / keep_rate
    hidden_out = gelu_exact(pre_act) * dropout
    grad_pre = cotangent * dropout * gelu_slope(pre_act)
    backward_scaled_rows = inv_root * grad_pre

    def backward_step(running_total, single_edge):
        target_nodes, source_nodes, surviving_mask = single_edge
        return (running_total.at[source_nodes].add(surviving_mask[:, None] * backward_scaled_rows[target_nodes]), None)
    returned, _ = lax.scan(backward_step, jnp.zeros((NODES, FH), jnp.float32), (target, source, live_mask))
    grad_z = inv_root * (returned + backward_scaled_rows)
    grad_features = jnp.dot(grad_z, weight.T, precision=highest, preferred_element_type=jnp.float32)
    grad_weight = jnp.dot(features.T, grad_z, precision=highest, preferred_element_type=jnp.float32)
    return (hidden_out, grad_features, grad_weight)
```

```python
import functools

import jax
import jax.numpy as jnp
from jax import lax
from jax.experimental import pallas as pl
from jax.experimental.pallas import tpu as pltpu
from jax.sharding import PartitionSpec as P

MESH = pl.DeviceIdType.MESH
HIGHEST = lax.Precision.HIGHEST
F32, BF16, I32 = jnp.float32, jnp.bfloat16, jnp.int32

T = 128
ROWS, COLS = 8, 32
TILE_ROWS, TPR, EPT = 64, 4, 64
SLOTS = TPR * EPT
SRC_TILES = 16
MB = 1 << 20
VMEM = pl.BlockSpec(memory_space=pltpu.VMEM)
SMEM = pl.BlockSpec(memory_space=pltpu.SMEM)
NT = (((1,), (1,)), ((), ()))


def rem(a, n):
    return lax.rem(a, jnp.int32(n))


def div(a, n):
    return lax.div(a, jnp.int32(n))


def shape(*dims, dtype=F32):
    return jax.ShapeDtypeStruct(dims, dtype)


def send(src, dst, sems, where, dev):
    copy = pltpu.make_async_remote_copy(
        src_ref=src,
        dst_ref=dst,
        send_sem=sems[0].at[where],
        recv_sem=sems[1].at[where],
        device_id=dev,
        device_id_type=MESH,
    )
    copy.start()
    return copy


def handle(ref, sems, where, dev):
    return pltpu.make_async_remote_copy(
        src_ref=ref,
        dst_ref=ref,
        send_sem=sems[0].at[where],
        recv_sem=sems[1].at[where],
        device_id=dev,
        device_id_type=MESH,
    )


def sem_pair(*dims):
    return [pltpu.SemaphoreType.DMA(dims), pltpu.SemaphoreType.DMA(dims)]


def position():
    row, col = lax.axis_index("row"), lax.axis_index("col")
    return row, col


def signal(barrier, dev):
    pl.semaphore_signal(barrier, inc=1, device_id=dev, device_id_type=MESH)


def greet_groups(barrier, row, col):
    def greet_col(o, carry):
        signal(barrier, (row, rem(col + o, COLS)))
        return carry

    def greet_row(o, carry):
        signal(barrier, (rem(row + o, ROWS), col))
        return carry

    lax.fori_loop(1, COLS, greet_col, 0)
    lax.fori_loop(1, ROWS, greet_row, 0)
    pl.semaphore_wait(barrier, COLS + ROWS - 2)


def slot_codes(counts, pos, keep):
    lane = lax.broadcasted_iota(I32, (TILE_ROWS, SLOTS), 1)
    limit = jnp.broadcast_to(counts[:, 0:1], (TILE_ROWS, SLOTS))
    for k in range(1, TPR):
        limit = jnp.where(
            lane >= k * EPT, jnp.broadcast_to(counts[:, k : k + 1], (TILE_ROWS, SLOTS)), limit
        )
    live = ((lane & (EPT - 1)) < limit) & (keep == 1)
    return jnp.where(live, pos >> 7, 4 * T)


def gather_kernel(
    x_ref,
    counts_ref,
    pos_ref,
    keep_ref,
    xg_ref,
    invg_ref,
    invo_ref,
    code_ref,
    deg,
    degin,
    ds,
    dr,
    vs,
    vr,
    zs,
    zr,
    ns,
    nr,
    fs,
    fr,
):
    row, col = position()
    zh, x = div(row, 4), rem(row, 4)
    dsem, vsem, zsem, nsem, fsem = (ds, dr), (vs, vr), (zs, zr), (ns, nr), (fs, fr)
    for h in range(2):
        xg_ref[row, h] = jnp.transpose(x_ref[h * T : (h + 1) * T, :])
    code_ref[...] = slot_codes(counts_ref[...], pos_ref[...], keep_ref[...])
    greet_groups(pltpu.get_barrier_semaphore(), row, col)

    right, left, pair = rem(x + 1, 4), rem(x + 3, 4), 1 - zh
    right_dev, left_dev, pair_dev = (
        (zh * 4 + right, col),
        (zh * 4 + left, col),
        (pair * 4 + x, col),
    )
    sent = []

    def near(k, zz):
        slot = xg_ref.at[zz * 4 + x]
        sent.append(send(slot.at[0], slot.at[0], nsem, (k, 0, 0), right_dev))
        sent.append(send(slot.at[1], slot.at[1], nsem, (k, 1, 1), left_dev))
        sent.append(send(slot.at[1], slot.at[1], nsem, (k, 0, 1), right_dev))
        sent.append(send(slot.at[0], slot.at[0], nsem, (k, 1, 0), left_dev))

    def far(k, zz):
        slot = xg_ref.at[zz * 4 + left]
        handle(slot.at[0], nsem, (k, 0, 0), left_dev).wait_recv()
        sent.append(send(slot.at[0], slot.at[0], fsem, (k, 0), right_dev))
        slot = xg_ref.at[zz * 4 + right]
        handle(slot.at[1], nsem, (k, 1, 1), right_dev).wait_recv()
        sent.append(send(slot.at[1], slot.at[1], fsem, (k, 1), left_dev))

    def rest(k, zz):
        handle(xg_ref.at[zz * 4 + left, 1], nsem, (k, 0, 1), left_dev).wait_recv()
        handle(xg_ref.at[zz * 4 + right, 0], nsem, (k, 1, 0), right_dev).wait_recv()
        slot = xg_ref.at[zz * 4 + rem(x + 2, 4)]
        handle(slot.at[0], fsem, (k, 0), left_dev).wait_recv()
        handle(slot.at[1], fsem, (k, 1), right_dev).wait_recv()

    sent.append(send(xg_ref.at[row], xg_ref.at[row], zsem, 0, pair_dev))
    near(0, zh)

    ones = jnp.ones((8, SLOTS), BF16)
    side = lax.broadcasted_iota(I32, (T, SLOTS), 0)
    sub = lax.broadcasted_iota(I32, (8, T), 0)

    def count(j, carry):
        halves = []
        for h in range(2):
            code = code_ref[pl.ds(2 * j + h, 1), :]
            hot = jnp.where(side == jnp.broadcast_to(code, (T, SLOTS)), 1.0, 0.0).astype(BF16)
            halves.append(lax.dot_general(ones, hot, NT, preferred_element_type=F32))
        deg[j] = jnp.where(sub == 0, halves[0], jnp.where(sub == 1, halves[1], 0.0))
        return carry

    lax.fori_loop(0, COLS, count, 0)

    def scatter(o, carry):
        peer = rem(col + o, COLS)
        send(deg.at[peer], degin.at[o], dsem, o, (row, peer))
        return carry

    lax.fori_loop(1, COLS, scatter, 0)
    far(0, zh)

    def collect(o, total):
        handle(degin.at[o], dsem, o, (row, rem(col + COLS - o, COLS))).wait_recv()
        return total + degin[o]

    total = lax.fori_loop(1, COLS, collect, deg[col])
    inv = lax.rsqrt(1.0 + total)
    invo_ref[...] = inv
    invg_ref[row] = inv

    def spread(o, carry):
        peer = rem(row + o, ROWS)
        send(invo_ref, invg_ref.at[row], vsem, o, (peer, col))
        return carry

    lax.fori_loop(1, ROWS, spread, 0)
    handle(xg_ref.at[pair * 4 + x], zsem, 0, pair_dev).wait_recv()
    near(1, pair)
    far(1, pair)
    rest(0, zh)
    rest(1, pair)

    def finish_row(o, carry):
        peer = rem(row + ROWS - o, ROWS)
        copy = handle(invg_ref.at[peer], vsem, o, (peer, col))
        copy.wait_recv()
        copy.wait_send()
        return carry

    lax.fori_loop(1, ROWS, finish_row, 0)

    def finish_col(o, carry):
        handle(degin.at[o], dsem, o, (row, rem(col + o, COLS))).wait_send()
        return carry

    lax.fori_loop(1, COLS, finish_col, 0)
    for copy in sent:
        copy.wait_send()


def gather_call(x, counts, pos, keep):
    return pl.pallas_call(
        gather_kernel,
        name="gather_features",
        out_shape=(
            shape(ROWS, 2, T, T),
            shape(ROWS, 8, T),
            shape(8, T),
            shape(TILE_ROWS, SLOTS, dtype=I32),
        ),
        in_specs=[VMEM] * 4,
        out_specs=(VMEM,) * 4,
        scratch_shapes=[pltpu.VMEM((COLS, 8, T), F32), pltpu.VMEM((COLS, 8, T), F32)]
        + sem_pair(COLS)
        + sem_pair(ROWS)
        + sem_pair(1)
        + sem_pair(2, 2, 2)
        + sem_pair(2, 2),
        compiler_params=pltpu.CompilerParams(
            collective_id=1, has_side_effects=True, vmem_limit_bytes=16 * MB
        ),
    )(x, counts, pos, keep)


def split(values):
    high = values.astype(BF16)
    low = (values - high.astype(F32)).astype(BF16)
    return jnp.concatenate([high, low], axis=0)


def hot_dst(code_row, side):
    return jnp.where(side == jnp.broadcast_to(code_row, (T, SLOTS)), 1.0, 0.0).astype(BF16)


def hot_src(pos_row, side, lane):
    code = (pos_row & (T - 1)) + ((lane >> 6) & 1) * T
    return jnp.where(side == jnp.broadcast_to(code, (2 * T, SLOTS)), 1.0, 0.0).astype(BF16)


def forward_kernel(cols_ref, xg_ref, invg_ref, code_ref, pos_ref, out_ref, scaled):
    for u in range(SRC_TILES):
        r, h = u // 2, u % 2
        scaled[u] = split(xg_ref[r, h] * jnp.broadcast_to(invg_ref[r, h : h + 1, :], (T, T)))
    side = lax.broadcasted_iota(I32, (T, SLOTS), 0)
    wide = lax.broadcasted_iota(I32, (2 * T, SLOTS), 0)
    lane = lax.broadcasted_iota(I32, (1, SLOTS), 1)

    def tile_row(t, carry):
        dst = hot_dst(code_ref[pl.ds(t, 1), :], side)
        src = hot_src(pos_ref[pl.ds(t, 1), :], wide, lane)
        picked = []
        for p in range(2):
            panel = jnp.concatenate(
                [scaled[cols_ref[t, 2 * p]], scaled[cols_ref[t, 2 * p + 1]]], axis=1
            )
            picked.append(
                jnp.dot(panel, src[:, p * T : (p + 1) * T], preferred_element_type=F32).astype(BF16)
            )
        both = lax.dot_general(
            jnp.concatenate(picked, axis=1), dst, NT, preferred_element_type=F32
        )
        out_ref[t] = both[:T] + both[T:]
        return carry

    lax.fori_loop(0, TILE_ROWS, tile_row, 0, unroll=4)


def forward_call(cols, xg, invg, code, pos):
    return pl.pallas_call(
        forward_kernel,
        name="forward_blocks",
        out_shape=shape(TILE_ROWS, T, T),
        in_specs=[SMEM] + [VMEM] * 4,
        out_specs=VMEM,
        scratch_shapes=[pltpu.VMEM((SRC_TILES, 2 * T, T), BF16)],
        compiler_params=pltpu.CompilerParams(vmem_limit_bytes=16 * MB),
        cost_estimate=pl.CostEstimate(
            flops=TILE_ROWS * 6 * 128 * 256 * 256, bytes_accessed=6 * MB, transcendentals=0
        ),
    )(cols, xg, invg, code, pos)


def backward_kernel(cols_ref, grads_ref, code_ref, pos_ref, out_ref):
    out_ref[...] = jnp.zeros_like(out_ref)
    side = lax.broadcasted_iota(I32, (T, SLOTS), 0)
    wide = lax.broadcasted_iota(I32, (2 * T, SLOTS), 0)
    lane = lax.broadcasted_iota(I32, (1, SLOTS), 1)

    def tile_row(t, carry):
        dst = hot_dst(code_ref[pl.ds(t, 1), :], side)
        src = hot_src(pos_ref[pl.ds(t, 1), :], wide, lane)
        picked = jnp.dot(split(grads_ref[t]), dst, preferred_element_type=F32).astype(BF16)
        for p in range(2):
            part = picked[:, p * T : (p + 1) * T]
            hot = src[:, p * T : (p + 1) * T]
            back = lax.dot_general(
                jnp.concatenate([part[:T], part[T:]], axis=1),
                jnp.concatenate([hot, hot], axis=1),
                NT,
                preferred_element_type=F32,
            )
            for k in range(2):
                out_ref[cols_ref[t, 2 * p + k]] += back[:, k * T : (k + 1) * T]
        return carry

    lax.fori_loop(0, TILE_ROWS, tile_row, 0, unroll=4)


def backward_call(cols, grads, code, pos):
    return pl.pallas_call(
        backward_kernel,
        name="backward_blocks",
        out_shape=shape(SRC_TILES, T, T),
        in_specs=[SMEM] + [VMEM] * 3,
        out_specs=VMEM,
        compiler_params=pltpu.CompilerParams(vmem_limit_bytes=16 * MB),
        cost_estimate=pl.CostEstimate(
            flops=TILE_ROWS * 6 * 128 * 256 * 256, bytes_accessed=6 * MB, transcendentals=0
        ),
    )(cols, grads, code, pos)


Z_ORDER = (3, 0, 2, 1)


def col_place(col):
    return div(col, 8), rem(div(col, 2), 4), rem(col, 2)


def greet_col_neighbours(barrier, zl, devs):
    core_dev, right_dev, left_dev, up_dev, down_dev = devs
    for dev in (core_dev, right_dev, left_dev):
        signal(barrier, dev)

    @pl.when(zl < 3)
    def _():
        signal(barrier, up_dev)

    @pl.when(zl > 0)
    def _():
        signal(barrier, down_dev)

    pl.semaphore_wait(
        barrier, 3 + jnp.where(zl < 3, 1, 0).astype(I32) + jnp.where(zl > 0, 1, 0).astype(I32)
    )


def col_devs(row, zl, y, c):
    def dev(z, yy, cc):
        return (row, (z * 4 + yy) * 2 + cc)

    return (
        dev(zl, y, 1 - c),
        dev(zl, rem(y + 1, 4), c),
        dev(zl, rem(y + 3, 4), c),
        dev(jnp.minimum(zl + 1, 3), y, c),
        dev(jnp.maximum(zl - 1, 0), y, c),
    )


def sum_col_kernel(
    p_ref,
    out_ref,
    cbuf,
    q,
    yfar,
    yacc,
    ynear,
    tot,
    zin,
    zout,
    cs,
    cr,
    fs,
    fr,
    ns,
    nr,
    zs,
    zr,
):
    row, col = position()
    zl, y, c = col_place(col)
    devs = col_devs(row, zl, y, c)
    core_dev, right_dev, left_dev, up_dev, down_dev = devs
    csem, fsem, nsem, zsem = (cs, cr), (fs, fr), (ns, nr), (zs, zr)
    greet_col_neighbours(pltpu.get_barrier_semaphore(), zl, devs)
    sent = []
    for z in Z_ORDER:
        for d in (2, 1, 3, 0):
            sent.append(
                send(p_ref.at[z, rem(y + d, 4), 1 - c], cbuf.at[z, d], csem, (z, d), core_dev)
            )
    for z in Z_ORDER:
        for d in (2, 1, 3, 0):
            handle(cbuf.at[z, d], csem, (z, d), core_dev).wait_recv()
            q[z, d] = p_ref[z, rem(y + d, 4), c] + cbuf[z, d]
            if d == 2:
                sent.append(send(q.at[z, 2, 0], yfar.at[z, 0], fsem, (z, 0), right_dev))
                sent.append(send(q.at[z, 2, 1], yfar.at[z, 1], fsem, (z, 1), left_dev))
            if d == 1:
                sent.append(send(q.at[z, 1, 1], ynear.at[z, 0, 1], nsem, (z, 0, 1), right_dev))
            if d == 3:
                sent.append(send(q.at[z, 3, 0], ynear.at[z, 1, 0], nsem, (z, 1, 0), left_dev))
    for z in Z_ORDER:
        handle(yfar.at[z, 0], fsem, (z, 0), left_dev).wait_recv()
        yacc[z, 0] = q[z, 1, 0] + yfar[z, 0]
        sent.append(send(yacc.at[z, 0], ynear.at[z, 0, 0], nsem, (z, 0, 0), right_dev))
        handle(yfar.at[z, 1], fsem, (z, 1), right_dev).wait_recv()
        yacc[z, 1] = q[z, 3, 1] + yfar[z, 1]
        sent.append(send(yacc.at[z, 1], ynear.at[z, 1, 1], nsem, (z, 1, 1), left_dev))

    def up_copy(z, h):
        return handle_to(zout.at[z, 0, h], zin.at[z, 0, h], zsem, (z, 0, h), up_dev)

    def down_copy(z, h):
        return handle_to(zout.at[z, 1, h], zin.at[z, 1, h], zsem, (z, 1, h), down_dev)

    for z in Z_ORDER:
        for h in (0, 1):
            for k, dev in ((0, left_dev), (1, right_dev)):
                handle(ynear.at[z, k, h], nsem, (z, k, h), dev).wait_recv()
            tot[z, h] = q[z, 0, h] + (ynear[z, 0, h] + ynear[z, 1, h])
            if z > 0:

                @pl.when(zl < z)
                def _():
                    @pl.when(zl == 0)
                    def _():
                        zout[z, 0, h] = tot[z, h]

                    @pl.when(zl > 0)
                    def _():
                        handle(zin.at[z, 0, h], zsem, (z, 0, h), down_dev).wait_recv()
                        zout[z, 0, h] = tot[z, h] + zin[z, 0, h]

                    up_copy(z, h).start()

            if z < 3:

                @pl.when(zl > z)
                def _():
                    @pl.when(zl == 3)
                    def _():
                        zout[z, 1, h] = tot[z, h]

                    @pl.when(zl < 3)
                    def _():
                        handle(zin.at[z, 1, h], zsem, (z, 1, h), up_dev).wait_recv()
                        zout[z, 1, h] = tot[z, h] + zin[z, 1, h]

                    down_copy(z, h).start()

    for z in range(4):

        @pl.when(zl == z)
        def _():
            for h in range(2):
                value = tot[z, h]
                if z > 0:
                    handle(zin.at[z, 0, h], zsem, (z, 0, h), down_dev).wait_recv()
                    value = value + zin[z, 0, h]
                if z < 3:
                    handle(zin.at[z, 1, h], zsem, (z, 1, h), up_dev).wait_recv()
                    value = value + zin[z, 1, h]
                out_ref[h] = value

        @pl.when(zl < z)
        def _():
            for h in range(2):
                up_copy(z, h).wait_send()

        @pl.when(zl > z)
        def _():
            for h in range(2):
                down_copy(z, h).wait_send()

    for copy in sent:
        copy.wait_send()


def handle_to(src, dst, sems, where, dev):
    return pltpu.make_async_remote_copy(
        src_ref=src,
        dst_ref=dst,
        send_sem=sems[0].at[where],
        recv_sem=sems[1].at[where],
        device_id=dev,
        device_id_type=MESH,
    )


def sum_col_call(parts):
    return pl.pallas_call(
        sum_col_kernel,
        name="sum_over_col",
        out_shape=shape(2, T, T),
        in_specs=[VMEM],
        out_specs=VMEM,
        scratch_shapes=[
            pltpu.VMEM((4, 4, 2, T, T), F32),
            pltpu.VMEM((4, 4, 2, T, T), F32),
            pltpu.VMEM((4, 2, T, T), F32),
            pltpu.VMEM((4, 2, T, T), F32),
            pltpu.VMEM((4, 2, 2, T, T), F32),
            pltpu.VMEM((4, 2, T, T), F32),
            pltpu.VMEM((4, 2, 2, T, T), F32),
            pltpu.VMEM((4, 2, 2, T, T), F32),
        ]
        + sem_pair(4, 4)
        + sem_pair(4, 2)
        + sem_pair(4, 2, 2)
        + sem_pair(4, 2, 2),
        compiler_params=pltpu.CompilerParams(
            collective_id=2, has_side_effects=True, vmem_limit_bytes=24 * MB
        ),
    )(parts.reshape(4, 4, 2, 2, T, T))


def gelu_pair(values):
    half = 0.5 * (1.0 + lax.erf(values * 0.7071067811865476))
    slope = half + values * jnp.exp(-0.5 * values * values) * 0.3989422804014327
    return values * half, slope


def node_kernel(agg_ref, x_ref, inv_ref, w_ref, b_ref, cot_ref, drop_ref, hid_ref, ht_ref, gw_ref):
    weight = w_ref[...]
    total = jnp.zeros((T, 2 * T), F32)
    for h in range(2):
        part = slice(h * T, (h + 1) * T)
        inv_row = jnp.broadcast_to(inv_ref[h : h + 1, :], (T, T))
        inv_col = jnp.transpose(inv_row)
        inv_col = jnp.concatenate([inv_col, inv_col], axis=1)
        agg = agg_ref[h] + jnp.transpose(x_ref[part, :]) * inv_row
        mixed = jnp.dot(
            jnp.transpose(agg), weight, precision=HIGHEST, preferred_element_type=F32
        )
        pre = inv_col * mixed + jnp.broadcast_to(b_ref[...], (T, 2 * T))
        gelu, slope = gelu_pair(pre)
        drop = drop_ref[part, :].astype(F32) / 0.9
        hid_ref[part, :] = gelu * drop
        grad = inv_col * (cot_ref[part, :] * drop * slope)
        ht_ref[h] = lax.dot_general(weight, grad, NT, precision=HIGHEST, preferred_element_type=F32)
        total = total + jnp.dot(agg, grad, precision=HIGHEST, preferred_element_type=F32)
    for k in range(2):
        gw_ref[k * 16 : (k + 1) * 16] = total[:, k * T : (k + 1) * T].reshape(16, 8, T)


def node_call(agg, x, inv, weight, bias, cot, drop):
    return pl.pallas_call(
        node_kernel,
        name="node_update",
        out_shape=(shape(2 * T, 2 * T), shape(2, T, T), shape(COLS, 8, T)),
        in_specs=[VMEM] * 7,
        out_specs=(VMEM,) * 3,
        compiler_params=pltpu.CompilerParams(vmem_limit_bytes=16 * MB),
    )(agg, x, inv, weight, bias.reshape(1, 2 * T), cot, drop)


def spread_kernel(
    ht_ref,
    gw_ref,
    g_ref,
    gwt_ref,
    gin,
    rin,
    mine,
    gs,
    gr,
    ws,
    wr,
    zs,
    zr,
    ns,
    nr,
    fs,
    fr,
    cs,
    cr,
):
    row, col = position()
    zl, y, c = col_place(col)
    core_dev, right_dev, left_dev, up_dev, down_dev = col_devs(row, zl, y, c)
    gsem, wsem, zsem, nsem, fsem, csem = (
        (gs, gr),
        (ws, wr),
        (zs, zr),
        (ns, nr),
        (fs, fr),
        (cs, cr),
    )
    right, left, across = rem(y + 1, 4), rem(y + 3, 4), rem(y + 2, 4)
    g_ref[zl, y, c] = ht_ref[...]
    greet_groups(pltpu.get_barrier_semaphore(), row, col)

    def z_copy(z, way, h):
        slot = g_ref.at[z, y, c, h]
        return handle(slot, zsem, (z, way, h), up_dev if way == 0 else down_dev)

    def z_send(z, way):
        @pl.when(zl < 3 if way == 0 else zl > 0)
        def _():
            for h in range(2):
                z_copy(z, way, h).start()

    def near_copy(z, way, h):
        slot = g_ref.at[z, y, c, h]
        return handle(slot, nsem, (z, way, h), right_dev if way == 0 else left_dev)

    def near_send(z):
        for way, h in ((0, 0), (1, 1), (0, 1), (1, 0)):
            near_copy(z, way, h).start()

    def core_copy(z, d):
        return handle(g_ref.at[z, rem(y + d, 4), c], csem, (z, d), core_dev)

    def far_copy(z, h):
        slot = g_ref.at[z, left if h == 0 else right, c, h]
        return handle(slot, fsem, (z, h), right_dev if h == 0 else left_dev)

    def near_wait(z, way, h):
        slot = g_ref.at[z, left if way == 0 else right, c, h]
        handle(slot, nsem, (z, way, h), left_dev if way == 0 else right_dev).wait_recv()

    def y_arrive(z):
        near_wait(z, 0, 0)
        far_copy(z, 0).start()
        near_wait(z, 1, 1)
        far_copy(z, 1).start()
        near_wait(z, 0, 1)
        core_copy(z, 3).start()
        near_wait(z, 1, 0)
        core_copy(z, 1).start()

    def y_far(z):
        for h in range(2):
            slot = g_ref.at[z, across, c, h]
            handle(slot, fsem, (z, h), left_dev if h == 0 else right_dev).wait_recv()
        core_copy(z, 2).start()

    def each(step, body):
        if step == 0:
            body(zl, None)
            return

        @pl.when(zl >= step)
        def _():
            body(zl - step, 0)

        @pl.when(zl + step <= 3)
        def _():
            body(zl + step, 1)

    def z_arrive(z, way):
        for h in range(2):
            handle(
                g_ref.at[z, y, c, h], zsem, (z, way, h), down_dev if way == 0 else up_dev
            ).wait_recv()
        z_send(z, way)
        near_send(z)
        core_copy(z, 0).start()

    z_send(zl, 0)
    z_send(zl, 1)
    near_send(zl)
    core_copy(zl, 0).start()

    def scatter(o, carry):
        peer = rem(col + o, COLS)
        send(gw_ref.at[peer], gin.at[o], gsem, o, (row, peer))
        return carry

    lax.fori_loop(1, COLS, scatter, 0)
    arrive = lambda z, way: y_arrive(z)
    last = lambda z, way: y_far(z)
    each(1, z_arrive)
    each(0, arrive)
    each(2, z_arrive)
    each(1, arrive)
    each(0, last)

    def collect(o, total):
        handle(gin.at[o], gsem, o, (row, rem(col + COLS - o, COLS))).wait_recv()
        return total + gin[o]

    mine[...] = lax.fori_loop(1, COLS, collect, gw_ref[col])
    rin[row] = mine[...]

    def share(o, carry):
        peer = rem(row + o, ROWS)
        send(mine, rin.at[row], wsem, o, (peer, col))
        return carry

    lax.fori_loop(1, ROWS, share, 0)
    each(3, z_arrive)
    each(2, arrive)
    each(1, last)
    each(3, arrive)
    each(2, last)
    each(3, last)

    def finish_row(o, carry):
        peer = rem(row + ROWS - o, ROWS)
        copy = handle(rin.at[peer], wsem, o, (peer, col))
        copy.wait_recv()
        copy.wait_send()
        return carry

    lax.fori_loop(1, ROWS, finish_row, 0)
    total = rin[0]
    for r in range(1, ROWS):
        total = total + rin[r]
    gwt_ref[...] = total

    for z in range(4):
        for d in range(4):
            slot = g_ref.at[z, rem(y + d, 4), 1 - c]
            handle(slot, csem, (z, d), core_dev).wait_recv()

    for z in range(4):
        for d in range(4):
            core_copy(z, d).wait_send()
        for way in range(2):
            for h in range(2):
                near_copy(z, way, h).wait_send()
        for h in range(2):
            far_copy(z, h).wait_send()

        @pl.when((zl >= z) & (zl < 3))
        def _():
            for h in range(2):
                z_copy(z, 0, h).wait_send()

        @pl.when((zl <= z) & (zl > 0))
        def _():
            for h in range(2):
                z_copy(z, 1, h).wait_send()

    def finish_col(o, carry):
        handle(gin.at[o], gsem, o, (row, rem(col + o, COLS))).wait_send()
        return carry

    lax.fori_loop(1, COLS, finish_col, 0)


def spread_call(ht, gw):
    return pl.pallas_call(
        spread_kernel,
        name="spread_over_col",
        out_shape=(shape(4, 4, 2, 2, T, T), shape(8, T)),
        in_specs=[VMEM] * 2,
        out_specs=(VMEM,) * 2,
        scratch_shapes=[
            pltpu.VMEM((COLS, 8, T), F32),
            pltpu.VMEM((ROWS, 8, T), F32),
            pltpu.VMEM((8, T), F32),
        ]
        + sem_pair(COLS)
        + sem_pair(ROWS)
        + sem_pair(4, 2, 2)
        + sem_pair(4, 2, 2)
        + sem_pair(4, 2)
        + sem_pair(4, 4),
        compiler_params=pltpu.CompilerParams(
            collective_id=3, has_side_effects=True, vmem_limit_bytes=16 * MB
        ),
    )(ht, gw)


def sum_row_kernel(
    q_ref,
    ht_ref,
    inv_ref,
    gwt_ref,
    gf_ref,
    gw_ref,
    xfar,
    xacc,
    xnear,
    tot,
    zin,
    gbuf,
    gs,
    gr,
    zs,
    zr,
    ns,
    nr,
    fs,
    fr,
):
    row, col = position()
    zh, x = div(row, 4), rem(row, 4)
    gsem, zsem, nsem, fsem = (gs, gr), (zs, zr), (ns, nr), (fs, fr)
    right_dev, left_dev, pair_dev = (
        (zh * 4 + rem(x + 1, 4), col),
        (zh * 4 + rem(x + 3, 4), col),
        ((1 - zh) * 4 + x, col),
    )
    gbuf[col] = gwt_ref[...]
    barrier = pltpu.get_barrier_semaphore()

    def greet_col(o, carry):
        signal(barrier, (row, rem(col + o, COLS)))
        return carry

    lax.fori_loop(1, COLS, greet_col, 0)
    for dev in (right_dev, left_dev, pair_dev):
        signal(barrier, dev)
    pl.semaphore_wait(barrier, COLS - 1 + 3)

    sent = []
    base = ((1 - zh) * 4, zh * 4)

    def block(k, d):
        return base[k] + rem(x + d, 4)

    for k in range(2):
        b2, b1, b3 = block(k, 2), block(k, 1), block(k, 3)
        sent.append(send(q_ref.at[b2, 0], xfar.at[k, 0], fsem, (k, 0), right_dev))
        sent.append(send(q_ref.at[b2, 1], xfar.at[k, 1], fsem, (k, 1), left_dev))
        sent.append(send(q_ref.at[b1, 1], xnear.at[k, 0, 1], nsem, (k, 0, 1), right_dev))
        sent.append(send(q_ref.at[b3, 0], xnear.at[k, 1, 0], nsem, (k, 1, 0), left_dev))

    def gather(o, carry):
        peer = rem(col + o, COLS)
        send(gwt_ref, gbuf.at[col], gsem, o, (row, peer))
        return carry

    lax.fori_loop(1, COLS, gather, 0)
    for k in range(2):
        handle(xfar.at[k, 0], fsem, (k, 0), left_dev).wait_recv()
        xacc[k, 0] = q_ref[block(k, 1), 0] + xfar[k, 0]
        sent.append(send(xacc.at[k, 0], xnear.at[k, 0, 0], nsem, (k, 0, 0), right_dev))
        handle(xfar.at[k, 1], fsem, (k, 1), right_dev).wait_recv()
        xacc[k, 1] = q_ref[block(k, 3), 1] + xfar[k, 1]
        sent.append(send(xacc.at[k, 1], xnear.at[k, 1, 1], nsem, (k, 1, 1), left_dev))
    for k in range(2):
        for h in range(2):
            for way, dev in ((0, left_dev), (1, right_dev)):
                handle(xnear.at[k, way, h], nsem, (k, way, h), dev).wait_recv()
            tot[k, h] = q_ref[block(k, 0), h] + (xnear[k, 0, h] + xnear[k, 1, h])
            if k == 0:
                sent.append(send(tot.at[0, h], zin.at[h], zsem, h, pair_dev))

    def collect(o, carry):
        peer = rem(col + COLS - o, COLS)
        copy = handle(gbuf.at[peer], gsem, o, (row, peer))
        copy.wait_recv()
        copy.wait_send()
        return carry

    lax.fori_loop(1, COLS, collect, 0)
    for k in range(2):
        gw_ref[:, k * T : (k + 1) * T] = gbuf[k * 16 : (k + 1) * 16].reshape(T, T)
    for h in range(2):
        handle(zin.at[h], zsem, h, pair_dev).wait_recv()
        back = (tot[1, h] + zin[h]) + ht_ref[h]
        gf_ref[h * T : (h + 1) * T, :] = jnp.transpose(
            back * jnp.broadcast_to(inv_ref[h : h + 1, :], (T, T))
        )
    for copy in sent:
        copy.wait_send()


def sum_row_call(parts, ht, inv, gwt):
    return pl.pallas_call(
        sum_row_kernel,
        name="sum_over_row",
        out_shape=(shape(2 * T, T), shape(T, 2 * T)),
        in_specs=[VMEM] * 4,
        out_specs=(VMEM,) * 2,
        scratch_shapes=[
            pltpu.VMEM((2, 2, T, T), F32),
            pltpu.VMEM((2, 2, T, T), F32),
            pltpu.VMEM((2, 2, 2, T, T), F32),
            pltpu.VMEM((2, 2, T, T), F32),
            pltpu.VMEM((2, T, T), F32),
            pltpu.VMEM((COLS, 8, T), F32),
        ]
        + sem_pair(COLS)
        + sem_pair(2)
        + sem_pair(2, 2, 2)
        + sem_pair(2, 2),
        compiler_params=pltpu.CompilerParams(
            collective_id=4, has_side_effects=True, vmem_limit_bytes=16 * MB
        ),
    )(parts.reshape(ROWS, 2, T, T), ht, inv, gwt)


def shards(features, weight, bias, cot, drop, tile_cols, counts, pos, keep):
    cols, pos = tile_cols[0, 0], pos[0, 0]
    xg, invg, inv, code = gather_call(features, counts[0, 0], pos, keep[0, 0])
    parts = forward_call(cols, xg, invg, code, pos)
    agg = sum_col_call(parts)
    hidden, ht, gw = node_call(agg, features, inv, weight, bias, cot, drop)
    grads, gwt = spread_call(ht, gw)
    back = backward_call(cols, grads.reshape(TILE_ROWS, T, T), code, pos)
    grad_features, grad_weight = sum_row_call(back, ht, inv, gwt)
    return hidden, grad_features, grad_weight


def solution(mesh):
    nodes = P(("row", "col"), None)
    block = P("row", "col", None, None)
    return jax.shard_map(
        shards,
        mesh=mesh,
        in_specs=(nodes, P(), P(), nodes, nodes, block, block, block, block),
        out_specs=(nodes, nodes, P()),
        check_vma=False,
    )
```

```python
import functools

import jax
import jax.numpy as jnp
from jax import lax
from jax.experimental import pallas as pl
from jax.experimental.pallas import tpu as pltpu
from jax.sharding import PartitionSpec as P

MESH = pl.DeviceIdType.MESH
HIGHEST = lax.Precision.HIGHEST
F32, BF16, I32 = jnp.float32, jnp.bfloat16, jnp.int32

T = 128
ROWS, COLS = 8, 32
TILE_ROWS, TPR, EPT = 64, 4, 64
SLOTS = TPR * EPT
SRC_TILES = 16
MB = 1 << 20
VMEM = pl.BlockSpec(memory_space=pltpu.VMEM)
SMEM = pl.BlockSpec(memory_space=pltpu.SMEM)
NT = (((1,), (1,)), ((), ()))


def rem(a, n):
    return lax.rem(a, jnp.int32(n))


def div(a, n):
    return lax.div(a, jnp.int32(n))


def shape(*dims, dtype=F32):
    return jax.ShapeDtypeStruct(dims, dtype)


def send(src, dst, sems, where, dev):
    copy = pltpu.make_async_remote_copy(
        src_ref=src,
        dst_ref=dst,
        send_sem=sems[0].at[where],
        recv_sem=sems[1].at[where],
        device_id=dev,
        device_id_type=MESH,
    )
    copy.start()
    return copy


def handle(ref, sems, where, dev):
    return pltpu.make_async_remote_copy(
        src_ref=ref,
        dst_ref=ref,
        send_sem=sems[0].at[where],
        recv_sem=sems[1].at[where],
        device_id=dev,
        device_id_type=MESH,
    )


def sem_pair(*dims):
    return [pltpu.SemaphoreType.DMA(dims), pltpu.SemaphoreType.DMA(dims)]


def position():
    row, col = lax.axis_index("row"), lax.axis_index("col")
    return row, col


def signal(barrier, dev):
    pl.semaphore_signal(barrier, inc=1, device_id=dev, device_id_type=MESH)


def greet_groups(barrier, row, col):
    def greet_col(o, carry):
        signal(barrier, (row, rem(col + o, COLS)))
        return carry

    def greet_row(o, carry):
        signal(barrier, (rem(row + o, ROWS), col))
        return carry

    lax.fori_loop(1, COLS, greet_col, 0)
    lax.fori_loop(1, ROWS, greet_row, 0)
    pl.semaphore_wait(barrier, COLS + ROWS - 2)


def slot_codes(counts, pos, keep):
    lane = lax.broadcasted_iota(I32, (TILE_ROWS, SLOTS), 1)
    limit = jnp.broadcast_to(counts[:, 0:1], (TILE_ROWS, SLOTS))
    for k in range(1, TPR):
        limit = jnp.where(
            lane >= k * EPT, jnp.broadcast_to(counts[:, k : k + 1], (TILE_ROWS, SLOTS)), limit
        )
    live = ((lane & (EPT - 1)) < limit) & (keep == 1)
    return jnp.where(live, pos >> 7, 4 * T)


def gather_kernel(
    x_ref,
    counts_ref,
    pos_ref,
    keep_ref,
    xg_ref,
    invg_ref,
    invo_ref,
    code_ref,
    deg,
    degin,
    ds,
    dr,
    vs,
    vr,
    zs,
    zr,
    ns,
    nr,
    fs,
    fr,
):
    row, col = position()
    zh, x = div(row, 4), rem(row, 4)
    dsem, vsem, zsem, nsem, fsem = (ds, dr), (vs, vr), (zs, zr), (ns, nr), (fs, fr)
    for h in range(2):
        xg_ref[row, h] = jnp.transpose(x_ref[h * T : (h + 1) * T, :])
    code_ref[...] = slot_codes(counts_ref[...], pos_ref[...], keep_ref[...])
    greet_groups(pltpu.get_barrier_semaphore(), row, col)

    right, left, pair = rem(x + 1, 4), rem(x + 3, 4), 1 - zh
    right_dev, left_dev, pair_dev = (
        (zh * 4 + right, col),
        (zh * 4 + left, col),
        (pair * 4 + x, col),
    )
    sent = []

    def near(k, zz):
        slot = xg_ref.at[zz * 4 + x]
        sent.append(send(slot.at[0], slot.at[0], nsem, (k, 0, 0), right_dev))
        sent.append(send(slot.at[1], slot.at[1], nsem, (k, 1, 1), left_dev))
        sent.append(send(slot.at[1], slot.at[1], nsem, (k, 0, 1), right_dev))
        sent.append(send(slot.at[0], slot.at[0], nsem, (k, 1, 0), left_dev))

    def far(k, zz):
        slot = xg_ref.at[zz * 4 + left]
        handle(slot.at[0], nsem, (k, 0, 0), left_dev).wait_recv()
        sent.append(send(slot.at[0], slot.at[0], fsem, (k, 0), right_dev))
        slot = xg_ref.at[zz * 4 + right]
        handle(slot.at[1], nsem, (k, 1, 1), right_dev).wait_recv()
        sent.append(send(slot.at[1], slot.at[1], fsem, (k, 1), left_dev))

    def rest(k, zz):
        handle(xg_ref.at[zz * 4 + left, 1], nsem, (k, 0, 1), left_dev).wait_recv()
        handle(xg_ref.at[zz * 4 + right, 0], nsem, (k, 1, 0), right_dev).wait_recv()
        slot = xg_ref.at[zz * 4 + rem(x + 2, 4)]
        handle(slot.at[0], fsem, (k, 0), left_dev).wait_recv()
        handle(slot.at[1], fsem, (k, 1), right_dev).wait_recv()

    sent.append(send(xg_ref.at[row], xg_ref.at[row], zsem, 0, pair_dev))
    near(0, zh)

    ones = jnp.ones((8, SLOTS), BF16)
    side = lax.broadcasted_iota(I32, (T, SLOTS), 0)
    sub = lax.broadcasted_iota(I32, (8, T), 0)

    def count(j, carry):
        halves = []
        for h in range(2):
            code = code_ref[pl.ds(2 * j + h, 1), :]
            hot = jnp.where(side == jnp.broadcast_to(code, (T, SLOTS)), 1.0, 0.0).astype(BF16)
            halves.append(lax.dot_general(ones, hot, NT, preferred_element_type=F32))
        deg[j] = jnp.where(sub == 0, halves[0], jnp.where(sub == 1, halves[1], 0.0))
        return carry

    lax.fori_loop(0, COLS, count, 0)

    def scatter(o, carry):
        peer = rem(col + o, COLS)
        send(deg.at[peer], degin.at[o], dsem, o, (row, peer))
        return carry

    lax.fori_loop(1, COLS, scatter, 0)
    far(0, zh)

    def collect(o, total):
        handle(degin.at[o], dsem, o, (row, rem(col + COLS - o, COLS))).wait_recv()
        return total + degin[o]

    total = lax.fori_loop(1, COLS, collect, deg[col])
    inv = lax.rsqrt(1.0 + total)
    invo_ref[...] = inv
    invg_ref[row] = inv

    def spread(o, carry):
        peer = rem(row + o, ROWS)
        send(invo_ref, invg_ref.at[row], vsem, o, (peer, col))
        return carry

    lax.fori_loop(1, ROWS, spread, 0)
    handle(xg_ref.at[pair * 4 + x], zsem, 0, pair_dev).wait_recv()
    near(1, pair)
    far(1, pair)
    rest(0, zh)
    rest(1, pair)

    def finish_row(o, carry):
        peer = rem(row + ROWS - o, ROWS)
        copy = handle(invg_ref.at[peer], vsem, o, (peer, col))
        copy.wait_recv()
        copy.wait_send()
        return carry

    lax.fori_loop(1, ROWS, finish_row, 0)

    def finish_col(o, carry):
        handle(degin.at[o], dsem, o, (row, rem(col + o, COLS))).wait_send()
        return carry

    lax.fori_loop(1, COLS, finish_col, 0)
    for copy in sent:
        copy.wait_send()


def gather_call(x, counts, pos, keep):
    return pl.pallas_call(
        gather_kernel,
        name="gather_features",
        out_shape=(
            shape(ROWS, 2, T, T),
            shape(ROWS, 8, T),
            shape(8, T),
            shape(TILE_ROWS, SLOTS, dtype=I32),
        ),
        in_specs=[VMEM] * 4,
        out_specs=(VMEM,) * 4,
        scratch_shapes=[pltpu.VMEM((COLS, 8, T), F32), pltpu.VMEM((COLS, 8, T), F32)]
        + sem_pair(COLS)
        + sem_pair(ROWS)
        + sem_pair(1)
        + sem_pair(2, 2, 2)
        + sem_pair(2, 2),
        compiler_params=pltpu.CompilerParams(
            collective_id=1, has_side_effects=True, vmem_limit_bytes=16 * MB
        ),
    )(x, counts, pos, keep)


def split(values):
    high = values.astype(BF16)
    low = (values - high.astype(F32)).astype(BF16)
    return jnp.concatenate([high, low], axis=0)


def hot_dst(code_row, side):
    return jnp.where(side == jnp.broadcast_to(code_row, (T, SLOTS)), 1.0, 0.0).astype(BF16)


def hot_src(pos_row, side, lane):
    code = (pos_row & (T - 1)) + ((lane >> 6) & 1) * T
    return jnp.where(side == jnp.broadcast_to(code, (2 * T, SLOTS)), 1.0, 0.0).astype(BF16)


def hot_iotas():
    return (
        lax.broadcasted_iota(I32, (T, SLOTS), 0),
        lax.broadcasted_iota(I32, (2 * T, SLOTS), 0),
        lax.broadcasted_iota(I32, (1, SLOTS), 1),
    )


def col_place(col):
    return div(col, 8), rem(div(col, 2), 4), rem(col, 2)


def col_devs(row, zl, y, c):
    def dev(z, yy, cc):
        return (row, (z * 4 + yy) * 2 + cc)

    return (
        dev(zl, y, 1 - c),
        dev(zl, rem(y + 1, 4), c),
        dev(zl, rem(y + 3, 4), c),
        dev(jnp.minimum(zl + 1, 3), y, c),
        dev(jnp.maximum(zl - 1, 0), y, c),
    )


def far_first(zl, k):
    near = jnp.where(zl >= 2, 3 - zl, zl)
    inner = jnp.where(k == 0, 3, jnp.where(k == 1, 0, 4 - k))
    plane = jnp.where(near == 0, 3 - k, inner)
    return jnp.where(zl >= 2, 3 - plane, plane)


def forward_kernel(
    cols_ref,
    xg_ref,
    invg_ref,
    code_ref,
    pos_ref,
    out_ref,
    scaled,
    pbuf,
    cbuf,
    q,
    yfar,
    yacc,
    ynear,
    tot,
    zin,
    zout,
    cs,
    cr,
    fs,
    fr,
    ns,
    nr,
    zs,
    zr,
):
    row, col = position()
    zl, y, c = col_place(col)
    core_dev, right_dev, left_dev, up_dev, down_dev = col_devs(row, zl, y, c)
    csem, fsem, nsem, zsem = (cs, cr), (fs, fr), (ns, nr), (zs, zr)
    barrier = pltpu.get_barrier_semaphore()
    for dev in (core_dev, right_dev, left_dev):
        signal(barrier, dev)

    @pl.when(zl < 3)
    def _():
        signal(barrier, up_dev)

    @pl.when(zl > 0)
    def _():
        signal(barrier, down_dev)

    for u in range(SRC_TILES):
        r, h = u // 2, u % 2
        scaled[u] = split(xg_ref[r, h] * jnp.broadcast_to(invg_ref[r, h : h + 1, :], (T, T)))
    side, wide, lane = hot_iotas()
    pl.semaphore_wait(
        barrier, 3 + jnp.where(zl < 3, 1, 0).astype(I32) + jnp.where(zl > 0, 1, 0).astype(I32)
    )

    def tile_row(t):
        dst = hot_dst(code_ref[pl.ds(t, 1), :], side)
        src = hot_src(pos_ref[pl.ds(t, 1), :], wide, lane)
        picked = []
        for p in range(2):
            panel = jnp.concatenate(
                [scaled[cols_ref[t, 2 * p]], scaled[cols_ref[t, 2 * p + 1]]], axis=1
            )
            picked.append(
                jnp.dot(panel, src[:, p * T : (p + 1) * T], preferred_element_type=F32).astype(BF16)
            )
        both = lax.dot_general(
            jnp.concatenate(picked, axis=1), dst, NT, preferred_element_type=F32
        )
        return both[:T] + both[T:]

    def core_copy(g):
        return link(pbuf.at[g], cbuf.at[g], csem, g, core_dev)

    def far_copy(k, way):
        return link(
            q.at[4 * k, way], yfar.at[k, way], fsem, (k, way), left_dev if way else right_dev
        )

    def near_copy(k, way, h):
        src = yacc.at[k, way] if way == h else q.at[4 * k + 1 + way, h]
        return link(src, ynear.at[k, way, h], nsem, (k, way, h), left_dev if way else right_dev)

    def near_wait(k, way, h):
        return link(
            ynear.at[k, way, h],
            ynear.at[k, way, h],
            nsem,
            (k, way, h),
            right_dev if way else left_dev,
        )

    def chain(k):
        z = far_first(zl, k)
        down = z < zl
        way = jnp.where(down, 1, 0)
        onward = (row, (jnp.where(down, zl - 1, zl + 1) * 4 + y) * 2 + c)
        source = jnp.where(down, zl < 3, zl > 0)
        return z, way, onward, source

    def chain_copy(k, h):
        z, way, onward, _ = chain(k)
        return link(zout.at[k, h], zin.at[z, way, h], zsem, (z, way, h), onward)

    def finish(g):
        k, j = div(g, 4), rem(g, 4)
        core_copy(g).wait_recv()
        q[g] = q[g] + cbuf[g]

        @pl.when(j == 0)
        def _():
            far_copy(k, 0).start()
            far_copy(k, 1).start()

        @pl.when(j == 1)
        def _():
            near_copy(k, 0, 1).start()

        @pl.when(j == 2)
        def _():
            near_copy(k, 1, 0).start()

    def accumulate(k):
        for way, dev in ((0, left_dev), (1, right_dev)):
            link(yfar.at[k, way], yfar.at[k, way], fsem, (k, way), dev).wait_recv()
            yacc[k, way] = q[4 * k + 1 + way, way] + yfar[k, way]
            near_copy(k, way, way).start()

    def plane_sum(k, h):
        near_wait(k, 0, h).wait_recv()
        near_wait(k, 1, h).wait_recv()
        return q[4 * k + 3, h] + (ynear[k, 0, h] + ynear[k, 1, h])

    def total(k):
        source = chain(k)[3]
        for h in range(2):
            tot[k, h] = plane_sum(k, h)

            @pl.when(jnp.logical_not(source))
            def _():
                zout[k, h] = tot[k, h]
                chain_copy(k, h).start()

    def onward(k):
        z, way, _, source = chain(k)

        @pl.when(source)
        def _():
            for h in range(2):
                link(
                    zin.at[z, way, h], zin.at[z, way, h], zsem, (z, way, h), core_dev
                ).wait_recv()
                zout[k, h] = tot[k, h] + zin[z, way, h]
                chain_copy(k, h).start()

    def step(g, carry):
        k, j = div(g, 4), rem(g, 4)
        d = jnp.where(j == 0, 2, jnp.where(j == 1, 1, jnp.where(j == 2, 3, 0)))
        first = (far_first(zl, k) * 4 + rem(y + d, 4)) * 4
        for h in range(2):
            pbuf[g, h] = tile_row(first + 2 * (1 - c) + h)
        for h in range(2):
            q[g, h] = tile_row(first + 2 * c + h)
        core_copy(g).start()

        @pl.when(g > 0)
        def _():
            finish(g - 1)

        @pl.when((j == 0) & (k > 0))
        def _():
            accumulate(k - 1)

        @pl.when((j == 2) & (k > 0))
        def _():
            total(k - 1)

        @pl.when((j == 0) & (k > 1))
        def _():
            onward(k - 2)

        return carry

    lax.fori_loop(0, 16, step, 0)
    finish(jnp.int32(15))
    accumulate(jnp.int32(3))
    onward(jnp.int32(2))
    for h in range(2):
        out_ref[h] = plane_sum(jnp.int32(3), h)
        for way, there in ((0, zl > 0), (1, zl < 3)):

            @pl.when(there)
            def _():
                link(
                    zin.at[zl, way, h], zin.at[zl, way, h], zsem, (zl, way, h), core_dev
                ).wait_recv()
                out_ref[h] = out_ref[h] + zin[zl, way, h]

    def drain(k, carry):
        for way in range(2):
            far_copy(k, way).wait_send()
            for h in range(2):
                near_copy(k, way, h).wait_send()
        for j in range(4):
            core_copy(4 * k + j).wait_send()

        @pl.when(k < 3)
        def _():
            for h in range(2):
                chain_copy(k, h).wait_send()

        return carry

    lax.fori_loop(0, 4, drain, 0)


def link(src, dst, sems, where, dev):
    return pltpu.make_async_remote_copy(
        src_ref=src,
        dst_ref=dst,
        send_sem=sems[0].at[where],
        recv_sem=sems[1].at[where],
        device_id=dev,
        device_id_type=MESH,
    )


def forward_call(cols, xg, invg, code, pos):
    return pl.pallas_call(
        forward_kernel,
        name="forward_sum",
        out_shape=shape(2, T, T),
        in_specs=[SMEM] + [VMEM] * 4,
        out_specs=VMEM,
        scratch_shapes=[
            pltpu.VMEM((SRC_TILES, 2 * T, T), BF16),
            pltpu.VMEM((16, 2, T, T), F32),
            pltpu.VMEM((16, 2, T, T), F32),
            pltpu.VMEM((16, 2, T, T), F32),
            pltpu.VMEM((4, 2, T, T), F32),
            pltpu.VMEM((4, 2, T, T), F32),
            pltpu.VMEM((4, 2, 2, T, T), F32),
            pltpu.VMEM((4, 2, T, T), F32),
            pltpu.VMEM((4, 2, 2, T, T), F32),
            pltpu.VMEM((4, 2, T, T), F32),
        ]
        + sem_pair(16)
        + sem_pair(4, 2)
        + sem_pair(4, 2, 2)
        + sem_pair(4, 2, 2),
        compiler_params=pltpu.CompilerParams(
            collective_id=2, has_side_effects=True, vmem_limit_bytes=14 * MB
        ),
    )(cols, xg, invg, code, pos)


def gelu_pair(values):
    half = 0.5 * (1.0 + lax.erf(values * 0.7071067811865476))
    slope = half + values * jnp.exp(-0.5 * values * values) * 0.3989422804014327
    return values * half, slope


def node_update(agg_ref, x_ref, inv_ref, w_ref, b_ref, cot_ref, drop_ref, hid_ref, ht_ref, gw_ref):
    weight = w_ref[...]
    total = jnp.zeros((T, 2 * T), F32)
    for h in range(2):
        part = slice(h * T, (h + 1) * T)
        inv_row = jnp.broadcast_to(inv_ref[h : h + 1, :], (T, T))
        inv_col = jnp.transpose(inv_row)
        inv_col = jnp.concatenate([inv_col, inv_col], axis=1)
        agg = agg_ref[h] + jnp.transpose(x_ref[part, :]) * inv_row
        mixed = jnp.dot(
            jnp.transpose(agg), weight, precision=HIGHEST, preferred_element_type=F32
        )
        pre = inv_col * mixed + jnp.broadcast_to(b_ref[...], (T, 2 * T))
        gelu, slope = gelu_pair(pre)
        drop = drop_ref[part, :].astype(F32) / 0.9
        hid_ref[part, :] = gelu * drop
        grad = inv_col * (cot_ref[part, :] * drop * slope)
        ht_ref[h] = lax.dot_general(weight, grad, NT, precision=HIGHEST, preferred_element_type=F32)
        total = total + jnp.dot(agg, grad, precision=HIGHEST, preferred_element_type=F32)
    for k in range(2):
        gw_ref[k * 16 : (k + 1) * 16] = total[:, k * T : (k + 1) * T].reshape(16, 8, T)


BLOCK_ORDER = (
    (0, 0), (0, 1), (0, 3), (1, 0), (0, 2), (2, 0), (1, 1), (1, 3),
    (3, 0), (1, 2), (2, 1), (2, 3), (2, 2), (3, 1), (3, 3), (3, 2),
)


def chosen(g, values):
    out = jnp.int32(values[0])
    for i in range(1, len(values)):
        out = jnp.where(g == i, values[i], out)
    return out


def node_kernel(
    agg_ref,
    x_ref,
    inv_ref,
    w_ref,
    b_ref,
    cot_ref,
    drop_ref,
    code_ref,
    pos_ref,
    hid_ref,
    ht_ref,
    parts_ref,
    gwt_ref,
    g_ref,
    gw_ref,
    gin,
    rin,
    mine,
    gs,
    gr,
    ws,
    wr,
    zs,
    zr,
    ns,
    nr,
    fs,
    fr,
    cs,
    cr,
):
    row, col = position()
    zl, y, c = col_place(col)
    core_dev, right_dev, left_dev, up_dev, down_dev = col_devs(row, zl, y, c)
    gsem, wsem, zsem, nsem, fsem, csem = (
        (gs, gr),
        (ws, wr),
        (zs, zr),
        (ns, nr),
        (fs, fr),
        (cs, cr),
    )
    right, left, across = rem(y + 1, 4), rem(y + 3, 4), rem(y + 2, 4)
    barrier = pltpu.get_barrier_semaphore()

    def greet_col(o, carry):
        signal(barrier, (row, rem(col + o, COLS)))
        return carry

    def greet_row(o, carry):
        signal(barrier, (rem(row + o, ROWS), col))
        return carry

    lax.fori_loop(1, COLS, greet_col, 0)
    lax.fori_loop(1, ROWS, greet_row, 0)
    node_update(agg_ref, x_ref, inv_ref, w_ref, b_ref, cot_ref, drop_ref, hid_ref, ht_ref, gw_ref)
    g_ref[zl, y, c] = ht_ref[...]
    side, wide, lane = hot_iotas()
    pl.semaphore_wait(barrier, COLS + ROWS - 2)

    def plane(k):
        return far_first(zl, 3 - k)

    def z_copy(z, up, h):
        slot = g_ref.at[z, y, c, h]
        return link(slot, slot, zsem, (z, 0 if up else 1, h), up_dev if up else down_dev)

    def near_copy(k, way, h):
        slot = g_ref.at[plane(k), y, c, h]
        return link(slot, slot, nsem, (k, way, h), left_dev if way else right_dev)

    def far_copy(k, h):
        slot = g_ref.at[plane(k), right if h else left, c, h]
        return link(slot, slot, fsem, (k, h), left_dev if h else right_dev)

    def core_copy(k, d):
        slot = g_ref.at[plane(k), rem(y + d, 4), c]
        return link(slot, slot, csem, (k, d), core_dev)

    def core_wait(k, d):
        slot = g_ref.at[plane(k), rem(y + d, 4), 1 - c]
        link(slot, slot, csem, (k, d), core_dev).wait_recv()

    def near_wait(k, way, h):
        slot = g_ref.at[plane(k), right if way else left, c, h]
        link(slot, slot, nsem, (k, way, h), right_dev if way else left_dev).wait_recv()

    def z_arrive(k):
        z = plane(k)
        below = z < zl
        way = jnp.where(below, 0, 1)
        for h in range(2):
            slot = g_ref.at[z, y, c, h]
            link(slot, slot, zsem, (z, way, h), core_dev).wait_recv()

            @pl.when(below & (zl < 3))
            def _():
                z_copy(z, True, h).start()

            @pl.when(jnp.logical_not(below) & (zl > 0))
            def _():
                z_copy(z, False, h).start()

            near_copy(k, h, h).start()
        near_copy(k, 0, 1).start()
        near_copy(k, 1, 0).start()
        core_copy(k, 0).start()

    def y_arrive(k):
        near_wait(k, 0, 0)
        far_copy(k, 0).start()
        near_wait(k, 1, 1)
        far_copy(k, 1).start()
        near_wait(k, 0, 1)
        core_copy(k, 3).start()
        near_wait(k, 1, 0)
        core_copy(k, 1).start()

    def y_far(k):
        for h in range(2):
            slot = g_ref.at[plane(k), across, c, h]
            link(slot, slot, fsem, (k, h), right_dev if h else left_dev).wait_recv()
        core_copy(k, 2).start()

    def tile_row(k, d, cc, h):
        z, yy = plane(k), rem(y + d, 4)
        t = ((z * 4 + yy) * 2 + cc) * 2 + h
        dst = hot_dst(code_ref[pl.ds(t, 1), :], side)
        src = hot_src(pos_ref[pl.ds(t, 1), :], wide, lane)
        picked = jnp.dot(
            split(g_ref[z, yy, cc, h]), dst, preferred_element_type=F32
        ).astype(BF16)
        for p in range(2):
            part = picked[:, p * T : (p + 1) * T]
            hot = src[:, p * T : (p + 1) * T]
            back = lax.dot_general(
                jnp.concatenate([part[:T], part[T:]], axis=1),
                jnp.concatenate([hot, hot], axis=1),
                NT,
                preferred_element_type=F32,
            )
            parts_ref[t, 2 * p] = back[:, :T]
            parts_ref[t, 2 * p + 1] = back[:, T:]

    def use(g, cc):
        k = chosen(g, [b[0] for b in BLOCK_ORDER])
        d = chosen(g, [b[1] for b in BLOCK_ORDER])
        return k, d, cc

    zero = jnp.int32(0)
    for h in range(2):

        @pl.when(zl < 3)
        def _():
            z_copy(zl, True, h).start()

        @pl.when(zl > 0)
        def _():
            z_copy(zl, False, h).start()

        near_copy(zero, h, h).start()
    near_copy(zero, 0, 1).start()
    near_copy(zero, 1, 0).start()
    core_copy(zero, 0).start()

    def scatter(o, carry):
        peer = rem(col + o, COLS)
        link(gw_ref.at[peer], gin.at[o], gsem, o, (row, peer)).start()
        return carry

    lax.fori_loop(1, COLS, scatter, 0)

    def reduce_weight():
        def collect(o, total):
            link(gin.at[o], gin.at[o], gsem, o, (row, rem(col + COLS - o, COLS))).wait_recv()
            return total + gin[o]

        mine[...] = lax.fori_loop(1, COLS, collect, gw_ref[col])
        rin[row] = mine[...]

        def share(o, carry):
            peer = rem(row + o, ROWS)
            link(mine, rin.at[row], wsem, o, (peer, col)).start()
            return carry

        lax.fori_loop(1, ROWS, share, 0)

    def events(g):
        for at, body in (
            (4, lambda: (y_far(zero), z_arrive(zero + 2))),
            (6, lambda: y_arrive(zero + 1)),
            (7, reduce_weight),
            (8, lambda: z_arrive(zero + 3)),
            (9, lambda: (y_far(zero + 1), y_arrive(zero + 2))),
            (12, lambda: (y_far(zero + 2), y_arrive(zero + 3))),
            (15, lambda: y_far(zero + 3)),
        ):

            @pl.when(g == at)
            def _():
                body()

    def step(g, carry):
        events(g)
        k, d, cc = use(g, c)
        kk, dd, pc = use(g - 2, 1 - c)
        core_wait(kk, dd)
        for h in range(2):
            tile_row(k, d, cc, h)
        for h in range(2):
            tile_row(kk, dd, pc, h)
        return carry

    for h in range(2):
        tile_row(zero, zero, c, h)
    z_arrive(zero + 1)
    y_arrive(zero)
    for h in range(2):
        tile_row(zero, zero + 1, c, h)
    lax.fori_loop(2, 16, step, 0)

    def last(g, carry):
        kk, dd, pc = use(g, 1 - c)
        core_wait(kk, dd)
        for h in range(2):
            tile_row(kk, dd, pc, h)
        return carry

    lax.fori_loop(14, 16, last, 0)

    def finish_row(o, carry):
        peer = rem(row + ROWS - o, ROWS)
        copy = link(rin.at[peer], rin.at[peer], wsem, o, (peer, col))
        copy.wait_recv()
        copy.wait_send()
        return carry

    lax.fori_loop(1, ROWS, finish_row, 0)
    total = rin[0]
    for r in range(1, ROWS):
        total = total + rin[r]
    gwt_ref[...] = total

    def drain(k, carry):
        z = plane(k)
        for d in range(4):
            core_copy(k, d).wait_send()
        for h in range(2):
            far_copy(k, h).wait_send()
            near_copy(k, 0, h).wait_send()
            near_copy(k, 1, h).wait_send()

            @pl.when((z <= zl) & (zl < 3))
            def _():
                z_copy(z, True, h).wait_send()

            @pl.when((z >= zl) & (zl > 0))
            def _():
                z_copy(z, False, h).wait_send()

        return carry

    lax.fori_loop(0, 4, drain, 0)

    def finish_col(o, carry):
        link(gin.at[o], gin.at[o], gsem, o, (row, rem(col + o, COLS))).wait_send()
        return carry

    lax.fori_loop(1, COLS, finish_col, 0)


def node_call(agg, x, inv, weight, bias, cot, drop, code, pos):
    return pl.pallas_call(
        node_kernel,
        name="node_spread",
        out_shape=(
            shape(2 * T, 2 * T),
            shape(2, T, T),
            shape(TILE_ROWS, TPR, T, T),
            shape(8, T),
        ),
        in_specs=[VMEM] * 9,
        out_specs=(VMEM,) * 4,
        scratch_shapes=[
            pltpu.VMEM((4, 4, 2, 2, T, T), F32),
            pltpu.VMEM((COLS, 8, T), F32),
            pltpu.VMEM((COLS, 8, T), F32),
            pltpu.VMEM((ROWS, 8, T), F32),
            pltpu.VMEM((8, T), F32),
        ]
        + sem_pair(COLS)
        + sem_pair(ROWS)
        + sem_pair(4, 2, 2)
        + sem_pair(4, 2, 2)
        + sem_pair(4, 2)
        + sem_pair(4, 4),
        compiler_params=pltpu.CompilerParams(
            collective_id=3, has_side_effects=True, vmem_limit_bytes=12 * MB
        ),
    )(agg, x, inv, weight, bias.reshape(1, 2 * T), cot, drop, code, pos)


def place_kernel(cols_ref, parts_ref, out_ref):
    out_ref[...] = jnp.zeros_like(out_ref)

    def tile_row(t, carry):
        for k in range(TPR):
            out_ref[cols_ref[t, k]] += parts_ref[t, k]
        return carry

    lax.fori_loop(0, TILE_ROWS, tile_row, 0, unroll=2)


def place_call(cols, parts):
    return pl.pallas_call(
        place_kernel,
        name="place_tiles",
        out_shape=shape(SRC_TILES, T, T),
        in_specs=[SMEM, VMEM],
        out_specs=VMEM,
        compiler_params=pltpu.CompilerParams(vmem_limit_bytes=4 * MB),
    )(cols, parts)


def sum_row_kernel(
    q_ref,
    ht_ref,
    inv_ref,
    gwt_ref,
    gf_ref,
    gw_ref,
    xfar,
    xacc,
    xnear,
    tot,
    zin,
    gbuf,
    gs,
    gr,
    zs,
    zr,
    ns,
    nr,
    fs,
    fr,
):
    row, col = position()
    zh, x = div(row, 4), rem(row, 4)
    gsem, zsem, nsem, fsem = (gs, gr), (zs, zr), (ns, nr), (fs, fr)
    right_dev, left_dev, pair_dev = (
        (zh * 4 + rem(x + 1, 4), col),
        (zh * 4 + rem(x + 3, 4), col),
        ((1 - zh) * 4 + x, col),
    )
    gbuf[col] = gwt_ref[...]
    barrier = pltpu.get_barrier_semaphore()

    def greet_col(o, carry):
        signal(barrier, (row, rem(col + o, COLS)))
        return carry

    lax.fori_loop(1, COLS, greet_col, 0)
    for dev in (right_dev, left_dev, pair_dev):
        signal(barrier, dev)
    pl.semaphore_wait(barrier, COLS - 1 + 3)

    sent = []
    base = ((1 - zh) * 4, zh * 4)

    def block(k, d):
        return base[k] + rem(x + d, 4)

    for k in range(2):
        b2, b1, b3 = block(k, 2), block(k, 1), block(k, 3)
        sent.append(send(q_ref.at[b2, 0], xfar.at[k, 0], fsem, (k, 0), right_dev))
        sent.append(send(q_ref.at[b2, 1], xfar.at[k, 1], fsem, (k, 1), left_dev))
        sent.append(send(q_ref.at[b1, 1], xnear.at[k, 0, 1], nsem, (k, 0, 1), right_dev))
        sent.append(send(q_ref.at[b3, 0], xnear.at[k, 1, 0], nsem, (k, 1, 0), left_dev))

    def gather(o, carry):
        peer = rem(col + o, COLS)
        send(gwt_ref, gbuf.at[col], gsem, o, (row, peer))
        return carry

    lax.fori_loop(1, COLS, gather, 0)
    for k in range(2):
        handle(xfar.at[k, 0], fsem, (k, 0), left_dev).wait_recv()
        xacc[k, 0] = q_ref[block(k, 1), 0] + xfar[k, 0]
        sent.append(send(xacc.at[k, 0], xnear.at[k, 0, 0], nsem, (k, 0, 0), right_dev))
        handle(xfar.at[k, 1], fsem, (k, 1), right_dev).wait_recv()
        xacc[k, 1] = q_ref[block(k, 3), 1] + xfar[k, 1]
        sent.append(send(xacc.at[k, 1], xnear.at[k, 1, 1], nsem, (k, 1, 1), left_dev))
    for k in range(2):
        for h in range(2):
            for way, dev in ((0, left_dev), (1, right_dev)):
                handle(xnear.at[k, way, h], nsem, (k, way, h), dev).wait_recv()
            tot[k, h] = q_ref[block(k, 0), h] + (xnear[k, 0, h] + xnear[k, 1, h])
            if k == 0:
                sent.append(send(tot.at[0, h], zin.at[h], zsem, h, pair_dev))

    def collect(o, carry):
        peer = rem(col + COLS - o, COLS)
        copy = handle(gbuf.at[peer], gsem, o, (row, peer))
        copy.wait_recv()
        copy.wait_send()
        return carry

    lax.fori_loop(1, COLS, collect, 0)
    for k in range(2):
        gw_ref[:, k * T : (k + 1) * T] = gbuf[k * 16 : (k + 1) * 16].reshape(T, T)
    for h in range(2):
        handle(zin.at[h], zsem, h, pair_dev).wait_recv()
        back = (tot[1, h] + zin[h]) + ht_ref[h]
        gf_ref[h * T : (h + 1) * T, :] = jnp.transpose(
            back * jnp.broadcast_to(inv_ref[h : h + 1, :], (T, T))
        )
    for copy in sent:
        copy.wait_send()


def sum_row_call(parts, ht, inv, gwt):
    return pl.pallas_call(
        sum_row_kernel,
        name="sum_over_row",
        out_shape=(shape(2 * T, T), shape(T, 2 * T)),
        in_specs=[VMEM] * 4,
        out_specs=(VMEM,) * 2,
        scratch_shapes=[
            pltpu.VMEM((2, 2, T, T), F32),
            pltpu.VMEM((2, 2, T, T), F32),
            pltpu.VMEM((2, 2, 2, T, T), F32),
            pltpu.VMEM((2, 2, T, T), F32),
            pltpu.VMEM((2, T, T), F32),
            pltpu.VMEM((COLS, 8, T), F32),
        ]
        + sem_pair(COLS)
        + sem_pair(2)
        + sem_pair(2, 2, 2)
        + sem_pair(2, 2),
        compiler_params=pltpu.CompilerParams(
            collective_id=4, has_side_effects=True, vmem_limit_bytes=16 * MB
        ),
    )(parts.reshape(ROWS, 2, T, T), ht, inv, gwt)


def shards(features, weight, bias, cot, drop, tile_cols, counts, pos, keep):
    cols, pos = tile_cols[0, 0], pos[0, 0]
    xg, invg, inv, code = gather_call(features, counts[0, 0], pos, keep[0, 0])
    agg = forward_call(cols, xg, invg, code, pos)
    hidden, ht, parts, gwt = node_call(agg, features, inv, weight, bias, cot, drop, code, pos)
    back = place_call(cols, parts)
    grad_features, grad_weight = sum_row_call(back, ht, inv, gwt)
    return hidden, grad_features, grad_weight


def solution(mesh):
    nodes = P(("row", "col"), None)
    block = P("row", "col", None, None)
    return jax.shard_map(
        shards,
        mesh=mesh,
        in_specs=(nodes, P(), P(), nodes, nodes, block, block, block, block),
        out_specs=(nodes, nodes, P()),
        check_vma=False,
    )
```

```python
from types import SimpleNamespace

import jax
import jax.numpy as jnp
from jax import lax
from jax.experimental import pallas as pl
from jax.experimental.pallas import tpu as pltpu
from jax.sharding import PartitionSpec as P

MESH = pl.DeviceIdType.MESH
HIGHEST = lax.Precision.HIGHEST
F32, BF16, I32 = jnp.float32, jnp.bfloat16, jnp.int32

T = 128
ROWS, COLS = 8, 32
TILE_ROWS, TPR, EPT = 64, 4, 64
SLOTS = TPR * EPT
SRC_TILES = 16
MB = 1 << 20
VMEM = pl.BlockSpec(memory_space=pltpu.VMEM)
HBM = pl.BlockSpec(memory_space=pltpu.HBM)
NT = (((1,), (1,)), ((), ()))


def in_hbm(array):
    return pltpu.with_memory_space_constraint(array, pltpu.HBM)


def rem(a, n):
    return lax.rem(a, jnp.int32(n))


def div(a, n):
    return lax.div(a, jnp.int32(n))


def shape(*dims, dtype=F32):
    return jax.ShapeDtypeStruct(dims, dtype)


def link(src, dst, sems, where, dev):
    return pltpu.make_async_remote_copy(
        src_ref=src,
        dst_ref=dst,
        send_sem=sems.send.at[where],
        recv_sem=sems.recv.at[where],
        device_id=dev,
        device_id_type=MESH,
    )


def arrival(ref, sems, where, dev):
    link(ref, ref, sems, where, dev).wait_recv()


def signal(barrier, dev):
    pl.semaphore_signal(barrier, inc=1, device_id=dev, device_id_type=MESH)


def named(names, refs, pairs=()):
    out = SimpleNamespace(**dict(zip(names, refs)))
    rest = refs[len(names) :]
    for i, name in enumerate(pairs):
        setattr(out, name, SimpleNamespace(send=rest[2 * i], recv=rest[2 * i + 1]))
    return out


def sem_pairs(dims):
    return [pltpu.SemaphoreType.DMA(d) for d in dims for _ in range(2)]


def each(low, high, body):
    def run(o, carry):
        body(o)
        return carry

    lax.fori_loop(low, high, run, 0)


def slot_codes(counts, pos, keep):
    lane = lax.broadcasted_iota(I32, (TILE_ROWS, SLOTS), 1)
    counts = jnp.transpose(counts)
    limit = jnp.broadcast_to(counts[:, 0:1], (TILE_ROWS, SLOTS))
    for k in range(1, TPR):
        limit = jnp.where(
            lane >= k * EPT, jnp.broadcast_to(counts[:, k : k + 1], (TILE_ROWS, SLOTS)), limit
        )
    live = ((lane & (EPT - 1)) < limit) & (keep == 1)
    return jnp.where(live, pos >> 7, 4 * T)


def split(values, axis):
    high = values.astype(BF16)
    low = (values - high.astype(F32)).astype(BF16)
    return jnp.concatenate([high, low], axis=axis)


def hot_dst(code_row, side):
    return jnp.where(side == jnp.broadcast_to(code_row, (T, SLOTS)), 1.0, 0.0).astype(BF16)


def hot_src(pos_row, side, lane):
    code = (pos_row & (T - 1)) + ((lane >> 6) & 1) * T
    return jnp.where(side == jnp.broadcast_to(code, (2 * T, SLOTS)), 1.0, 0.0).astype(BF16)


def gelu_pair(values):
    half = 0.5 * (1.0 + lax.erf(values * 0.7071067811865476))
    slope = half + values * jnp.exp(-0.5 * values * values) * 0.3989422804014327
    return values * half, slope


def far_first(zl, k):
    near = jnp.where(zl >= 2, 3 - zl, zl)
    inner = jnp.where(k == 0, 3, jnp.where(k == 1, 0, 4 - k))
    plane = jnp.where(near == 0, 3 - k, inner)
    return jnp.where(zl >= 2, 3 - plane, plane)


def chosen(g, values):
    out = jnp.int32(values[0])
    for i in range(1, len(values)):
        out = jnp.where(g == i, values[i], out)
    return out


class Place:
    def __init__(self):
        self.row, self.col = lax.axis_index("row"), lax.axis_index("col")
        self.zh, self.x = div(self.row, 4), rem(self.row, 4)
        self.zl, self.y, self.c = div(self.col, 8), rem(div(self.col, 2), 4), rem(self.col, 2)

    def in_row(self, zh, x):
        return (zh * 4 + x, self.col)

    def in_col(self, zl, y, c):
        return (self.row, (zl * 4 + y) * 2 + c)


def gather_features(p, r, barrier_wait):
    row, col, zh, x = p.row, p.col, p.zh, p.x
    pair = 1 - zh
    right, left = rem(x + 1, 4), rem(x + 3, 4)
    right_dev, left_dev, pair_dev = p.in_row(zh, right), p.in_row(zh, left), p.in_row(pair, x)
    for h in range(2):
        r.xg[row, h] = jnp.transpose(r.x[h * T : (h + 1) * T, :])
    r.code[...] = slot_codes(r.counts[...], r.pos[...], r.keep[...])
    barrier_wait()

    def near_copy(k, zz, way, h):
        slot = r.xg.at[zz * 4 + x, h]
        return link(slot, slot, r.xnear, (k, way, h), left_dev if way else right_dev)

    def far_copy(k, zz, h):
        slot = r.xg.at[zz * 4 + (right if h else left), h]
        return link(slot, slot, r.xfar, (k, h), left_dev if h else right_dev)

    def near_wait(k, zz, way, h):
        slot = r.xg.at[zz * 4 + (right if way else left), h]
        arrival(slot, r.xnear, (k, way, h), right_dev if way else left_dev)

    def pair_copy(h):
        return link(r.xg.at[row, h], r.xg.at[row, h], r.xpair, h, pair_dev)

    def forward(k, zz):
        for h in range(2):
            near_wait(k, zz, h, h)
            far_copy(k, zz, h).start()

    def rest(k, zz):
        for h in range(2):
            near_wait(k, zz, 1 - h, h)
            slot = r.xg.at[zz * 4 + rem(x + 2, 4), h]
            arrival(slot, r.xfar, (k, h), right_dev if h else left_dev)

    for h in range(2):
        pair_copy(h).start()
    for way, h in ((0, 0), (1, 1), (0, 1), (1, 0)):
        near_copy(0, zh, way, h).start()

    ones = jnp.ones((8, SLOTS), BF16)
    side = lax.broadcasted_iota(I32, (T, SLOTS), 0)
    wide = lax.broadcasted_iota(I32, (2 * T, SLOTS), 0)
    lane = lax.broadcasted_iota(I32, (1, SLOTS), 1)
    sub = lax.broadcasted_iota(I32, (8, T), 0)

    def count(i, carry):
        for u in range(2):
            j = 2 * i + u
            halves = []
            for h in range(2):
                hot = hot_dst(r.code[pl.ds(2 * j + h, 1), :], side)
                halves.append(lax.dot_general(ones, hot, NT, preferred_element_type=F32))
            r.deg[j] = jnp.where(sub == 0, halves[0], jnp.where(sub == 1, halves[1], 0.0))
        return carry

    lax.fori_loop(0, COLS // 2, count, 0)

    def degree_copy(o):
        peer = rem(col + o, COLS)
        return link(r.deg.at[peer], r.degin.at[o], r.dsem, o, (row, peer))

    each(1, COLS, lambda o: degree_copy(o).start())
    forward(0, zh)

    def block(i, carry):
        for u in range(4):
            t = 4 * i + u
            dst = hot_dst(r.code[pl.ds(t, 1), :], side)
            src = hot_src(r.pos[pl.ds(t, 1), :], wide, lane)
            for q in range(2):
                part = slice(q * T, (q + 1) * T)
                r.adj[t, :, q * 2 * T : (q + 1) * 2 * T] = lax.dot_general(
                    dst[:, part], src[:, part], NT, preferred_element_type=F32
                ).astype(BF16)
        return carry

    lax.fori_loop(0, 5, block, 0)
    for h in range(2):
        arrival(r.xg.at[pair * 4 + x, h], r.xpair, h, pair_dev)
        near_copy(1, pair, h, h).start()
        near_copy(1, pair, 1 - h, h).start()

    def collect(o, total):
        arrival(r.degin.at[o], r.dsem, o, (row, rem(col + COLS - o, COLS)))
        return total + r.degin[o]

    total = lax.fori_loop(1, COLS, collect, r.deg[col])
    inv = lax.rsqrt(1.0 + total)
    r.inv[...] = inv
    r.invg[row] = inv

    def inv_copy(o):
        return link(r.inv, r.invg.at[row], r.vsem, o, (rem(row + o, ROWS), col))

    each(1, ROWS, lambda o: inv_copy(o).start())
    lax.fori_loop(5, 10, block, 0)
    forward(1, pair)
    lax.fori_loop(10, 16, block, 0)
    rest(0, zh)

    def inv_wait(o):
        peer = rem(row + ROWS - o, ROWS)
        arrival(r.invg.at[peer], r.vsem, o, (peer, col))

    each(1, ROWS, inv_wait)
    rest(1, pair)

    def drain():
        for h in range(2):
            pair_copy(h).wait_send()
            for k, zz in ((0, zh), (1, pair)):
                far_copy(k, zz, h).wait_send()
                for way in range(2):
                    near_copy(k, zz, way, h).wait_send()
        each(1, ROWS, lambda o: inv_copy(o).wait_send())
        each(1, COLS, lambda o: degree_copy(o).wait_send())

    return drain


def forward_sum(p, r, out_ref):
    row, zl, y, c = p.row, p.zl, p.y, p.c
    core_dev = p.in_col(zl, y, 1 - c)
    right_dev, left_dev = p.in_col(zl, rem(y + 1, 4), c), p.in_col(zl, rem(y + 3, 4), c)
    for u in range(SRC_TILES):
        i, h = u // 2, u % 2
        r.scaled[u] = split(
            r.xg[i, h] * jnp.broadcast_to(r.invg[i, h : h + 1, :], (T, T)), axis=0
        )
    q = r.q

    def tile_row(t):
        panel = jnp.concatenate([r.scaled[r.cols[k, t]] for k in range(TPR)], axis=1)
        both = lax.dot_general(panel, r.adj[t], NT, preferred_element_type=F32)
        return both[:T] + both[T:]

    def core_copy(g):
        return link(r.pbuf.at[g], r.cbuf.at[g], r.fcore, g, core_dev)

    def far_copy(k, way):
        return link(
            q.at[4 * k, way],
            r.yfar.at[k, way],
            r.ffar,
            (k, way),
            left_dev if way else right_dev,
        )

    def near_copy(k, way, h):
        src = r.yacc.at[k, way] if way == h else q.at[4 * k + 1 + way, h]
        return link(
            src, r.ynear.at[k, way, h], r.fnear, (k, way, h), left_dev if way else right_dev
        )

    def chain(k):
        z = far_first(zl, k)
        down = z < zl
        way = jnp.where(down, 1, 0)
        onward = p.in_col(jnp.where(down, zl - 1, zl + 1), y, c)
        source = jnp.where(down, zl < 3, zl > 0)
        return z, way, onward, source

    def chain_copy(k, h):
        z, way, onward, _ = chain(k)
        return link(r.zout.at[k, h], r.zin.at[z, way, h], r.fchain, (z, way, h), onward)

    def finish(g):
        k, j = div(g, 4), rem(g, 4)
        core_copy(g).wait_recv()
        q[g] = q[g] + r.cbuf[g]

        @pl.when(j == 0)
        def _():
            far_copy(k, 0).start()
            far_copy(k, 1).start()

        @pl.when(j == 1)
        def _():
            near_copy(k, 0, 1).start()

        @pl.when(j == 2)
        def _():
            near_copy(k, 1, 0).start()

    def accumulate(k):
        for way, dev in ((0, left_dev), (1, right_dev)):
            arrival(r.yfar.at[k, way], r.ffar, (k, way), dev)
            r.yacc[k, way] = q[4 * k + 1 + way, way] + r.yfar[k, way]
            near_copy(k, way, way).start()

    def plane_sum(k, h):
        arrival(r.ynear.at[k, 0, h], r.fnear, (k, 0, h), left_dev)
        arrival(r.ynear.at[k, 1, h], r.fnear, (k, 1, h), right_dev)
        return q[4 * k + 3, h] + (r.ynear[k, 0, h] + r.ynear[k, 1, h])

    def total(k):
        source = chain(k)[3]
        for h in range(2):
            r.tot[k, h] = plane_sum(k, h)

            @pl.when(jnp.logical_not(source))
            def _():
                r.zout[k, h] = r.tot[k, h]
                chain_copy(k, h).start()

    def onward(k):
        z, way, _, source = chain(k)

        @pl.when(source)
        def _():
            for h in range(2):
                arrival(r.zin.at[z, way, h], r.fchain, (z, way, h), core_dev)
                r.zout[k, h] = r.tot[k, h] + r.zin[z, way, h]
                chain_copy(k, h).start()

    def step(g, carry):
        k, j = div(g, 4), rem(g, 4)
        d = chosen(j, (2, 1, 3, 0))
        first = (far_first(zl, k) * 4 + rem(y + d, 4)) * 4
        for h in range(2):
            r.pbuf[g, h] = tile_row(first + 2 * (1 - c) + h)
        for h in range(2):
            q[g, h] = tile_row(first + 2 * c + h)
        core_copy(g).start()

        @pl.when(g > 0)
        def _():
            finish(g - 1)

        @pl.when((j == 0) & (k > 0))
        def _():
            accumulate(k - 1)

        @pl.when((j == 2) & (k > 0))
        def _():
            total(k - 1)

        @pl.when((j == 0) & (k > 1))
        def _():
            onward(k - 2)

        return carry

    lax.fori_loop(0, 16, step, 0)
    finish(jnp.int32(15))
    accumulate(jnp.int32(3))
    onward(jnp.int32(2))
    for h in range(2):
        out_ref[h] = plane_sum(jnp.int32(3), h)
        for way, there in ((0, zl > 0), (1, zl < 3)):

            @pl.when(there)
            def _():
                arrival(r.zin.at[zl, way, h], r.fchain, (zl, way, h), core_dev)
                out_ref[h] = out_ref[h] + r.zin[zl, way, h]

    def drain_plane(k):
        for way in range(2):
            far_copy(k, way).wait_send()
            for h in range(2):
                near_copy(k, way, h).wait_send()
        for j in range(4):
            core_copy(4 * k + j).wait_send()

        @pl.when(k < 3)
        def _():
            for h in range(2):
                chain_copy(k, h).wait_send()

    return lambda: each(0, 4, drain_plane)


def node_update(r, hid_ref, ht_ref):
    weight = r.w[...]
    bias = jnp.broadcast_to(r.b[...], (T, 2 * T))
    total = jnp.zeros((T, 2 * T), F32)
    for h in range(2):
        part = slice(h * T, (h + 1) * T)
        inv_row = jnp.broadcast_to(r.inv[h : h + 1, :], (T, T))
        inv_col = jnp.transpose(inv_row)
        inv_col = jnp.concatenate([inv_col, inv_col], axis=1)
        agg = r.agg[h] + jnp.transpose(r.x[part, :]) * inv_row
        mixed = jnp.dot(
            jnp.transpose(agg), weight, precision=HIGHEST, preferred_element_type=F32
        )
        gelu, slope = gelu_pair(inv_col * mixed + bias)
        drop = r.drop[part, :].astype(F32) / 0.9
        hid_ref[part, :] = gelu * drop
        grad = inv_col * (r.cot[part, :] * drop * slope)
        ht_ref[h] = lax.dot_general(weight, grad, NT, precision=HIGHEST, preferred_element_type=F32)
        total = total + jnp.dot(agg, grad, precision=HIGHEST, preferred_element_type=F32)
    for k in range(2):
        r.gw[k * 16 : (k + 1) * 16] = total[:, k * T : (k + 1) * T].reshape(16, 8, T)


BLOCK_ORDER = (
    (0, 0), (0, 1), (0, 3), (1, 0), (0, 2), (2, 0), (1, 1), (1, 3),
    (3, 0), (1, 2), (2, 1), (2, 3), (2, 2), (3, 1), (3, 3), (3, 2),
)


def spread_gradients(p, r, ht_ref, parts_ref, gwo_ref):
    row, col, zl, y, c = p.row, p.col, p.zl, p.y, p.c
    right, left, across = rem(y + 1, 4), rem(y + 3, 4), rem(y + 2, 4)
    core_dev = p.in_col(zl, y, 1 - c)
    right_dev, left_dev = p.in_col(zl, right, c), p.in_col(zl, left, c)
    up_dev = p.in_col(jnp.minimum(zl + 1, 3), y, c)
    down_dev = p.in_col(jnp.maximum(zl - 1, 0), y, c)
    r.g[zl, y, c] = ht_ref[...]

    def plane(k):
        return far_first(zl, 3 - k)

    def z_copy(z, up, h):
        slot = r.g.at[z, y, c, h]
        return link(slot, slot, r.gchain, (z, 0 if up else 1, h), up_dev if up else down_dev)

    def near_copy(k, way, h):
        slot = r.g.at[plane(k), y, c, h]
        return link(slot, slot, r.gnear, (k, way, h), left_dev if way else right_dev)

    def far_copy(k, h):
        slot = r.g.at[plane(k), right if h else left, c, h]
        return link(slot, slot, r.gfar, (k, h), left_dev if h else right_dev)

    def core_copy(k, d):
        slot = r.g.at[plane(k), rem(y + d, 4), c]
        return link(slot, slot, r.gcore, (k, d), core_dev)

    def core_wait(k, d):
        arrival(r.g.at[plane(k), rem(y + d, 4), 1 - c], r.gcore, (k, d), core_dev)

    def near_wait(k, way, h):
        slot = r.g.at[plane(k), right if way else left, c, h]
        arrival(slot, r.gnear, (k, way, h), right_dev if way else left_dev)

    def z_arrive(k):
        z = plane(k)
        below = z < zl
        way = jnp.where(below, 0, 1)
        for h in range(2):
            arrival(r.g.at[z, y, c, h], r.gchain, (z, way, h), core_dev)

            @pl.when(below & (zl < 3))
            def _():
                z_copy(z, True, h).start()

            @pl.when(jnp.logical_not(below) & (zl > 0))
            def _():
                z_copy(z, False, h).start()

            near_copy(k, h, h).start()
        near_copy(k, 0, 1).start()
        near_copy(k, 1, 0).start()
        core_copy(k, 0).start()

    def y_arrive(k):
        near_wait(k, 0, 0)
        far_copy(k, 0).start()
        near_wait(k, 1, 1)
        far_copy(k, 1).start()
        near_wait(k, 0, 1)
        core_copy(k, 3).start()
        near_wait(k, 1, 0)
        core_copy(k, 1).start()

    def y_far(k):
        for h in range(2):
            arrival(
                r.g.at[plane(k), across, c, h], r.gfar, (k, h), right_dev if h else left_dev
            )
        core_copy(k, 2).start()

    def tile_row(k, d, cc, h):
        z, yy = plane(k), rem(y + d, 4)
        t = ((z * 4 + yy) * 2 + cc) * 2 + h
        adj = r.adj[t]
        back = jnp.dot(
            split(r.g[z, yy, cc, h], axis=1),
            jnp.concatenate([adj, adj], axis=0),
            preferred_element_type=F32,
        )
        for i in range(TPR):
            parts_ref[t, i] = back[:, i * T : (i + 1) * T]

    def use(g):
        return chosen(g, [b[0] for b in BLOCK_ORDER]), chosen(g, [b[1] for b in BLOCK_ORDER])

    zero = jnp.int32(0)
    for h in range(2):

        @pl.when(zl < 3)
        def _():
            z_copy(zl, True, h).start()

        @pl.when(zl > 0)
        def _():
            z_copy(zl, False, h).start()

        near_copy(zero, h, h).start()
    near_copy(zero, 0, 1).start()
    near_copy(zero, 1, 0).start()
    core_copy(zero, 0).start()

    def scatter_copy(o):
        peer = rem(col + o, COLS)
        return link(r.gw.at[peer], r.gin.at[o], r.gsem, o, (row, peer))

    def share_copy(o):
        return link(r.mine, r.rin.at[row], r.wsem, o, (rem(row + o, ROWS), col))

    def return_copy(o):
        return link(r.full.at[col], r.full.at[col], r.bsem, o, (row, rem(col + o, COLS)))

    each(1, COLS, lambda o: scatter_copy(o).start())

    def reduce_col():
        def collect(o, total):
            arrival(r.gin.at[o], r.gsem, o, (row, rem(col + COLS - o, COLS)))
            return total + r.gin[o]

        r.mine[...] = lax.fori_loop(1, COLS, collect, r.gw[col])
        r.rin[row] = r.mine[...]
        each(1, ROWS, lambda o: share_copy(o).start())

    def reduce_row():
        def wait(o):
            peer = rem(row + ROWS - o, ROWS)
            arrival(r.rin.at[peer], r.wsem, o, (peer, col))

        each(1, ROWS, wait)
        total = r.rin[0]
        for i in range(1, ROWS):
            total = total + r.rin[i]
        r.full[col] = total
        each(1, COLS, lambda o: return_copy(o).start())

    def events(g):
        for at, body in (
            (4, lambda: (y_far(zero), z_arrive(zero + 2))),
            (6, lambda: y_arrive(zero + 1)),
            (7, reduce_col),
            (8, lambda: z_arrive(zero + 3)),
            (9, lambda: (y_far(zero + 1), y_arrive(zero + 2))),
            (11, reduce_row),
            (12, lambda: (y_far(zero + 2), y_arrive(zero + 3))),
            (15, lambda: y_far(zero + 3)),
        ):

            @pl.when(g == at)
            def _():
                body()

    def step(g, carry):
        events(g)
        k, d = use(g)
        kk, dd = use(g - 2)
        core_wait(kk, dd)
        for h in range(2):
            tile_row(k, d, c, h)
        for h in range(2):
            tile_row(kk, dd, 1 - c, h)
        return carry

    for h in range(2):
        tile_row(zero, zero, c, h)
    z_arrive(zero + 1)
    y_arrive(zero)
    for h in range(2):
        tile_row(zero, zero + 1, c, h)
    lax.fori_loop(2, 16, step, 0)

    def last(g):
        kk, dd = use(g)
        core_wait(kk, dd)
        for h in range(2):
            tile_row(kk, dd, 1 - c, h)

    each(14, 16, last)

    def return_wait(o):
        peer = rem(col + COLS - o, COLS)
        arrival(r.full.at[peer], r.bsem, o, (row, peer))

    each(1, COLS, return_wait)
    for k in range(2):
        gwo_ref[:, k * T : (k + 1) * T] = r.full[k * 16 : (k + 1) * 16].reshape(T, T)

    def drain_plane(k):
        z = plane(k)
        for d in range(4):
            core_copy(k, d).wait_send()
        for h in range(2):
            far_copy(k, h).wait_send()
            near_copy(k, 0, h).wait_send()
            near_copy(k, 1, h).wait_send()

            @pl.when((z <= zl) & (zl < 3))
            def _():
                z_copy(z, True, h).wait_send()

            @pl.when((z >= zl) & (zl > 0))
            def _():
                z_copy(z, False, h).wait_send()

    def drain():
        each(0, 4, drain_plane)

        def sent(o):
            scatter_copy(o).wait_send()
            return_copy(o).wait_send()

        each(1, COLS, sent)
        each(1, ROWS, lambda o: share_copy(o).wait_send())

    return drain


SOURCES = ("cols", "x", "counts", "pos", "keep", "w", "b", "cot", "drop")
RESULTS = ("hid", "ht", "invo", "parts", "gwo")
BUFFERS = {
    "cols": ((TPR, TILE_ROWS), I32),
    "x": ((2 * T, T), F32),
    "counts": ((TPR, TILE_ROWS), I32),
    "pos": ((TILE_ROWS, SLOTS), I32),
    "keep": ((TILE_ROWS, SLOTS), I32),
    "w": ((T, 2 * T), F32),
    "b": ((1, 2 * T), F32),
    "cot": ((2 * T, 2 * T), F32),
    "drop": ((2 * T, 2 * T), I32),
    "code": ((TILE_ROWS, SLOTS), I32),
    "xg": ((ROWS, 2, T, T), F32),
    "deg": ((COLS, 8, T), F32),
    "degin": ((COLS, 8, T), F32),
    "inv": ((8, T), F32),
    "invg": ((ROWS, 8, T), F32),
    "adj": ((TILE_ROWS, T, TPR * T), BF16),
    "scaled": ((SRC_TILES, 2 * T, T), BF16),
    "pbuf": ((16, 2, T, T), F32),
    "cbuf": ((16, 2, T, T), F32),
    "q": ((16, 2, T, T), F32),
    "yfar": ((4, 2, T, T), F32),
    "yacc": ((4, 2, T, T), F32),
    "ynear": ((4, 2, 2, T, T), F32),
    "tot": ((4, 2, T, T), F32),
    "zin": ((4, 2, 2, T, T), F32),
    "zout": ((4, 2, T, T), F32),
    "agg": ((2, T, T), F32),
    "g": ((4, 4, 2, 2, T, T), F32),
    "gw": ((COLS, 8, T), F32),
    "gin": ((COLS, 8, T), F32),
    "rin": ((ROWS, 8, T), F32),
    "mine": ((8, T), F32),
    "full": ((COLS, 8, T), F32),
}
LINKS = {
    "xpair": (2,),
    "xnear": (2, 2, 2),
    "xfar": (2, 2),
    "dsem": (COLS,),
    "vsem": (ROWS,),
    "fcore": (16,),
    "ffar": (4, 2),
    "fnear": (4, 2, 2),
    "fchain": (4, 2, 2),
    "gchain": (4, 2, 2),
    "gnear": (4, 2, 2),
    "gfar": (4, 2),
    "gcore": (4, 4),
    "gsem": (COLS,),
    "wsem": (ROWS,),
    "bsem": (COLS,),
}
LOADS = SOURCES


def layer_kernel(*refs):
    inputs = named(SOURCES, refs)
    outputs = named(RESULTS, refs[len(SOURCES) :])
    r = named(tuple(BUFFERS), refs[len(SOURCES) + len(RESULTS) : -1], tuple(LINKS))
    p = Place()
    loads = {
        name: pltpu.make_async_copy(getattr(inputs, name), getattr(r, name), refs[-1].at[i])
        for i, name in enumerate(LOADS)
    }
    for copy in loads.values():
        copy.start()
    barrier = pltpu.get_barrier_semaphore()
    each(1, COLS, lambda o: signal(barrier, (p.row, rem(p.col + o, COLS))))
    each(1, ROWS, lambda o: signal(barrier, (rem(p.row + o, ROWS), p.col)))
    for copy in loads.values():
        copy.wait()
    drain_gather = gather_features(p, r, lambda: pl.semaphore_wait(barrier, COLS + ROWS - 2))
    drain_forward = forward_sum(p, r, r.agg)
    node_update(r, outputs.hid, outputs.ht)
    drain_spread = spread_gradients(p, r, outputs.ht, outputs.parts, outputs.gwo)
    outputs.invo[...] = r.inv[...]
    drain_gather()
    drain_forward()
    drain_spread()


def layer_call(*args):
    return pl.pallas_call(
        layer_kernel,
        name="layer",
        out_shape=(
            shape(2 * T, 2 * T),
            shape(2, T, T),
            shape(8, T),
            shape(TILE_ROWS, TPR, T, T),
            shape(T, 2 * T),
        ),
        in_specs=[HBM] * 9,
        out_specs=(VMEM,) * 5,
        scratch_shapes=[
            (pltpu.SMEM if name == "cols" else pltpu.VMEM)(dims, dtype)
            for name, (dims, dtype) in BUFFERS.items()
        ]
        + sem_pairs(LINKS.values())
        + [pltpu.SemaphoreType.DMA((len(LOADS),))],
        compiler_params=pltpu.CompilerParams(
            collective_id=1, has_side_effects=True, vmem_limit_bytes=32 * MB
        ),
    )(*[in_hbm(arg) for arg in args])


def place_kernel(
    cols_hbm, parts_ref, hid_ref, gw_ref, out_ref, hid_out, gw_out, cols_ref, sems
):
    copy = pltpu.make_async_copy(cols_hbm, cols_ref, sems.at[0])
    hid_copy = pltpu.make_async_copy(hid_ref, hid_out, sems.at[1])
    gw_copy = pltpu.make_async_copy(gw_ref, gw_out, sems.at[2])
    copy.start()
    hid_copy.start()
    gw_copy.start()
    out_ref[...] = jnp.zeros_like(out_ref)
    copy.wait()

    def tile_row(t, carry):
        for k in range(TPR):
            out_ref[cols_ref[k, t]] += parts_ref[t, k]
        return carry

    lax.fori_loop(0, TILE_ROWS, tile_row, 0, unroll=2)
    hid_copy.wait()
    gw_copy.wait()


def place_call(cols, parts, hidden, grad_weight):
    return pl.pallas_call(
        place_kernel,
        name="place_tiles",
        out_shape=(
            shape(SRC_TILES, T, T),
            pltpu.HBM((2 * T, 2 * T), F32),
            pltpu.HBM((T, 2 * T), F32),
        ),
        in_specs=[HBM] + [VMEM] * 3,
        out_specs=(VMEM, HBM, HBM),
        scratch_shapes=[pltpu.SMEM((TPR, TILE_ROWS), I32), pltpu.SemaphoreType.DMA((3,))],
        compiler_params=pltpu.CompilerParams(vmem_limit_bytes=4 * MB),
    )(in_hbm(cols), parts, hidden, grad_weight)


def sum_row_kernel(*refs):
    q_ref, ht_ref, inv_ref, gf_ref = refs[:4]
    r = named(("xfar", "xacc", "xnear", "tot", "zin"), refs[4:], ("fsem", "nsem", "zsem"))
    p = Place()
    zh, x = p.zh, p.x
    right_dev, left_dev = p.in_row(zh, rem(x + 1, 4)), p.in_row(zh, rem(x + 3, 4))
    pair_dev = p.in_row(1 - zh, x)
    barrier = pltpu.get_barrier_semaphore()
    for dev in (right_dev, left_dev, pair_dev):
        signal(barrier, dev)
    pl.semaphore_wait(barrier, 3)
    base = ((1 - zh) * 4, zh * 4)

    def block(k, d):
        return base[k] + rem(x + d, 4)

    def far_copy(k, way):
        return link(
            q_ref.at[block(k, 2), way],
            r.xfar.at[k, way],
            r.fsem,
            (k, way),
            left_dev if way else right_dev,
        )

    def near_copy(k, way, h):
        src = r.xacc.at[k, way] if way == h else q_ref.at[block(k, 1 + 2 * way), h]
        return link(
            src, r.xnear.at[k, way, h], r.nsem, (k, way, h), left_dev if way else right_dev
        )

    def pair_copy(h):
        return link(r.tot.at[0, h], r.zin.at[h], r.zsem, h, pair_dev)

    def first(k):
        for way in range(2):
            far_copy(k, way).start()
        for way in range(2):
            near_copy(k, way, 1 - way).start()

    def second(k):
        for way, dev in ((0, left_dev), (1, right_dev)):
            arrival(r.xfar.at[k, way], r.fsem, (k, way), dev)
            r.xacc[k, way] = q_ref[block(k, 1 + 2 * way), way] + r.xfar[k, way]
            near_copy(k, way, way).start()

    def total(k, h):
        for way, dev in ((0, left_dev), (1, right_dev)):
            arrival(r.xnear.at[k, way, h], r.nsem, (k, way, h), dev)
        r.tot[k, h] = q_ref[block(k, 0), h] + (r.xnear[k, 0, h] + r.xnear[k, 1, h])

    first(0)
    second(0)
    first(1)
    for h in range(2):
        total(0, h)
        pair_copy(h).start()
    second(1)
    for h in range(2):
        total(1, h)
    for h in range(2):
        arrival(r.zin.at[h], r.zsem, h, pair_dev)
        back = (r.tot[1, h] + r.zin[h]) + ht_ref[h]
        gf_ref[h * T : (h + 1) * T, :] = jnp.transpose(
            back * jnp.broadcast_to(inv_ref[h : h + 1, :], (T, T))
        )
    for h in range(2):
        pair_copy(h).wait_send()
        for k in range(2):
            far_copy(k, h).wait_send()
            for way in range(2):
                near_copy(k, way, h).wait_send()


def sum_row_call(parts, ht, inv):
    return pl.pallas_call(
        sum_row_kernel,
        name="sum_over_row",
        out_shape=shape(2 * T, T),
        in_specs=[VMEM] * 3,
        out_specs=VMEM,
        scratch_shapes=[
            pltpu.VMEM((2, 2, T, T), F32),
            pltpu.VMEM((2, 2, T, T), F32),
            pltpu.VMEM((2, 2, 2, T, T), F32),
            pltpu.VMEM((2, 2, T, T), F32),
            pltpu.VMEM((2, T, T), F32),
        ]
        + sem_pairs(((2, 2), (2, 2, 2), (2,))),
        compiler_params=pltpu.CompilerParams(
            collective_id=2, has_side_effects=True, vmem_limit_bytes=6 * MB
        ),
    )(parts.reshape(ROWS, 2, T, T), ht, inv)


def shards(features, weight, bias, cot, drop, tile_cols, counts, pos, keep):
    cols = jnp.transpose(tile_cols[0, 0])
    hidden, ht, inv, parts, grad_weight = layer_call(
        cols,
        features,
        jnp.transpose(counts[0, 0]),
        pos[0, 0],
        keep[0, 0],
        weight,
        bias.reshape(1, 2 * T),
        cot,
        drop,
    )
    back, hidden, grad_weight = place_call(cols, parts, hidden, grad_weight)
    grad_features = sum_row_call(back, ht, inv)
    return hidden, grad_features, grad_weight


def solution(mesh):
    nodes = P(("row", "col"), None)
    block = P("row", "col", None, None)
    return jax.shard_map(
        shards,
        mesh=mesh,
        in_specs=(nodes, P(), P(), nodes, nodes, block, block, block, block),
        out_specs=(nodes, nodes, P()),
        check_vma=False,
    )
```

```python
from types import SimpleNamespace

import jax
import jax.numpy as jnp
from jax import lax
from jax.experimental import pallas as pl
from jax.experimental.pallas import tpu as pltpu
from jax.sharding import PartitionSpec as P

MESH = pl.DeviceIdType.MESH
HIGHEST = lax.Precision.HIGHEST
F32, BF16, I32 = jnp.float32, jnp.bfloat16, jnp.int32

T = 128
ROWS, COLS = 8, 32
TILE_ROWS, TPR, EPT = 64, 4, 64
SLOTS = TPR * EPT
SRC_TILES = 16
MB = 1 << 20
VMEM = pl.BlockSpec(memory_space=pltpu.VMEM)
HBM = pl.BlockSpec(memory_space=pltpu.HBM)
NT = (((1,), (1,)), ((), ()))


def in_hbm(array):
    return pltpu.with_memory_space_constraint(array, pltpu.HBM)


def rem(a, n):
    return lax.rem(a, jnp.int32(n))


def div(a, n):
    return lax.div(a, jnp.int32(n))


def shape(*dims, dtype=F32):
    return jax.ShapeDtypeStruct(dims, dtype)


def link_from(src, dst, sems, sent, received, dev):
    return pltpu.make_async_remote_copy(
        src_ref=src,
        dst_ref=dst,
        send_sem=sems.send.at[sent],
        recv_sem=sems.recv.at[received],
        device_id=dev,
        device_id_type=MESH,
    )


def link(src, dst, sems, where, dev):
    return link_from(src, dst, sems, where, where, dev)


def arrival(ref, sems, where, dev):
    link(ref, ref, sems, where, dev).wait_recv()


def signal(barrier, dev):
    pl.semaphore_signal(barrier, inc=1, device_id=dev, device_id_type=MESH)


def named(names, refs, pairs=()):
    out = SimpleNamespace(**dict(zip(names, refs)))
    rest = refs[len(names) :]
    for i, name in enumerate(pairs):
        setattr(out, name, SimpleNamespace(send=rest[2 * i], recv=rest[2 * i + 1]))
    return out


def sem_pairs(dims):
    return [pltpu.SemaphoreType.DMA(d) for d in dims for _ in range(2)]


def each(low, high, body):
    def run(o, carry):
        body(o)
        return carry

    lax.fori_loop(low, high, run, 0)


def slot_codes(counts, pos, keep):
    lane = lax.broadcasted_iota(I32, (TILE_ROWS, SLOTS), 1)
    counts = jnp.transpose(counts)
    limit = jnp.broadcast_to(counts[:, 0:1], (TILE_ROWS, SLOTS))
    for k in range(1, TPR):
        limit = jnp.where(
            lane >= k * EPT, jnp.broadcast_to(counts[:, k : k + 1], (TILE_ROWS, SLOTS)), limit
        )
    live = ((lane & (EPT - 1)) < limit) & (keep == 1)
    return jnp.where(live, pos >> 7, 4 * T)


def split(values, axis):
    high = values.astype(BF16)
    low = (values - high.astype(F32)).astype(BF16)
    return jnp.concatenate([high, low], axis=axis)


def hot_dst(code_row, side):
    return jnp.where(side == jnp.broadcast_to(code_row, (T, SLOTS)), 1.0, 0.0).astype(BF16)


def hot_src(pos_row, side, lane):
    code = (pos_row & (T - 1)) + ((lane >> 6) & 1) * T
    return jnp.where(side == jnp.broadcast_to(code, (2 * T, SLOTS)), 1.0, 0.0).astype(BF16)


def gelu_pair(values):
    half = 0.5 * (1.0 + lax.erf(values * 0.7071067811865476))
    slope = half + values * jnp.exp(-0.5 * values * values) * 0.3989422804014327
    return values * half, slope


def far_first(zl, k):
    near = jnp.where(zl >= 2, 3 - zl, zl)
    inner = jnp.where(k == 0, 3, jnp.where(k == 1, 0, 4 - k))
    plane = jnp.where(near == 0, 3 - k, inner)
    return jnp.where(zl >= 2, 3 - plane, plane)


def chosen(g, values):
    out = jnp.int32(values[0])
    for i in range(1, len(values)):
        out = jnp.where(g == i, values[i], out)
    return out


class Place:
    def __init__(self):
        self.row, self.col = lax.axis_index("row"), lax.axis_index("col")
        self.zh, self.x = div(self.row, 4), rem(self.row, 4)
        self.zl, self.y, self.c = div(self.col, 8), rem(div(self.col, 2), 4), rem(self.col, 2)

    def in_row(self, zh, x):
        return (zh * 4 + x, self.col)

    def in_col(self, zl, y, c):
        return (self.row, (zl * 4 + y) * 2 + c)


def gather_features(p, r, barrier_wait):
    row, col, zh, x = p.row, p.col, p.zh, p.x
    pair = 1 - zh
    right, left = rem(x + 1, 4), rem(x + 3, 4)
    right_dev, left_dev, pair_dev = p.in_row(zh, right), p.in_row(zh, left), p.in_row(pair, x)
    across_dev = p.in_row(zh, rem(x + 2, 4))
    for h in range(2):
        r.xg[row, h] = jnp.transpose(r.x[h * T : (h + 1) * T, :])
    r.code[...] = slot_codes(r.counts[...], r.pos[...], r.keep[...])
    barrier_wait()

    def near_copy(k, zz, way, h):
        slot = r.xg.at[zz * 4 + x, h]
        return link(slot, slot, r.xnear, (k, way, h), left_dev if way else right_dev)

    def near_wait(k, zz, way, h):
        slot = r.xg.at[zz * 4 + (right if way else left), h]
        arrival(slot, r.xnear, (k, way, h), right_dev if way else left_dev)

    def far_copy(h):
        slot = r.xg.at[zh * 4 + (right if h else left), h]
        return link(slot, slot, r.xfar, (0, h), left_dev if h else right_dev)

    def across_copy(h):
        slot = r.xg.at[pair * 4 + x, h]
        return link(slot, slot, r.xfar, (1, h), across_dev)

    def pair_copy(h):
        return link(r.xg.at[row, h], r.xg.at[row, h], r.xpair, h, pair_dev)

    for h in range(2):
        pair_copy(h).start()
    for way, h in ((0, 0), (1, 1), (0, 1), (1, 0)):
        near_copy(0, zh, way, h).start()

    ones = jnp.ones((8, SLOTS), BF16)
    side = lax.broadcasted_iota(I32, (T, SLOTS), 0)
    wide = lax.broadcasted_iota(I32, (2 * T, SLOTS), 0)
    lane = lax.broadcasted_iota(I32, (1, SLOTS), 1)
    sub = lax.broadcasted_iota(I32, (8, T), 0)

    def count(i, carry):
        for u in range(4):
            j = 4 * i + u
            halves = []
            for h in range(2):
                hot = hot_dst(r.code[pl.ds(2 * j + h, 1), :], side)
                halves.append(lax.dot_general(ones, hot, NT, preferred_element_type=F32))
            r.deg[j] = jnp.where(sub == 0, halves[0], jnp.where(sub == 1, halves[1], 0.0))
        return carry

    lax.fori_loop(0, COLS // 4, count, 0)

    def degree_copy(o):
        peer = rem(col + o, COLS)
        return link(r.deg.at[peer], r.degin.at[o], r.dsem, o, (row, peer))

    each(1, COLS, lambda o: degree_copy(o).start())

    def block(i, carry):
        for u in range(4):
            t = 4 * i + u
            dst = hot_dst(r.code[pl.ds(t, 1), :], side)
            src = hot_src(r.pos[pl.ds(t, 1), :], wide, lane)
            for q in range(2):
                part = slice(q * T, (q + 1) * T)
                r.adj[t, :, q * 2 * T : (q + 1) * 2 * T] = lax.dot_general(
                    dst[:, part], src[:, part], NT, preferred_element_type=F32
                ).astype(BF16)
        return carry

    def pass_on(h):
        arrival(r.xg.at[pair * 4 + x, h], r.xpair, h, pair_dev)
        across_copy(h).start()
        near_copy(1, pair, 0, h).start()
        near_copy(1, pair, 1, h).start()

    lax.fori_loop(0, 3, block, 0)
    for h in range(2):
        near_wait(0, zh, h, h)
        far_copy(h).start()
    pass_on(0)

    def collect(o, total):
        arrival(r.degin.at[o], r.dsem, o, (row, rem(col + COLS - o, COLS)))
        return total + r.degin[o]

    total = lax.fori_loop(1, COLS, collect, r.deg[col])
    inv = lax.rsqrt(1.0 + total)
    r.inv[...] = inv
    r.invg[row] = inv

    def inv_copy(o):
        return link(r.inv, r.invg.at[row], r.vsem, o, (rem(row + o, ROWS), col))

    each(1, ROWS, lambda o: inv_copy(o).start())
    pass_on(1)
    lax.fori_loop(3, 16, block, 0)

    def inv_wait(o):
        peer = rem(row + ROWS - o, ROWS)
        arrival(r.invg.at[peer], r.vsem, o, (peer, col))

    each(1, ROWS, inv_wait)
    for h in range(2):
        near_wait(0, zh, 1 - h, h)
        slot = r.xg.at[zh * 4 + rem(x + 2, 4), h]
        arrival(slot, r.xfar, (0, h), right_dev if h else left_dev)
        near_wait(1, pair, 0, h)
        near_wait(1, pair, 1, h)
        arrival(r.xg.at[pair * 4 + rem(x + 2, 4), h], r.xfar, (1, h), across_dev)

    def drain():
        for h in range(2):
            pair_copy(h).wait_send()
            far_copy(h).wait_send()
            across_copy(h).wait_send()
            for k, zz in ((0, zh), (1, pair)):
                for way in range(2):
                    near_copy(k, zz, way, h).wait_send()
        each(1, ROWS, lambda o: inv_copy(o).wait_send())
        each(1, COLS, lambda o: degree_copy(o).wait_send())

    return drain


SUM_ORDER = (
    (0, 0), (1, 0), (2, 0), (3, 0), (0, 1), (0, 2), (0, 3), (1, 1),
    (1, 2), (1, 3), (2, 1), (2, 2), (2, 3), (3, 1), (3, 2), (3, 3),
)
SUM_LAG = 3


def forward_sum(p, r, out_ref):
    row, zl, y, c = p.row, p.zl, p.y, p.c
    core_dev = p.in_col(zl, y, 1 - c)
    right_dev, left_dev = p.in_col(zl, rem(y + 1, 4), c), p.in_col(zl, rem(y + 3, 4), c)
    for u in range(SRC_TILES):
        i, h = u // 2, u % 2
        r.scaled[u] = split(
            r.xg[i, h] * jnp.broadcast_to(r.invg[i, h : h + 1, :], (T, T)), axis=0
        )
    q = r.q

    def tile_row(t):
        panel = jnp.concatenate([r.scaled[r.cols[k, t]] for k in range(TPR)], axis=1)
        both = lax.dot_general(panel, r.adj[t], NT, preferred_element_type=F32)
        return both[:T] + both[T:]

    def core_copy(g):
        return link(r.pbuf.at[g], r.cbuf.at[g], r.fcore, g, core_dev)

    def far_copy(k, way):
        return link(
            q.at[4 * k, way],
            r.yfar.at[k, way],
            r.ffar,
            (k, way),
            left_dev if way else right_dev,
        )

    def near_copy(k, way, h):
        src = r.yacc.at[k, way] if way == h else q.at[4 * k + 1 + way, h]
        return link(
            src, r.ynear.at[k, way, h], r.fnear, (k, way, h), left_dev if way else right_dev
        )

    inner = (zl == 1) | (zl == 2)
    inner_plane = jnp.where(zl <= 1, 1, 2)

    def plane_copy(k, h):
        slot = r.zin.at[zl, h]
        dev = p.in_col(far_first(zl, k), y, c)
        return link_from(r.tot.at[k, h], slot, r.fplane, (k, h), (zl, h), dev)

    def joint_copy(h):
        dev = p.in_col(far_first(zl, 0), y, c)
        return link_from(r.zout.at[h], r.zin.at[zl, h], r.fplane, (0, h), (zl, h), dev)

    def end_copy(h):
        return link(r.tot.at[0, h], r.zmid.at[h], r.fend, h, p.in_col(inner_plane, y, c))

    def finish(k, j):
        g = 4 * k + j
        core_copy(g).wait_recv()
        q[g] = q[g] + r.cbuf[g]

        @pl.when(j == 0)
        def _():
            far_copy(k, 0).start()
            far_copy(k, 1).start()

    def accumulate(k):
        for way, dev in ((0, left_dev), (1, right_dev)):
            arrival(r.yfar.at[k, way], r.ffar, (k, way), dev)
            r.yacc[k, way] = q[4 * k + 1 + way, way] + r.yfar[k, way]
            near_copy(k, way, way).start()
        for way in range(2):
            near_copy(k, way, 1 - way).start()

    def plane_sum(k, h):
        arrival(r.ynear.at[k, 0, h], r.fnear, (k, 0, h), left_dev)
        arrival(r.ynear.at[k, 1, h], r.fnear, (k, 1, h), right_dev)
        return q[4 * k + 3, h] + (r.ynear[k, 0, h] + r.ynear[k, 1, h])

    def place_in(i):
        return chosen(i, [b[0] for b in SUM_ORDER]), chosen(i, [b[1] for b in SUM_ORDER])

    def step(i, carry):
        k, j = place_in(i)
        g = 4 * k + j
        d = chosen(j, (2, 1, 3, 0))
        first = (far_first(zl, k) * 4 + rem(y + d, 4)) * 4
        for h in range(2):
            r.pbuf[g, h] = tile_row(first + 2 * (1 - c) + h)
        for h in range(2):
            q[g, h] = tile_row(first + 2 * c + h)
        core_copy(g).start()
        ready_k, ready_j = place_in(i - SUM_LAG)

        @pl.when(i >= SUM_LAG)
        def _():
            finish(ready_k, ready_j)

        @pl.when((i >= SUM_LAG) & (ready_j == 3))
        def _():
            accumulate(ready_k)

        return carry

    lax.fori_loop(0, 16, step, 0)

    def rest(i):
        k, j = place_in(i)
        finish(k, j)

    each(16 - SUM_LAG, 16, rest)
    accumulate(jnp.int32(3))
    for k in range(3):
        for h in range(2):
            r.tot[k, h] = plane_sum(k, h)
            if k > 0:
                plane_copy(k, h).start()
            else:

                @pl.when(jnp.logical_not(inner))
                def _():
                    end_copy(h).start()

        if k == 1:

            @pl.when(inner)
            def _():
                for h in range(2):
                    arrival(r.zmid.at[h], r.fend, h, core_dev)
                    r.zout[h] = r.tot[0, h] + r.zmid[h]
                    joint_copy(h).start()

    for h in range(2):
        out_ref[h] = plane_sum(3, h)
        for s in range(4):

            @pl.when((zl != s) & (zl + s != 3) | ((zl == 1) & (s == 2)) | ((zl == 2) & (s == 1)))
            def _():
                arrival(r.zin.at[s, h], r.fplane, (s, h), core_dev)
                out_ref[h] = out_ref[h] + r.zin[s, h]

    def drain_plane(k):
        for way in range(2):
            far_copy(k, way).wait_send()
            for h in range(2):
                near_copy(k, way, h).wait_send()
        for j in range(4):
            core_copy(4 * k + j).wait_send()

    def drain():
        each(0, 4, drain_plane)
        for h in range(2):
            for k in (1, 2):
                plane_copy(k, h).wait_send()

            @pl.when(inner)
            def _():
                joint_copy(h).wait_send()

            @pl.when(jnp.logical_not(inner))
            def _():
                end_copy(h).wait_send()

    return drain


def node_update(r, hid_ref, ht_ref):
    weight = r.w[...]
    bias = jnp.broadcast_to(r.b[...], (T, 2 * T))
    total = jnp.zeros((T, 2 * T), F32)
    for h in range(2):
        part = slice(h * T, (h + 1) * T)
        inv_row = jnp.broadcast_to(r.inv[h : h + 1, :], (T, T))
        inv_col = jnp.transpose(inv_row)
        inv_col = jnp.concatenate([inv_col, inv_col], axis=1)
        agg = r.agg[h] + jnp.transpose(r.x[part, :]) * inv_row
        mixed = jnp.dot(
            jnp.transpose(agg), weight, precision=HIGHEST, preferred_element_type=F32
        )
        gelu, slope = gelu_pair(inv_col * mixed + bias)
        drop = r.drop[part, :].astype(F32) / 0.9
        hid_ref[part, :] = gelu * drop
        grad = inv_col * (r.cot[part, :] * drop * slope)
        ht_ref[h] = lax.dot_general(weight, grad, NT, precision=HIGHEST, preferred_element_type=F32)
        total = total + jnp.dot(agg, grad, precision=HIGHEST, preferred_element_type=F32)
    for k in range(2):
        r.gw[k * 16 : (k + 1) * 16] = total[:, k * T : (k + 1) * T].reshape(16, 8, T)


BLOCK_ORDER = (
    (0, 0), (0, 1), (0, 3), (1, 0), (0, 2), (2, 0), (1, 1), (1, 3),
    (3, 0), (1, 2), (2, 1), (2, 3), (2, 2), (3, 1), (3, 3), (3, 2),
)


def spread_gradients(p, r, ht_ref, parts_ref, gwo_ref):
    row, col, zl, y, c = p.row, p.col, p.zl, p.y, p.c
    right, left, across = rem(y + 1, 4), rem(y + 3, 4), rem(y + 2, 4)
    core_dev = p.in_col(zl, y, 1 - c)
    right_dev, left_dev = p.in_col(zl, right, c), p.in_col(zl, left, c)
    up_dev = p.in_col(jnp.minimum(zl + 1, 3), y, c)
    down_dev = p.in_col(jnp.maximum(zl - 1, 0), y, c)
    r.g[zl, y, c] = ht_ref[...]

    def plane(k):
        return far_first(zl, 3 - k)

    def z_copy(z, up, h):
        slot = r.g.at[z, y, c, h]
        return link(slot, slot, r.gchain, (z, 0 if up else 1, h), up_dev if up else down_dev)

    end = (zl == 0) | (zl == 3)

    def end_copy(h):
        slot = r.g.at[zl, y, c, h]
        low = jnp.where(zl == 0, 1, 0)
        return link_from(
            slot, slot, r.gchain, (zl, low, h), (zl, 1 - low, h), p.in_col(3 - zl, y, c)
        )

    def near_copy(k, way, h):
        slot = r.g.at[plane(k), y, c, h]
        return link(slot, slot, r.gnear, (k, way, h), left_dev if way else right_dev)

    def far_copy(k, h):
        slot = r.g.at[plane(k), right if h else left, c, h]
        return link(slot, slot, r.gfar, (k, h), left_dev if h else right_dev)

    def core_copy(k, d):
        slot = r.g.at[plane(k), rem(y + d, 4), c]
        return link(slot, slot, r.gcore, (k, d), core_dev)

    def core_wait(k, d):
        arrival(r.g.at[plane(k), rem(y + d, 4), 1 - c], r.gcore, (k, d), core_dev)

    def near_wait(k, way, h):
        slot = r.g.at[plane(k), right if way else left, c, h]
        arrival(slot, r.gnear, (k, way, h), right_dev if way else left_dev)

    def z_arrive(k):
        z = plane(k)
        below = z < zl
        way = jnp.where(below, 0, 1)
        for h in range(2):
            arrival(r.g.at[z, y, c, h], r.gchain, (z, way, h), core_dev)

            @pl.when((zl - z == 1) & (zl < 3))
            def _():
                z_copy(z, True, h).start()

            @pl.when((z - zl == 1) & (zl > 0))
            def _():
                z_copy(z, False, h).start()

            near_copy(k, h, h).start()
        near_copy(k, 0, 1).start()
        near_copy(k, 1, 0).start()
        core_copy(k, 0).start()

    def y_arrive(k):
        near_wait(k, 0, 0)
        far_copy(k, 0).start()
        near_wait(k, 1, 1)
        far_copy(k, 1).start()
        near_wait(k, 0, 1)
        core_copy(k, 3).start()
        near_wait(k, 1, 0)
        core_copy(k, 1).start()

    def y_far(k):
        for h in range(2):
            arrival(
                r.g.at[plane(k), across, c, h], r.gfar, (k, h), right_dev if h else left_dev
            )
        core_copy(k, 2).start()

    def tile_row(k, d, cc, h):
        z, yy = plane(k), rem(y + d, 4)
        t = ((z * 4 + yy) * 2 + cc) * 2 + h
        adj = r.adj[t]
        back = jnp.dot(
            split(r.g[z, yy, cc, h], axis=1),
            jnp.concatenate([adj, adj], axis=0),
            preferred_element_type=F32,
        )
        for i in range(TPR):
            parts_ref[t, i] = back[:, i * T : (i + 1) * T]

    def use(g):
        return chosen(g, [b[0] for b in BLOCK_ORDER]), chosen(g, [b[1] for b in BLOCK_ORDER])

    zero = jnp.int32(0)
    for h in range(2):

        @pl.when(zl < 3)
        def _():
            z_copy(zl, True, h).start()

        @pl.when(zl > 0)
        def _():
            z_copy(zl, False, h).start()

        @pl.when(end)
        def _():
            end_copy(h).start()

        near_copy(zero, h, h).start()
    near_copy(zero, 0, 1).start()
    near_copy(zero, 1, 0).start()
    core_copy(zero, 0).start()

    def scatter_copy(o):
        peer = rem(col + o, COLS)
        return link(r.gw.at[peer], r.gin.at[o], r.gsem, o, (row, peer))

    def share_copy(o):
        return link(r.mine, r.rin.at[row], r.wsem, o, (rem(row + o, ROWS), col))

    def return_copy(o):
        return link(r.full.at[col], r.full.at[col], r.bsem, o, (row, rem(col + o, COLS)))

    each(1, COLS, lambda o: scatter_copy(o).start())

    def reduce_col():
        def collect(o, total):
            arrival(r.gin.at[o], r.gsem, o, (row, rem(col + COLS - o, COLS)))
            return total + r.gin[o]

        r.mine[...] = lax.fori_loop(1, COLS, collect, r.gw[col])
        r.rin[row] = r.mine[...]
        each(1, ROWS, lambda o: share_copy(o).start())

    def reduce_row():
        def wait(o):
            peer = rem(row + ROWS - o, ROWS)
            arrival(r.rin.at[peer], r.wsem, o, (peer, col))

        each(1, ROWS, wait)
        total = r.rin[0]
        for i in range(1, ROWS):
            total = total + r.rin[i]
        r.full[col] = total
        each(1, COLS, lambda o: return_copy(o).start())

    def events(g):
        for at, body in (
            (4, lambda: (y_far(zero), z_arrive(zero + 2))),
            (6, lambda: y_arrive(zero + 1)),
            (7, reduce_col),
            (8, lambda: z_arrive(zero + 3)),
            (9, lambda: (y_far(zero + 1), y_arrive(zero + 2))),
            (11, reduce_row),
            (12, lambda: (y_far(zero + 2), y_arrive(zero + 3))),
            (15, lambda: y_far(zero + 3)),
        ):

            @pl.when(g == at)
            def _():
                body()

    def step(g, carry):
        events(g)
        k, d = use(g)
        kk, dd = use(g - 2)
        core_wait(kk, dd)
        for h in range(2):
            tile_row(k, d, c, h)
        for h in range(2):
            tile_row(kk, dd, 1 - c, h)
        return carry

    for h in range(2):
        tile_row(zero, zero, c, h)
    z_arrive(zero + 1)
    y_arrive(zero)
    for h in range(2):
        tile_row(zero, zero + 1, c, h)
    lax.fori_loop(2, 16, step, 0)

    def last(g):
        kk, dd = use(g)
        core_wait(kk, dd)
        for h in range(2):
            tile_row(kk, dd, 1 - c, h)

    each(14, 16, last)

    def return_wait(o):
        peer = rem(col + COLS - o, COLS)
        arrival(r.full.at[peer], r.bsem, o, (row, peer))

    each(1, COLS, return_wait)
    for k in range(2):
        gwo_ref[:, k * T : (k + 1) * T] = r.full[k * 16 : (k + 1) * 16].reshape(T, T)

    def drain_plane(k):
        z = plane(k)
        for d in range(4):
            core_copy(k, d).wait_send()
        for h in range(2):
            far_copy(k, h).wait_send()
            near_copy(k, 0, h).wait_send()
            near_copy(k, 1, h).wait_send()

            @pl.when(((z == zl) | (zl - z == 1)) & (zl < 3))
            def _():
                z_copy(z, True, h).wait_send()

            @pl.when(((z == zl) | (z - zl == 1)) & (zl > 0))
            def _():
                z_copy(z, False, h).wait_send()

            @pl.when((z == zl) & end)
            def _():
                end_copy(h).wait_send()

    def drain():
        each(0, 4, drain_plane)

        def sent(o):
            scatter_copy(o).wait_send()
            return_copy(o).wait_send()

        each(1, COLS, sent)
        each(1, ROWS, lambda o: share_copy(o).wait_send())

    return drain


SOURCES = ("cols", "x", "counts", "pos", "keep", "w", "b", "cot", "drop")
RESULTS = ("hid", "ht", "invo", "parts", "gwo")
BUFFERS = {
    "cols": ((TPR, TILE_ROWS), I32),
    "x": ((2 * T, T), F32),
    "counts": ((TPR, TILE_ROWS), I32),
    "pos": ((TILE_ROWS, SLOTS), I32),
    "keep": ((TILE_ROWS, SLOTS), I32),
    "w": ((T, 2 * T), F32),
    "b": ((1, 2 * T), F32),
    "cot": ((2 * T, 2 * T), F32),
    "drop": ((2 * T, 2 * T), I32),
    "code": ((TILE_ROWS, SLOTS), I32),
    "xg": ((ROWS, 2, T, T), F32),
    "deg": ((COLS, 8, T), F32),
    "degin": ((COLS, 8, T), F32),
    "inv": ((8, T), F32),
    "invg": ((ROWS, 8, T), F32),
    "adj": ((TILE_ROWS, T, TPR * T), BF16),
    "scaled": ((SRC_TILES, 2 * T, T), BF16),
    "pbuf": ((16, 2, T, T), F32),
    "cbuf": ((16, 2, T, T), F32),
    "q": ((16, 2, T, T), F32),
    "yfar": ((4, 2, T, T), F32),
    "yacc": ((4, 2, T, T), F32),
    "ynear": ((4, 2, 2, T, T), F32),
    "tot": ((4, 2, T, T), F32),
    "zin": ((4, 2, T, T), F32),
    "zmid": ((2, T, T), F32),
    "zout": ((2, T, T), F32),
    "agg": ((2, T, T), F32),
    "g": ((4, 4, 2, 2, T, T), F32),
    "gw": ((COLS, 8, T), F32),
    "gin": ((COLS, 8, T), F32),
    "rin": ((ROWS, 8, T), F32),
    "mine": ((8, T), F32),
    "full": ((COLS, 8, T), F32),
}
LINKS = {
    "xpair": (2,),
    "xnear": (2, 2, 2),
    "xfar": (2, 2),
    "dsem": (COLS,),
    "vsem": (ROWS,),
    "fcore": (16,),
    "ffar": (4, 2),
    "fnear": (4, 2, 2),
    "fplane": (4, 2),
    "fend": (2,),
    "gchain": (4, 2, 2),
    "gnear": (4, 2, 2),
    "gfar": (4, 2),
    "gcore": (4, 4),
    "gsem": (COLS,),
    "wsem": (ROWS,),
    "bsem": (COLS,),
}
LOADS = SOURCES


def layer_kernel(*refs):
    inputs = named(SOURCES, refs)
    outputs = named(RESULTS, refs[len(SOURCES) :])
    r = named(tuple(BUFFERS), refs[len(SOURCES) + len(RESULTS) : -1], tuple(LINKS))
    p = Place()
    loads = {
        name: pltpu.make_async_copy(getattr(inputs, name), getattr(r, name), refs[-1].at[i])
        for i, name in enumerate(LOADS)
    }
    for copy in loads.values():
        copy.start()
    barrier = pltpu.get_barrier_semaphore()
    each(1, COLS, lambda o: signal(barrier, (p.row, rem(p.col + o, COLS))))
    each(1, ROWS, lambda o: signal(barrier, (rem(p.row + o, ROWS), p.col)))
    for copy in loads.values():
        copy.wait()
    drain_gather = gather_features(p, r, lambda: pl.semaphore_wait(barrier, COLS + ROWS - 2))
    drain_forward = forward_sum(p, r, r.agg)
    node_update(r, outputs.hid, outputs.ht)
    drain_spread = spread_gradients(p, r, outputs.ht, outputs.parts, outputs.gwo)
    outputs.invo[...] = r.inv[...]
    drain_gather()
    drain_forward()
    drain_spread()


def layer_call(*args):
    return pl.pallas_call(
        layer_kernel,
        name="layer",
        out_shape=(
            shape(2 * T, 2 * T),
            shape(2, T, T),
            shape(8, T),
            shape(TILE_ROWS, TPR, T, T),
            shape(T, 2 * T),
        ),
        in_specs=[HBM] * 9,
        out_specs=(VMEM,) * 5,
        scratch_shapes=[
            (pltpu.SMEM if name == "cols" else pltpu.VMEM)(dims, dtype)
            for name, (dims, dtype) in BUFFERS.items()
        ]
        + sem_pairs(LINKS.values())
        + [pltpu.SemaphoreType.DMA((len(LOADS),))],
        compiler_params=pltpu.CompilerParams(
            collective_id=1, has_side_effects=True, vmem_limit_bytes=32 * MB
        ),
    )(*[in_hbm(arg) for arg in args])


def place_kernel(
    cols_hbm, parts_ref, hid_ref, gw_ref, out_ref, hid_out, gw_out, cols_ref, sems
):
    copy = pltpu.make_async_copy(cols_hbm, cols_ref, sems.at[0])
    hid_copy = pltpu.make_async_copy(hid_ref, hid_out, sems.at[1])
    gw_copy = pltpu.make_async_copy(gw_ref, gw_out, sems.at[2])
    copy.start()
    hid_copy.start()
    gw_copy.start()
    out_ref[...] = jnp.zeros_like(out_ref)
    copy.wait()

    def tile_row(t, carry):
        for k in range(TPR):
            out_ref[cols_ref[k, t]] += parts_ref[t, k]
        return carry

    lax.fori_loop(0, TILE_ROWS, tile_row, 0, unroll=2)
    hid_copy.wait()
    gw_copy.wait()


def place_call(cols, parts, hidden, grad_weight):
    return pl.pallas_call(
        place_kernel,
        name="place_tiles",
        out_shape=(
            shape(SRC_TILES, T, T),
            pltpu.HBM((2 * T, 2 * T), F32),
            pltpu.HBM((T, 2 * T), F32),
        ),
        in_specs=[HBM] + [VMEM] * 3,
        out_specs=(VMEM, HBM, HBM),
        scratch_shapes=[pltpu.SMEM((TPR, TILE_ROWS), I32), pltpu.SemaphoreType.DMA((3,))],
        compiler_params=pltpu.CompilerParams(vmem_limit_bytes=4 * MB),
    )(in_hbm(cols), parts, hidden, grad_weight)


def sum_row_kernel(*refs):
    q_ref, ht_ref, inv_ref, gf_ref = refs[:4]
    r = named(("xfar", "xacc", "xnear", "tot", "zin"), refs[4:], ("fsem", "nsem", "zsem"))
    p = Place()
    zh, x = p.zh, p.x
    right_dev, left_dev = p.in_row(zh, rem(x + 1, 4)), p.in_row(zh, rem(x + 3, 4))
    pair_dev = p.in_row(1 - zh, x)
    barrier = pltpu.get_barrier_semaphore()
    for dev in (right_dev, left_dev, pair_dev):
        signal(barrier, dev)
    pl.semaphore_wait(barrier, 3)
    base = ((1 - zh) * 4, zh * 4)

    def block(k, d):
        return base[k] + rem(x + d, 4)

    def far_copy(k, way):
        return link(
            q_ref.at[block(k, 2), way],
            r.xfar.at[k, way],
            r.fsem,
            (k, way),
            left_dev if way else right_dev,
        )

    def near_copy(k, way, h):
        src = r.xacc.at[k, way] if way == h else q_ref.at[block(k, 1 + 2 * way), h]
        return link(
            src, r.xnear.at[k, way, h], r.nsem, (k, way, h), left_dev if way else right_dev
        )

    def pair_copy(h):
        return link(r.tot.at[0, h], r.zin.at[h], r.zsem, h, pair_dev)

    def first(k):
        for way in range(2):
            far_copy(k, way).start()
        for way in range(2):
            near_copy(k, way, 1 - way).start()

    def second(k):
        for way, dev in ((0, left_dev), (1, right_dev)):
            arrival(r.xfar.at[k, way], r.fsem, (k, way), dev)
            r.xacc[k, way] = q_ref[block(k, 1 + 2 * way), way] + r.xfar[k, way]
            near_copy(k, way, way).start()

    def total(k, h):
        for way, dev in ((0, left_dev), (1, right_dev)):
            arrival(r.xnear.at[k, way, h], r.nsem, (k, way, h), dev)
        r.tot[k, h] = q_ref[block(k, 0), h] + (r.xnear[k, 0, h] + r.xnear[k, 1, h])

    first(0)
    second(0)
    first(1)
    for h in range(2):
        total(0, h)
        pair_copy(h).start()
    second(1)
    for h in range(2):
        total(1, h)
    for h in range(2):
        arrival(r.zin.at[h], r.zsem, h, pair_dev)
        back = (r.tot[1, h] + r.zin[h]) + ht_ref[h]
        gf_ref[h * T : (h + 1) * T, :] = jnp.transpose(
            back * jnp.broadcast_to(inv_ref[h : h + 1, :], (T, T))
        )
    for h in range(2):
        pair_copy(h).wait_send()
        for k in range(2):
            far_copy(k, h).wait_send()
            for way in range(2):
                near_copy(k, way, h).wait_send()


def sum_row_call(parts, ht, inv):
    return pl.pallas_call(
        sum_row_kernel,
        name="sum_over_row",
        out_shape=shape(2 * T, T),
        in_specs=[VMEM] * 3,
        out_specs=VMEM,
        scratch_shapes=[
            pltpu.VMEM((2, 2, T, T), F32),
            pltpu.VMEM((2, 2, T, T), F32),
            pltpu.VMEM((2, 2, 2, T, T), F32),
            pltpu.VMEM((2, 2, T, T), F32),
            pltpu.VMEM((2, T, T), F32),
        ]
        + sem_pairs(((2, 2), (2, 2, 2), (2,))),
        compiler_params=pltpu.CompilerParams(
            collective_id=2, has_side_effects=True, vmem_limit_bytes=6 * MB
        ),
    )(parts.reshape(ROWS, 2, T, T), ht, inv)


def shards(features, weight, bias, cot, drop, tile_cols, counts, pos, keep):
    cols = jnp.transpose(tile_cols[0, 0])
    hidden, ht, inv, parts, grad_weight = layer_call(
        cols,
        features,
        jnp.transpose(counts[0, 0]),
        pos[0, 0],
        keep[0, 0],
        weight,
        bias.reshape(1, 2 * T),
        cot,
        drop,
    )
    back, hidden, grad_weight = place_call(cols, parts, hidden, grad_weight)
    grad_features = sum_row_call(back, ht, inv)
    return hidden, grad_features, grad_weight


def solution(mesh):
    nodes = P(("row", "col"), None)
    block = P("row", "col", None, None)
    return jax.shard_map(
        shards,
        mesh=mesh,
        in_specs=(nodes, P(), P(), nodes, nodes, block, block, block, block),
        out_specs=(nodes, nodes, P()),
        check_vma=False,
    )
```

```python
from types import SimpleNamespace

import jax
import jax.numpy as jnp
from jax import lax
from jax.experimental import pallas as pl
from jax.experimental.pallas import tpu as pltpu
from jax.sharding import PartitionSpec as P

MESH = pl.DeviceIdType.MESH
HIGHEST = lax.Precision.HIGHEST
F32, BF16, I32 = jnp.float32, jnp.bfloat16, jnp.int32

T = 128
ROWS, COLS = 8, 32
TILE_ROWS, TPR, EPT = 64, 4, 64
SLOTS = TPR * EPT
SRC_TILES = 16
MB = 1 << 20
VMEM = pl.BlockSpec(memory_space=pltpu.VMEM)
HBM = pl.BlockSpec(memory_space=pltpu.HBM)
NT = (((1,), (1,)), ((), ()))


def in_hbm(array):
    return pltpu.with_memory_space_constraint(array, pltpu.HBM)


def rem(a, n):
    return lax.rem(a, jnp.int32(n))


def div(a, n):
    return lax.div(a, jnp.int32(n))


def shape(*dims, dtype=F32):
    return jax.ShapeDtypeStruct(dims, dtype)


def link_from(src, dst, sems, sent, received, dev):
    return pltpu.make_async_remote_copy(
        src_ref=src,
        dst_ref=dst,
        send_sem=sems.send.at[sent],
        recv_sem=sems.recv.at[received],
        device_id=dev,
        device_id_type=MESH,
    )


def link(src, dst, sems, where, dev):
    return link_from(src, dst, sems, where, where, dev)


def arrival(ref, sems, where, dev):
    link(ref, ref, sems, where, dev).wait_recv()


def signal(barrier, dev):
    pl.semaphore_signal(barrier, inc=1, device_id=dev, device_id_type=MESH)


def named(names, refs, pairs=()):
    out = SimpleNamespace(**dict(zip(names, refs)))
    rest = refs[len(names) :]
    for i, name in enumerate(pairs):
        setattr(out, name, SimpleNamespace(send=rest[2 * i], recv=rest[2 * i + 1]))
    return out


def sem_pairs(dims):
    return [pltpu.SemaphoreType.DMA(d) for d in dims for _ in range(2)]


def each(low, high, body):
    def run(o, carry):
        body(o)
        return carry

    lax.fori_loop(low, high, run, 0)


def slot_codes(counts, pos, keep):
    lane = lax.broadcasted_iota(I32, (TILE_ROWS, SLOTS), 1)
    counts = jnp.transpose(counts)
    limit = jnp.broadcast_to(counts[:, 0:1], (TILE_ROWS, SLOTS))
    for k in range(1, TPR):
        limit = jnp.where(
            lane >= k * EPT, jnp.broadcast_to(counts[:, k : k + 1], (TILE_ROWS, SLOTS)), limit
        )
    live = ((lane & (EPT - 1)) < limit) & (keep == 1)
    return jnp.where(live, pos >> 7, 4 * T)


def split(values, axis):
    high = values.astype(BF16)
    low = (values - high.astype(F32)).astype(BF16)
    return jnp.concatenate([high, low], axis=axis)


def hot_dst(code_row, side):
    return jnp.where(side == jnp.broadcast_to(code_row, (T, SLOTS)), 1.0, 0.0).astype(BF16)


def hot_src(pos_row, side, lane):
    code = (pos_row & (T - 1)) + ((lane >> 6) & 1) * T
    return jnp.where(side == jnp.broadcast_to(code, (2 * T, SLOTS)), 1.0, 0.0).astype(BF16)


def gelu_pair(values):
    half = 0.5 * (1.0 + lax.erf(values * 0.7071067811865476))
    slope = half + values * jnp.exp(-0.5 * values * values) * 0.3989422804014327
    return values * half, slope


def far_first(zl, k):
    near = jnp.where(zl >= 2, 3 - zl, zl)
    inner = jnp.where(k == 0, 3, jnp.where(k == 1, 0, 4 - k))
    plane = jnp.where(near == 0, 3 - k, inner)
    return jnp.where(zl >= 2, 3 - plane, plane)


def chosen(g, values):
    out = jnp.int32(values[0])
    for i in range(1, len(values)):
        out = jnp.where(g == i, values[i], out)
    return out


class Place:
    def __init__(self):
        self.row, self.col = lax.axis_index("row"), lax.axis_index("col")
        self.zh, self.x = div(self.row, 4), rem(self.row, 4)
        self.zl, self.y, self.c = div(self.col, 8), rem(div(self.col, 2), 4), rem(self.col, 2)

    def in_row(self, zh, x):
        return (zh * 4 + x, self.col)

    def in_col(self, zl, y, c):
        return (self.row, (zl * 4 + y) * 2 + c)


def gather_features(p, r, barrier_wait):
    row, col, zh, x = p.row, p.col, p.zh, p.x
    pair = 1 - zh
    right, left = rem(x + 1, 4), rem(x + 3, 4)
    right_dev, left_dev, pair_dev = p.in_row(zh, right), p.in_row(zh, left), p.in_row(pair, x)
    across_dev = p.in_row(zh, rem(x + 2, 4))
    for h in range(2):
        r.xg[row, h] = jnp.transpose(r.x[h * T : (h + 1) * T, :])
    r.code[...] = slot_codes(r.counts[...], r.pos[...], r.keep[...])
    def near_copy(k, zz, way, h):
        slot = r.xg.at[zz * 4 + x, h]
        return link(slot, slot, r.xnear, (k, way, h), left_dev if way else right_dev)

    def near_wait(k, zz, way, h):
        slot = r.xg.at[zz * 4 + (right if way else left), h]
        arrival(slot, r.xnear, (k, way, h), right_dev if way else left_dev)

    def far_copy(h):
        slot = r.xg.at[zh * 4 + (right if h else left), h]
        return link(slot, slot, r.xfar, (0, h), left_dev if h else right_dev)

    def across_copy(h):
        slot = r.xg.at[pair * 4 + x, h]
        return link(slot, slot, r.xfar, (1, h), across_dev)

    def pair_copy(h):
        return link(r.xg.at[row, h], r.xg.at[row, h], r.xpair, h, pair_dev)

    ones = jnp.ones((8, SLOTS), BF16)
    side = lax.broadcasted_iota(I32, (T, SLOTS), 0)
    wide = lax.broadcasted_iota(I32, (2 * T, SLOTS), 0)
    lane = lax.broadcasted_iota(I32, (1, SLOTS), 1)
    sub = lax.broadcasted_iota(I32, (8, T), 0)

    zl, member = p.zl, rem(col, 8)

    def count(m, carry):
        tile = jnp.zeros((8, T), F32)
        for i in range(8):
            t = 2 * ((i // 2) * 8 + m) + i % 2
            hot = hot_dst(r.code[pl.ds(t, 1), :], side)
            row_sums = lax.dot_general(ones, hot, NT, preferred_element_type=F32)
            tile = jnp.where(sub == i, row_sums, tile)
        r.deg[m] = tile
        return carry

    lax.fori_loop(0, 8, count, 0)
    barrier_wait()
    for h in range(2):
        pair_copy(h).start()
    for way, h in ((0, 0), (1, 1), (0, 1), (1, 0)):
        near_copy(0, zh, way, h).start()


    def member_copy(o):
        peer = rem(member + o, 8)
        return link(r.deg.at[peer], r.degin.at[o], r.dsem, o, (row, zl * 8 + peer))

    def member_wait(o):
        peer = rem(member + 8 - o, 8)
        arrival(r.degin.at[o], r.dsem, o, (row, zl * 8 + peer))

    def plane_copy(o):
        dev = (row, rem(zl + o, 4) * 8 + member)
        return link(r.degsum, r.degz.at[o], r.esem, o, dev)

    def plane_wait(o):
        arrival(r.degz.at[o], r.esem, o, (row, rem(zl + 4 - o, 4) * 8 + member))

    for o in range(1, 8):
        member_copy(o).start()

    def block(i, carry):
        for u in range(4):
            t = 4 * i + u
            dst = hot_dst(r.code[pl.ds(t, 1), :], side)
            src = hot_src(r.pos[pl.ds(t, 1), :], wide, lane)
            for q in range(2):
                part = slice(q * T, (q + 1) * T)
                r.adj[t, :, q * 2 * T : (q + 1) * 2 * T] = lax.dot_general(
                    dst[:, part], src[:, part], NT, preferred_element_type=F32
                ).astype(BF16)
        return carry

    def pass_on(h):
        arrival(r.xg.at[pair * 4 + x, h], r.xpair, h, pair_dev)
        across_copy(h).start()
        near_copy(1, pair, 0, h).start()
        near_copy(1, pair, 1, h).start()

    lax.fori_loop(0, 3, block, 0)
    total = r.deg[member]
    for o in range(1, 8):
        member_wait(o)
        total = total + r.degin[o]
    r.degsum[...] = total
    for o in range(1, 4):
        plane_copy(o).start()
    for h in range(2):
        near_wait(0, zh, h, h)
        far_copy(h).start()
    pass_on(0)
    mine = pl.ds(2 * zl, 2)
    total = r.degsum[mine, :]
    for o in range(1, 4):
        plane_wait(o)
        total = total + r.degz[o, mine, :]
    r.inv[...] = jnp.ones((8, T), F32)
    r.inv[0:2, :] = lax.rsqrt(1.0 + total)
    r.invg[row] = r.inv[...]

    def inv_copy(o):
        return link(r.inv, r.invg.at[row], r.vsem, o, (rem(row + o, ROWS), col))

    each(1, ROWS, lambda o: inv_copy(o).start())
    pass_on(1)
    lax.fori_loop(3, 16, block, 0)

    def inv_wait(o):
        peer = rem(row + ROWS - o, ROWS)
        arrival(r.invg.at[peer], r.vsem, o, (peer, col))

    each(1, ROWS, inv_wait)
    for h in range(2):
        near_wait(0, zh, 1 - h, h)
        slot = r.xg.at[zh * 4 + rem(x + 2, 4), h]
        arrival(slot, r.xfar, (0, h), right_dev if h else left_dev)
        near_wait(1, pair, 0, h)
        near_wait(1, pair, 1, h)
        arrival(r.xg.at[pair * 4 + rem(x + 2, 4), h], r.xfar, (1, h), across_dev)

    def drain():
        for h in range(2):
            pair_copy(h).wait_send()
            far_copy(h).wait_send()
            across_copy(h).wait_send()
            for k, zz in ((0, zh), (1, pair)):
                for way in range(2):
                    near_copy(k, zz, way, h).wait_send()
        each(1, ROWS, lambda o: inv_copy(o).wait_send())
        for o in range(1, 8):
            member_copy(o).wait_send()
        for o in range(1, 4):
            plane_copy(o).wait_send()

    return drain


SUM_ORDER = (
    (0, 0), (1, 0), (2, 0), (3, 0), (0, 1), (0, 2), (0, 3), (1, 1),
    (1, 2), (1, 3), (2, 1), (2, 2), (2, 3), (3, 1), (3, 2), (3, 3),
)
SUM_LAG = 3


def forward_sum(p, r, out_ref):
    row, zl, y, c = p.row, p.zl, p.y, p.c
    core_dev = p.in_col(zl, y, 1 - c)
    right_dev, left_dev = p.in_col(zl, rem(y + 1, 4), c), p.in_col(zl, rem(y + 3, 4), c)
    for u in range(SRC_TILES):
        i, h = u // 2, u % 2
        r.scaled[u] = split(
            r.xg[i, h] * jnp.broadcast_to(r.invg[i, h : h + 1, :], (T, T)), axis=0
        )
    q = r.q

    def tile_row(t):
        panel = jnp.concatenate([r.scaled[r.cols[k, t]] for k in range(TPR)], axis=1)
        both = lax.dot_general(panel, r.adj[t], NT, preferred_element_type=F32)
        return both[:T] + both[T:]

    def core_copy(g):
        return link(r.pbuf.at[g], r.cbuf.at[g], r.fcore, g, core_dev)

    def far_copy(k, way):
        return link(
            q.at[4 * k, way],
            r.yfar.at[k, way],
            r.ffar,
            (k, way),
            left_dev if way else right_dev,
        )

    def near_copy(k, way, h):
        src = r.yacc.at[k, way] if way == h else q.at[4 * k + 1 + way, h]
        return link(
            src, r.ynear.at[k, way, h], r.fnear, (k, way, h), left_dev if way else right_dev
        )

    inner = (zl == 1) | (zl == 2)
    inner_plane = jnp.where(zl <= 1, 1, 2)

    def plane_copy(k, h):
        slot = r.zin.at[zl, h]
        dev = p.in_col(far_first(zl, k), y, c)
        return link_from(r.tot.at[k, h], slot, r.fplane, (k, h), (zl, h), dev)

    def joint_copy(h):
        dev = p.in_col(far_first(zl, 0), y, c)
        return link_from(r.zout.at[h], r.zin.at[zl, h], r.fplane, (0, h), (zl, h), dev)

    def end_copy(h):
        return link(r.tot.at[0, h], r.zmid.at[h], r.fend, h, p.in_col(inner_plane, y, c))

    def finish(k, j):
        g = 4 * k + j
        core_copy(g).wait_recv()
        q[g] = q[g] + r.cbuf[g]

        @pl.when(j == 0)
        def _():
            far_copy(k, 0).start()
            far_copy(k, 1).start()

    def accumulate(k):
        for way, dev in ((0, left_dev), (1, right_dev)):
            arrival(r.yfar.at[k, way], r.ffar, (k, way), dev)
            r.yacc[k, way] = q[4 * k + 1 + way, way] + r.yfar[k, way]
            near_copy(k, way, way).start()
        for way in range(2):
            near_copy(k, way, 1 - way).start()

    def plane_sum(k, h):
        arrival(r.ynear.at[k, 0, h], r.fnear, (k, 0, h), left_dev)
        arrival(r.ynear.at[k, 1, h], r.fnear, (k, 1, h), right_dev)
        return q[4 * k + 3, h] + (r.ynear[k, 0, h] + r.ynear[k, 1, h])

    def place_in(i):
        return chosen(i, [b[0] for b in SUM_ORDER]), chosen(i, [b[1] for b in SUM_ORDER])

    def step(i, carry):
        k, j = place_in(i)
        g = 4 * k + j
        d = chosen(j, (2, 1, 3, 0))
        first = (far_first(zl, k) * 4 + rem(y + d, 4)) * 4
        for h in range(2):
            r.pbuf[g, h] = tile_row(first + 2 * (1 - c) + h)
        for h in range(2):
            q[g, h] = tile_row(first + 2 * c + h)
        core_copy(g).start()
        ready_k, ready_j = place_in(i - SUM_LAG)

        @pl.when(i >= SUM_LAG)
        def _():
            finish(ready_k, ready_j)

        @pl.when((i >= SUM_LAG) & (ready_j == 3))
        def _():
            accumulate(ready_k)

        return carry

    lax.fori_loop(0, 16, step, 0)

    def rest(i):
        k, j = place_in(i)
        finish(k, j)

    each(16 - SUM_LAG, 16, rest)
    accumulate(jnp.int32(3))
    for k in range(3):
        for h in range(2):
            r.tot[k, h] = plane_sum(k, h)
            if k > 0:
                plane_copy(k, h).start()
            else:

                @pl.when(jnp.logical_not(inner))
                def _():
                    end_copy(h).start()

        if k == 1:

            @pl.when(inner)
            def _():
                for h in range(2):
                    arrival(r.zmid.at[h], r.fend, h, core_dev)
                    r.zout[h] = r.tot[0, h] + r.zmid[h]
                    joint_copy(h).start()

    for h in range(2):
        out_ref[h] = plane_sum(3, h)
        for s in range(4):

            @pl.when((zl != s) & (zl + s != 3) | ((zl == 1) & (s == 2)) | ((zl == 2) & (s == 1)))
            def _():
                arrival(r.zin.at[s, h], r.fplane, (s, h), core_dev)
                out_ref[h] = out_ref[h] + r.zin[s, h]

    def drain_plane(k):
        for way in range(2):
            far_copy(k, way).wait_send()
            for h in range(2):
                near_copy(k, way, h).wait_send()
        for j in range(4):
            core_copy(4 * k + j).wait_send()

    def drain():
        each(0, 4, drain_plane)
        for h in range(2):
            for k in (1, 2):
                plane_copy(k, h).wait_send()

            @pl.when(inner)
            def _():
                joint_copy(h).wait_send()

            @pl.when(jnp.logical_not(inner))
            def _():
                end_copy(h).wait_send()

    return drain


def node_update(r, hid_ref, ht_ref):
    weight = r.w[...]
    bias = jnp.broadcast_to(r.b[...], (T, 2 * T))
    total = jnp.zeros((T, 2 * T), F32)
    for h in range(2):
        part = slice(h * T, (h + 1) * T)
        inv_row = jnp.broadcast_to(r.inv[h : h + 1, :], (T, T))
        inv_col = jnp.transpose(inv_row)
        inv_col = jnp.concatenate([inv_col, inv_col], axis=1)
        agg = r.agg[h] + jnp.transpose(r.x[part, :]) * inv_row
        mixed = jnp.dot(
            jnp.transpose(agg), weight, precision=HIGHEST, preferred_element_type=F32
        )
        gelu, slope = gelu_pair(inv_col * mixed + bias)
        drop = r.drop[part, :].astype(F32) / 0.9
        hid_ref[part, :] = gelu * drop
        grad = inv_col * (r.cot[part, :] * drop * slope)
        ht_ref[h] = lax.dot_general(weight, grad, NT, precision=HIGHEST, preferred_element_type=F32)
        total = total + jnp.dot(agg, grad, precision=HIGHEST, preferred_element_type=F32)
    for k in range(2):
        r.gw[k * 4 : (k + 1) * 4] = total[:, k * T : (k + 1) * T].reshape(4, 4, 8, T)


BLOCK_ORDER = (
    (0, 0), (0, 1), (0, 3), (1, 0), (0, 2), (2, 0), (1, 1), (1, 3),
    (3, 0), (1, 2), (2, 1), (2, 3), (2, 2), (3, 1), (3, 3), (3, 2),
)


def spread_gradients(p, r, ht_ref, parts_ref, gwo_ref):
    row, col, zl, y, c = p.row, p.col, p.zl, p.y, p.c
    right, left, across = rem(y + 1, 4), rem(y + 3, 4), rem(y + 2, 4)
    core_dev = p.in_col(zl, y, 1 - c)
    right_dev, left_dev = p.in_col(zl, right, c), p.in_col(zl, left, c)
    up_dev = p.in_col(jnp.minimum(zl + 1, 3), y, c)
    down_dev = p.in_col(jnp.maximum(zl - 1, 0), y, c)
    r.g[zl, y, c] = ht_ref[...]

    def plane(k):
        return far_first(zl, 3 - k)

    def z_copy(z, up, h):
        slot = r.g.at[z, y, c, h]
        return link(slot, slot, r.gchain, (z, 0 if up else 1, h), up_dev if up else down_dev)

    end = (zl == 0) | (zl == 3)

    def end_copy(h):
        slot = r.g.at[zl, y, c, h]
        low = jnp.where(zl == 0, 1, 0)
        return link_from(
            slot, slot, r.gchain, (zl, low, h), (zl, 1 - low, h), p.in_col(3 - zl, y, c)
        )

    def near_copy(k, way, h):
        slot = r.g.at[plane(k), y, c, h]
        return link(slot, slot, r.gnear, (k, way, h), left_dev if way else right_dev)

    def far_copy(k, h):
        slot = r.g.at[plane(k), right if h else left, c, h]
        return link(slot, slot, r.gfar, (k, h), left_dev if h else right_dev)

    def core_copy(k, d):
        slot = r.g.at[plane(k), rem(y + d, 4), c]
        return link(slot, slot, r.gcore, (k, d), core_dev)

    def core_wait(k, d):
        arrival(r.g.at[plane(k), rem(y + d, 4), 1 - c], r.gcore, (k, d), core_dev)

    def near_wait(k, way, h):
        slot = r.g.at[plane(k), right if way else left, c, h]
        arrival(slot, r.gnear, (k, way, h), right_dev if way else left_dev)

    def z_arrive(k):
        z = plane(k)
        below = z < zl
        way = jnp.where(below, 0, 1)
        for h in range(2):
            arrival(r.g.at[z, y, c, h], r.gchain, (z, way, h), core_dev)

            @pl.when((zl - z == 1) & (zl < 3))
            def _():
                z_copy(z, True, h).start()

            @pl.when((z - zl == 1) & (zl > 0))
            def _():
                z_copy(z, False, h).start()

            near_copy(k, h, h).start()
        near_copy(k, 0, 1).start()
        near_copy(k, 1, 0).start()
        core_copy(k, 0).start()

    def y_arrive(k):
        near_wait(k, 0, 0)
        far_copy(k, 0).start()
        near_wait(k, 1, 1)
        far_copy(k, 1).start()
        near_wait(k, 0, 1)
        core_copy(k, 3).start()
        near_wait(k, 1, 0)
        core_copy(k, 1).start()

    def y_far(k):
        for h in range(2):
            arrival(
                r.g.at[plane(k), across, c, h], r.gfar, (k, h), right_dev if h else left_dev
            )
        core_copy(k, 2).start()

    def tile_row(k, d, cc, h):
        z, yy = plane(k), rem(y + d, 4)
        t = ((z * 4 + yy) * 2 + cc) * 2 + h
        adj = r.adj[t]
        back = jnp.dot(
            split(r.g[z, yy, cc, h], axis=1),
            jnp.concatenate([adj, adj], axis=0),
            preferred_element_type=F32,
        )
        for i in range(TPR):
            parts_ref[t, i] = back[:, i * T : (i + 1) * T]

    def use(g):
        return chosen(g, [b[0] for b in BLOCK_ORDER]), chosen(g, [b[1] for b in BLOCK_ORDER])

    zero = jnp.int32(0)
    for h in range(2):

        @pl.when(zl < 3)
        def _():
            z_copy(zl, True, h).start()

        @pl.when(zl > 0)
        def _():
            z_copy(zl, False, h).start()

        @pl.when(end)
        def _():
            end_copy(h).start()

        near_copy(zero, h, h).start()
    near_copy(zero, 0, 1).start()
    near_copy(zero, 1, 0).start()
    core_copy(zero, 0).start()

    member = rem(col, 8)

    def member_dev(o):
        return (row, zl * 8 + rem(member + o, 8))

    def plane_dev(o):
        return (row, rem(zl + o, 4) * 8 + member)

    def scatter_copy(o):
        return link(r.gw.at[rem(member + o, 8)], r.gin.at[o], r.gsem, o, member_dev(o))

    def reduce_copy(o):
        return link(r.gsum.at[rem(zl + o, 4)], r.gz.at[o], r.hsem, o, plane_dev(o))

    def share_copy(o):
        return link(r.mine, r.rin.at[row], r.wsem, o, (rem(row + o, ROWS), col))

    def plane_return(o):
        slot = r.full.at[member, zl]
        return link(slot, slot, r.isem, o, plane_dev(o))

    def member_return(o):
        slot = r.full.at[member]
        return link(slot, slot, r.bsem, o, member_dev(o))

    for o in range(1, 8):
        scatter_copy(o).start()

    def reduce_members():
        total = r.gw[member]
        for o in range(1, 8):
            arrival(r.gin.at[o], r.gsem, o, member_dev(8 - o))
            total = total + r.gin[o]
        r.gsum[...] = total
        for o in range(1, 4):
            reduce_copy(o).start()

    def reduce_planes():
        total = r.gsum[zl]
        for o in range(1, 4):
            arrival(r.gz.at[o], r.hsem, o, plane_dev(4 - o))
            total = total + r.gz[o]
        r.mine[...] = total
        r.rin[row] = total
        each(1, ROWS, lambda o: share_copy(o).start())

    def reduce_row():
        def wait(o):
            peer = rem(row + ROWS - o, ROWS)
            arrival(r.rin.at[peer], r.wsem, o, (peer, col))

        each(1, ROWS, wait)
        total = r.rin[0]
        for i in range(1, ROWS):
            total = total + r.rin[i]
        r.full[member, zl] = total
        for o in range(1, 4):
            plane_return(o).start()

    def return_members():
        for o in range(1, 4):
            arrival(r.full.at[member, rem(zl + 4 - o, 4)], r.isem, o, plane_dev(4 - o))
        for o in range(1, 8):
            member_return(o).start()

    def events(g):
        for at, body in (
            (4, lambda: (y_far(zero), z_arrive(zero + 2))),
            (6, lambda: y_arrive(zero + 1)),
            (5, reduce_members),
            (7, reduce_planes),
            (8, lambda: z_arrive(zero + 3)),
            (9, lambda: (y_far(zero + 1), y_arrive(zero + 2))),
            (10, reduce_row),
            (12, lambda: (y_far(zero + 2), y_arrive(zero + 3))),
            (13, return_members),
            (15, lambda: y_far(zero + 3)),
        ):

            @pl.when(g == at)
            def _():
                body()

    def step(g, carry):
        events(g)
        k, d = use(g)
        kk, dd = use(g - 2)
        core_wait(kk, dd)
        for h in range(2):
            tile_row(k, d, c, h)
        for h in range(2):
            tile_row(kk, dd, 1 - c, h)
        return carry

    for h in range(2):
        tile_row(zero, zero, c, h)
    z_arrive(zero + 1)
    y_arrive(zero)
    for h in range(2):
        tile_row(zero, zero + 1, c, h)
    lax.fori_loop(2, 16, step, 0)

    def last(g):
        kk, dd = use(g)
        core_wait(kk, dd)
        for h in range(2):
            tile_row(kk, dd, 1 - c, h)

    each(14, 16, last)

    for o in range(1, 8):
        arrival(r.full.at[rem(member + 8 - o, 8)], r.bsem, o, member_dev(8 - o))
    for k in range(2):
        gwo_ref[:, k * T : (k + 1) * T] = r.full[k * 4 : (k + 1) * 4].reshape(T, T)

    def drain_plane(k):
        z = plane(k)
        for d in range(4):
            core_copy(k, d).wait_send()
        for h in range(2):
            far_copy(k, h).wait_send()
            near_copy(k, 0, h).wait_send()
            near_copy(k, 1, h).wait_send()

            @pl.when(((z == zl) | (zl - z == 1)) & (zl < 3))
            def _():
                z_copy(z, True, h).wait_send()

            @pl.when(((z == zl) | (z - zl == 1)) & (zl > 0))
            def _():
                z_copy(z, False, h).wait_send()

            @pl.when((z == zl) & end)
            def _():
                end_copy(h).wait_send()

    def drain():
        each(0, 4, drain_plane)

        for o in range(1, 8):
            scatter_copy(o).wait_send()
            member_return(o).wait_send()
        for o in range(1, 4):
            reduce_copy(o).wait_send()
            plane_return(o).wait_send()
        each(1, ROWS, lambda o: share_copy(o).wait_send())

    return drain


SOURCES = ("cols", "x", "counts", "pos", "keep", "w", "b", "cot", "drop")
RESULTS = ("hid", "ht", "invo", "parts", "gwo")
BUFFERS = {
    "cols": ((TPR, TILE_ROWS), I32),
    "x": ((2 * T, T), F32),
    "counts": ((TPR, TILE_ROWS), I32),
    "pos": ((TILE_ROWS, SLOTS), I32),
    "keep": ((TILE_ROWS, SLOTS), I32),
    "w": ((T, 2 * T), F32),
    "b": ((1, 2 * T), F32),
    "cot": ((2 * T, 2 * T), F32),
    "drop": ((2 * T, 2 * T), I32),
    "code": ((TILE_ROWS, SLOTS), I32),
    "xg": ((ROWS, 2, T, T), F32),
    "deg": ((8, 8, T), F32),
    "degin": ((8, 8, T), F32),
    "degsum": ((8, T), F32),
    "degz": ((4, 8, T), F32),
    "inv": ((8, T), F32),
    "invg": ((ROWS, 8, T), F32),
    "adj": ((TILE_ROWS, T, TPR * T), BF16),
    "scaled": ((SRC_TILES, 2 * T, T), BF16),
    "pbuf": ((16, 2, T, T), F32),
    "cbuf": ((16, 2, T, T), F32),
    "q": ((16, 2, T, T), F32),
    "yfar": ((4, 2, T, T), F32),
    "yacc": ((4, 2, T, T), F32),
    "ynear": ((4, 2, 2, T, T), F32),
    "tot": ((4, 2, T, T), F32),
    "zin": ((4, 2, T, T), F32),
    "zmid": ((2, T, T), F32),
    "zout": ((2, T, T), F32),
    "agg": ((2, T, T), F32),
    "g": ((4, 4, 2, 2, T, T), F32),
    "gw": ((8, 4, 8, T), F32),
    "gin": ((8, 4, 8, T), F32),
    "gsum": ((4, 8, T), F32),
    "gz": ((4, 8, T), F32),
    "rin": ((ROWS, 8, T), F32),
    "mine": ((8, T), F32),
    "full": ((8, 4, 8, T), F32),
}
LINKS = {
    "xpair": (2,),
    "xnear": (2, 2, 2),
    "xfar": (2, 2),
    "dsem": (8,),
    "esem": (4,),
    "vsem": (ROWS,),
    "fcore": (16,),
    "ffar": (4, 2),
    "fnear": (4, 2, 2),
    "fplane": (4, 2),
    "fend": (2,),
    "gchain": (4, 2, 2),
    "gnear": (4, 2, 2),
    "gfar": (4, 2),
    "gcore": (4, 4),
    "gsem": (8,),
    "hsem": (4,),
    "wsem": (ROWS,),
    "isem": (4,),
    "bsem": (8,),
}
LOADS = SOURCES


def layer_kernel(*refs):
    inputs = named(SOURCES, refs)
    outputs = named(RESULTS, refs[len(SOURCES) :])
    r = named(tuple(BUFFERS), refs[len(SOURCES) + len(RESULTS) : -1], tuple(LINKS))
    p = Place()
    loads = {
        name: pltpu.make_async_copy(getattr(inputs, name), getattr(r, name), refs[-1].at[i])
        for i, name in enumerate(LOADS)
    }
    for copy in loads.values():
        copy.start()
    barrier = pltpu.get_barrier_semaphore()
    for o in range(1, ROWS):
        signal(barrier, (rem(p.row + o, ROWS), p.col))
    for o in range(1, 8):
        signal(barrier, (p.row, p.zl * 8 + rem(rem(p.col, 8) + o, 8)))
    for o in range(1, 4):
        signal(barrier, (p.row, rem(p.zl + o, 4) * 8 + rem(p.col, 8)))
    for copy in loads.values():
        copy.wait()
    drain_gather = gather_features(p, r, lambda: pl.semaphore_wait(barrier, ROWS + 9))
    drain_forward = forward_sum(p, r, r.agg)
    node_update(r, outputs.hid, outputs.ht)
    drain_spread = spread_gradients(p, r, outputs.ht, outputs.parts, outputs.gwo)
    outputs.invo[...] = r.inv[...]
    drain_gather()
    drain_forward()
    drain_spread()


def layer_call(*args):
    return pl.pallas_call(
        layer_kernel,
        name="layer",
        out_shape=(
            shape(2 * T, 2 * T),
            shape(2, T, T),
            shape(8, T),
            shape(TILE_ROWS, TPR, T, T),
            shape(T, 2 * T),
        ),
        in_specs=[HBM] * 9,
        out_specs=(VMEM,) * 5,
        scratch_shapes=[
            (pltpu.SMEM if name == "cols" else pltpu.VMEM)(dims, dtype)
            for name, (dims, dtype) in BUFFERS.items()
        ]
        + sem_pairs(LINKS.values())
        + [pltpu.SemaphoreType.DMA((len(LOADS),))],
        compiler_params=pltpu.CompilerParams(
            collective_id=1, has_side_effects=True, vmem_limit_bytes=32 * MB
        ),
    )(*[in_hbm(arg) for arg in args])


def place_kernel(
    cols_hbm, parts_ref, hid_ref, gw_ref, out_ref, hid_out, gw_out, cols_ref, sems
):
    copy = pltpu.make_async_copy(cols_hbm, cols_ref, sems.at[0])
    hid_copy = pltpu.make_async_copy(hid_ref, hid_out, sems.at[1])
    gw_copy = pltpu.make_async_copy(gw_ref, gw_out, sems.at[2])
    copy.start()
    hid_copy.start()
    gw_copy.start()
    out_ref[...] = jnp.zeros_like(out_ref)
    copy.wait()

    def tile_row(t, carry):
        for k in range(TPR):
            out_ref[cols_ref[k, t]] += parts_ref[t, k]
        return carry

    lax.fori_loop(0, TILE_ROWS, tile_row, 0, unroll=2)
    hid_copy.wait()
    gw_copy.wait()


def place_call(cols, parts, hidden, grad_weight):
    return pl.pallas_call(
        place_kernel,
        name="place_tiles",
        out_shape=(
            shape(SRC_TILES, T, T),
            pltpu.HBM((2 * T, 2 * T), F32),
            pltpu.HBM((T, 2 * T), F32),
        ),
        in_specs=[HBM] + [VMEM] * 3,
        out_specs=(VMEM, HBM, HBM),
        scratch_shapes=[pltpu.SMEM((TPR, TILE_ROWS), I32), pltpu.SemaphoreType.DMA((3,))],
        compiler_params=pltpu.CompilerParams(vmem_limit_bytes=4 * MB),
    )(in_hbm(cols), parts, hidden, grad_weight)


def sum_row_kernel(*refs):
    q_ref, ht_ref, inv_ref, gf_ref = refs[:4]
    r = named(("xfar", "xacc", "xnear", "tot", "zin"), refs[4:], ("fsem", "nsem", "zsem"))
    p = Place()
    zh, x = p.zh, p.x
    right_dev, left_dev = p.in_row(zh, rem(x + 1, 4)), p.in_row(zh, rem(x + 3, 4))
    pair_dev = p.in_row(1 - zh, x)
    barrier = pltpu.get_barrier_semaphore()
    for dev in (right_dev, left_dev, pair_dev):
        signal(barrier, dev)
    pl.semaphore_wait(barrier, 3)
    base = ((1 - zh) * 4, zh * 4)

    def block(k, d):
        return base[k] + rem(x + d, 4)

    def far_copy(k, way):
        return link(
            q_ref.at[block(k, 2), way],
            r.xfar.at[k, way],
            r.fsem,
            (k, way),
            left_dev if way else right_dev,
        )

    def near_copy(k, way, h):
        src = r.xacc.at[k, way] if way == h else q_ref.at[block(k, 1 + 2 * way), h]
        return link(
            src, r.xnear.at[k, way, h], r.nsem, (k, way, h), left_dev if way else right_dev
        )

    def pair_copy(h):
        return link(r.tot.at[0, h], r.zin.at[h], r.zsem, h, pair_dev)

    def first(k):
        for way in range(2):
            far_copy(k, way).start()
        for way in range(2):
            near_copy(k, way, 1 - way).start()

    def second(k):
        for way, dev in ((0, left_dev), (1, right_dev)):
            arrival(r.xfar.at[k, way], r.fsem, (k, way), dev)
            r.xacc[k, way] = q_ref[block(k, 1 + 2 * way), way] + r.xfar[k, way]
            near_copy(k, way, way).start()

    def total(k, h):
        for way, dev in ((0, left_dev), (1, right_dev)):
            arrival(r.xnear.at[k, way, h], r.nsem, (k, way, h), dev)
        r.tot[k, h] = q_ref[block(k, 0), h] + (r.xnear[k, 0, h] + r.xnear[k, 1, h])

    first(0)
    second(0)
    first(1)
    for h in range(2):
        total(0, h)
        pair_copy(h).start()
    second(1)
    for h in range(2):
        total(1, h)
    for h in range(2):
        arrival(r.zin.at[h], r.zsem, h, pair_dev)
        back = (r.tot[1, h] + r.zin[h]) + ht_ref[h]
        gf_ref[h * T : (h + 1) * T, :] = jnp.transpose(
            back * jnp.broadcast_to(inv_ref[h : h + 1, :], (T, T))
        )
    for h in range(2):
        pair_copy(h).wait_send()
        for k in range(2):
            far_copy(k, h).wait_send()
            for way in range(2):
                near_copy(k, way, h).wait_send()


def sum_row_call(parts, ht, inv):
    return pl.pallas_call(
        sum_row_kernel,
        name="sum_over_row",
        out_shape=shape(2 * T, T),
        in_specs=[VMEM] * 3,
        out_specs=VMEM,
        scratch_shapes=[
            pltpu.VMEM((2, 2, T, T), F32),
            pltpu.VMEM((2, 2, T, T), F32),
            pltpu.VMEM((2, 2, 2, T, T), F32),
            pltpu.VMEM((2, 2, T, T), F32),
            pltpu.VMEM((2, T, T), F32),
        ]
        + sem_pairs(((2, 2), (2, 2, 2), (2,))),
        compiler_params=pltpu.CompilerParams(
            collective_id=2, has_side_effects=True, vmem_limit_bytes=6 * MB
        ),
    )(parts.reshape(ROWS, 2, T, T), ht, inv)


def shards(features, weight, bias, cot, drop, tile_cols, counts, pos, keep):
    cols = jnp.transpose(tile_cols[0, 0])
    hidden, ht, inv, parts, grad_weight = layer_call(
        cols,
        features,
        jnp.transpose(counts[0, 0]),
        pos[0, 0],
        keep[0, 0],
        weight,
        bias.reshape(1, 2 * T),
        cot,
        drop,
    )
    back, hidden, grad_weight = place_call(cols, parts, hidden, grad_weight)
    grad_features = sum_row_call(back, ht, inv)
    return hidden, grad_features, grad_weight


def solution(mesh):
    nodes = P(("row", "col"), None)
    block = P("row", "col", None, None)
    return jax.shard_map(
        shards,
        mesh=mesh,
        in_specs=(nodes, P(), P(), nodes, nodes, block, block, block, block),
        out_specs=(nodes, nodes, P()),
        check_vma=False,
    )
```

```python
from types import SimpleNamespace

import jax
import jax.numpy as jnp
from jax import lax
from jax.experimental import pallas as pl
from jax.experimental.pallas import tpu as pltpu
from jax.sharding import PartitionSpec as P

MESH = pl.DeviceIdType.MESH
HIGHEST = lax.Precision.HIGHEST
F32, BF16, I32 = jnp.float32, jnp.bfloat16, jnp.int32

T = 128
ROWS, COLS = 8, 32
TILE_ROWS, TPR, EPT = 64, 4, 64
SLOTS = TPR * EPT
SRC_TILES = 16
MB = 1 << 20
VMEM = pl.BlockSpec(memory_space=pltpu.VMEM)
HBM = pl.BlockSpec(memory_space=pltpu.HBM)
NT = (((1,), (1,)), ((), ()))


def in_hbm(array):
    return pltpu.with_memory_space_constraint(array, pltpu.HBM)


def rem(a, n):
    return lax.rem(a, jnp.int32(n))


def div(a, n):
    return lax.div(a, jnp.int32(n))


def shape(*dims, dtype=F32):
    return jax.ShapeDtypeStruct(dims, dtype)


def link_from(src, dst, sems, sent, received, dev):
    return pltpu.make_async_remote_copy(
        src_ref=src,
        dst_ref=dst,
        send_sem=sems.send.at[sent],
        recv_sem=sems.recv.at[received],
        device_id=dev,
        device_id_type=MESH,
    )


def link(src, dst, sems, where, dev):
    return link_from(src, dst, sems, where, where, dev)


def arrival(ref, sems, where, dev):
    link(ref, ref, sems, where, dev).wait_recv()


def signal(barrier, dev):
    pl.semaphore_signal(barrier, inc=1, device_id=dev, device_id_type=MESH)


def named(names, refs, pairs=()):
    out = SimpleNamespace(**dict(zip(names, refs)))
    rest = refs[len(names) :]
    for i, name in enumerate(pairs):
        setattr(out, name, SimpleNamespace(send=rest[2 * i], recv=rest[2 * i + 1]))
    return out


def sem_pairs(dims):
    return [pltpu.SemaphoreType.DMA(d) for d in dims for _ in range(2)]


def each(low, high, body):
    def run(o, carry):
        body(o)
        return carry

    lax.fori_loop(low, high, run, 0)


def slot_codes(counts, pos, keep):
    lane = lax.broadcasted_iota(I32, (TILE_ROWS, SLOTS), 1)
    counts = jnp.transpose(counts)
    limit = jnp.broadcast_to(counts[:, 0:1], (TILE_ROWS, SLOTS))
    for k in range(1, TPR):
        limit = jnp.where(
            lane >= k * EPT, jnp.broadcast_to(counts[:, k : k + 1], (TILE_ROWS, SLOTS)), limit
        )
    live = ((lane & (EPT - 1)) < limit) & (keep == 1)
    return jnp.where(live, pos >> 7, 4 * T)


def split(values, axis):
    high = values.astype(BF16)
    low = (values - high.astype(F32)).astype(BF16)
    return jnp.concatenate([high, low], axis=axis)


def hot_dst(code_row, side):
    return jnp.where(side == jnp.broadcast_to(code_row, (T, SLOTS)), 1.0, 0.0).astype(BF16)


def hot_src(pos_row, side, lane):
    code = (pos_row & (T - 1)) + ((lane >> 6) & 1) * T
    return jnp.where(side == jnp.broadcast_to(code, (2 * T, SLOTS)), 1.0, 0.0).astype(BF16)


def gelu_pair(values):
    half = 0.5 * (1.0 + lax.erf(values * 0.7071067811865476))
    slope = half + values * jnp.exp(-0.5 * values * values) * 0.3989422804014327
    return values * half, slope


def far_first(zl, k):
    near = jnp.where(zl >= 2, 3 - zl, zl)
    inner = jnp.where(k == 0, 3, jnp.where(k == 1, 0, 4 - k))
    plane = jnp.where(near == 0, 3 - k, inner)
    return jnp.where(zl >= 2, 3 - plane, plane)


def chosen(g, values):
    out = jnp.int32(values[0])
    for i in range(1, len(values)):
        out = jnp.where(g == i, values[i], out)
    return out


class Place:
    def __init__(self):
        self.row, self.col = lax.axis_index("row"), lax.axis_index("col")
        self.zh, self.x = div(self.row, 4), rem(self.row, 4)
        self.zl, self.y, self.c = div(self.col, 8), rem(div(self.col, 2), 4), rem(self.col, 2)

    def in_row(self, zh, x):
        return (zh * 4 + x, self.col)

    def in_col(self, zl, y, c):
        return (self.row, (zl * 4 + y) * 2 + c)


def gather_features(p, r, barrier_wait):
    row, col, zh, x = p.row, p.col, p.zh, p.x
    pair = 1 - zh
    right, left = rem(x + 1, 4), rem(x + 3, 4)
    right_dev, left_dev, pair_dev = p.in_row(zh, right), p.in_row(zh, left), p.in_row(pair, x)
    across_dev = p.in_row(zh, rem(x + 2, 4))
    for h in range(2):
        r.xg[row, h] = jnp.transpose(r.x[h * T : (h + 1) * T, :])
    r.code[...] = slot_codes(r.counts[...], r.pos[...], r.keep[...])
    def near_copy(k, zz, way, h):
        slot = r.xg.at[zz * 4 + x, h]
        return link(slot, slot, r.xnear, (k, way, h), left_dev if way else right_dev)

    def near_wait(k, zz, way, h):
        slot = r.xg.at[zz * 4 + (right if way else left), h]
        arrival(slot, r.xnear, (k, way, h), right_dev if way else left_dev)

    def far_copy(h):
        slot = r.xg.at[zh * 4 + (right if h else left), h]
        return link(slot, slot, r.xfar, (0, h), left_dev if h else right_dev)

    def across_copy(h):
        slot = r.xg.at[pair * 4 + x, h]
        return link(slot, slot, r.xfar, (1, h), across_dev)

    def pair_copy(h):
        return link(r.xg.at[row, h], r.xg.at[row, h], r.xpair, h, pair_dev)

    ones = jnp.ones((8, SLOTS), BF16)
    side = lax.broadcasted_iota(I32, (T, SLOTS), 0)
    wide = lax.broadcasted_iota(I32, (2 * T, SLOTS), 0)
    lane = lax.broadcasted_iota(I32, (1, SLOTS), 1)
    sub = lax.broadcasted_iota(I32, (8, T), 0)

    zl, member = p.zl, rem(col, 8)

    def count(m, carry):
        tile = jnp.zeros((8, T), F32)
        for i in range(8):
            t = 2 * ((i // 2) * 8 + m) + i % 2
            hot = hot_dst(r.code[pl.ds(t, 1), :], side)
            row_sums = lax.dot_general(ones, hot, NT, preferred_element_type=F32)
            tile = jnp.where(sub == i, row_sums, tile)
        r.deg[m] = tile
        return carry

    lax.fori_loop(0, 8, count, 0)
    barrier_wait()
    for h in range(2):
        pair_copy(h).start()
    for way, h in ((0, 0), (1, 1), (0, 1), (1, 0)):
        near_copy(0, zh, way, h).start()


    def member_copy(o):
        peer = rem(member + o, 8)
        return link(r.deg.at[peer], r.degin.at[o], r.dsem, o, (row, zl * 8 + peer))

    def member_wait(o):
        peer = rem(member + 8 - o, 8)
        arrival(r.degin.at[o], r.dsem, o, (row, zl * 8 + peer))

    def plane_copy(o):
        dev = (row, rem(zl + o, 4) * 8 + member)
        return link(r.degsum, r.degz.at[o], r.esem, o, dev)

    def plane_wait(o):
        arrival(r.degz.at[o], r.esem, o, (row, rem(zl + 4 - o, 4) * 8 + member))

    for o in range(1, 8):
        member_copy(o).start()

    def block(i, carry):
        for u in range(4):
            t = 4 * i + u
            dst = hot_dst(r.code[pl.ds(t, 1), :], side)
            src = hot_src(r.pos[pl.ds(t, 1), :], wide, lane)
            for q in range(2):
                part = slice(q * T, (q + 1) * T)
                r.adj[t, :, q * 2 * T : (q + 1) * 2 * T] = lax.dot_general(
                    dst[:, part], src[:, part], NT, preferred_element_type=F32
                ).astype(BF16)
        return carry

    def pass_on(h):
        arrival(r.xg.at[pair * 4 + x, h], r.xpair, h, pair_dev)
        across_copy(h).start()
        near_copy(1, pair, 0, h).start()
        near_copy(1, pair, 1, h).start()

    lax.fori_loop(0, 3, block, 0)
    total = r.deg[member]
    for o in range(1, 8):
        member_wait(o)
        total = total + r.degin[o]
    r.degsum[...] = total
    for o in range(1, 4):
        plane_copy(o).start()
    for h in range(2):
        near_wait(0, zh, h, h)
        far_copy(h).start()
    pass_on(0)
    mine = pl.ds(2 * zl, 2)
    total = r.degsum[mine, :]
    for o in range(1, 4):
        plane_wait(o)
        total = total + r.degz[o, mine, :]
    r.inv[...] = jnp.ones((8, T), F32)
    r.inv[0:2, :] = lax.rsqrt(1.0 + total)
    r.invg[row] = r.inv[...]

    def inv_copy(o):
        return link(r.inv, r.invg.at[row], r.vsem, o, (rem(row + o, ROWS), col))

    each(1, ROWS, lambda o: inv_copy(o).start())
    pass_on(1)
    lax.fori_loop(3, 16, block, 0)

    def inv_wait(o):
        peer = rem(row + ROWS - o, ROWS)
        arrival(r.invg.at[peer], r.vsem, o, (peer, col))

    each(1, ROWS, inv_wait)
    for h in range(2):
        near_wait(0, zh, 1 - h, h)
        slot = r.xg.at[zh * 4 + rem(x + 2, 4), h]
        arrival(slot, r.xfar, (0, h), right_dev if h else left_dev)
        near_wait(1, pair, 0, h)
        near_wait(1, pair, 1, h)
        arrival(r.xg.at[pair * 4 + rem(x + 2, 4), h], r.xfar, (1, h), across_dev)

    def drain():
        for h in range(2):
            pair_copy(h).wait_send()
            far_copy(h).wait_send()
            across_copy(h).wait_send()
            for k, zz in ((0, zh), (1, pair)):
                for way in range(2):
                    near_copy(k, zz, way, h).wait_send()
        each(1, ROWS, lambda o: inv_copy(o).wait_send())
        for o in range(1, 8):
            member_copy(o).wait_send()
        for o in range(1, 4):
            plane_copy(o).wait_send()

    return drain


SUM_ORDER = (
    (0, 0), (1, 0), (2, 0), (3, 0), (0, 1), (0, 2), (0, 3), (1, 1),
    (1, 2), (1, 3), (2, 1), (2, 2), (2, 3), (3, 1), (3, 2), (3, 3),
)
SUM_LAG = 3


def forward_sum(p, r, out_ref):
    row, zl, y, c = p.row, p.zl, p.y, p.c
    core_dev = p.in_col(zl, y, 1 - c)
    right_dev, left_dev = p.in_col(zl, rem(y + 1, 4), c), p.in_col(zl, rem(y + 3, 4), c)
    for u in range(SRC_TILES):
        i, h = u // 2, u % 2
        r.scaled[u] = split(
            r.xg[i, h] * jnp.broadcast_to(r.invg[i, h : h + 1, :], (T, T)), axis=0
        )
    q = r.q

    def tile_row(t):
        panel = jnp.concatenate([r.scaled[r.cols[k, t]] for k in range(TPR)], axis=1)
        both = lax.dot_general(panel, r.adj[t], NT, preferred_element_type=F32)
        return both[:T] + both[T:]

    def core_copy(g):
        return link(r.pbuf.at[g], r.cbuf.at[g], r.fcore, g, core_dev)

    def far_copy(k, way):
        return link(
            q.at[4 * k, way],
            r.yfar.at[k, way],
            r.ffar,
            (k, way),
            left_dev if way else right_dev,
        )

    def near_copy(k, way, h):
        src = r.yacc.at[k, way] if way == h else q.at[4 * k + 1 + way, h]
        return link(
            src, r.ynear.at[k, way, h], r.fnear, (k, way, h), left_dev if way else right_dev
        )

    inner = (zl == 1) | (zl == 2)
    inner_plane = jnp.where(zl <= 1, 1, 2)

    def plane_copy(k, h):
        slot = r.zin.at[zl, h]
        dev = p.in_col(far_first(zl, k), y, c)
        return link_from(r.tot.at[k, h], slot, r.fplane, (k, h), (zl, h), dev)

    def joint_copy(h):
        dev = p.in_col(far_first(zl, 0), y, c)
        return link_from(r.zout.at[h], r.zin.at[zl, h], r.fplane, (0, h), (zl, h), dev)

    def end_copy(h):
        return link(r.tot.at[0, h], r.zmid.at[h], r.fend, h, p.in_col(inner_plane, y, c))

    def finish(k, j):
        g = 4 * k + j
        core_copy(g).wait_recv()
        q[g] = q[g] + r.cbuf[g]

        @pl.when(j == 0)
        def _():
            far_copy(k, 0).start()
            far_copy(k, 1).start()

    def accumulate(k):
        for way, dev in ((0, left_dev), (1, right_dev)):
            arrival(r.yfar.at[k, way], r.ffar, (k, way), dev)
            r.yacc[k, way] = q[4 * k + 1 + way, way] + r.yfar[k, way]
            near_copy(k, way, way).start()
        for way in range(2):
            near_copy(k, way, 1 - way).start()

    def plane_sum(k, h):
        arrival(r.ynear.at[k, 0, h], r.fnear, (k, 0, h), left_dev)
        arrival(r.ynear.at[k, 1, h], r.fnear, (k, 1, h), right_dev)
        return q[4 * k + 3, h] + (r.ynear[k, 0, h] + r.ynear[k, 1, h])

    def place_in(i):
        return chosen(i, [b[0] for b in SUM_ORDER]), chosen(i, [b[1] for b in SUM_ORDER])

    def step(i, carry):
        k, j = place_in(i)
        g = 4 * k + j
        d = chosen(j, (2, 1, 3, 0))
        first = (far_first(zl, k) * 4 + rem(y + d, 4)) * 4
        for h in range(2):
            r.pbuf[g, h] = tile_row(first + 2 * (1 - c) + h)
        for h in range(2):
            q[g, h] = tile_row(first + 2 * c + h)
        core_copy(g).start()
        ready_k, ready_j = place_in(i - SUM_LAG)

        @pl.when(i >= SUM_LAG)
        def _():
            finish(ready_k, ready_j)

        @pl.when((i >= SUM_LAG) & (ready_j == 3))
        def _():
            accumulate(ready_k)

        return carry

    lax.fori_loop(0, 16, step, 0)

    def rest(i):
        k, j = place_in(i)
        finish(k, j)

    each(16 - SUM_LAG, 16, rest)
    accumulate(jnp.int32(3))
    for k in range(3):
        for h in range(2):
            r.tot[k, h] = plane_sum(k, h)
            if k > 0:
                plane_copy(k, h).start()
            else:

                @pl.when(jnp.logical_not(inner))
                def _():
                    end_copy(h).start()

        if k == 1:

            @pl.when(inner)
            def _():
                for h in range(2):
                    arrival(r.zmid.at[h], r.fend, h, core_dev)
                    r.zout[h] = r.tot[0, h] + r.zmid[h]
                    joint_copy(h).start()

    for h in range(2):
        out_ref[h] = plane_sum(3, h)
        for s in range(4):

            @pl.when((zl != s) & (zl + s != 3) | ((zl == 1) & (s == 2)) | ((zl == 2) & (s == 1)))
            def _():
                arrival(r.zin.at[s, h], r.fplane, (s, h), core_dev)
                out_ref[h] = out_ref[h] + r.zin[s, h]

    def drain_plane(k):
        for way in range(2):
            far_copy(k, way).wait_send()
            for h in range(2):
                near_copy(k, way, h).wait_send()
        for j in range(4):
            core_copy(4 * k + j).wait_send()

    def drain():
        each(0, 4, drain_plane)
        for h in range(2):
            for k in (1, 2):
                plane_copy(k, h).wait_send()

            @pl.when(inner)
            def _():
                joint_copy(h).wait_send()

            @pl.when(jnp.logical_not(inner))
            def _():
                end_copy(h).wait_send()

    return drain


def node_update(r, hid_ref, ht_ref):
    weight = r.w[...]
    bias = jnp.broadcast_to(r.b[...], (T, 2 * T))
    for h in range(2):
        part = slice(h * T, (h + 1) * T)
        inv_row = jnp.broadcast_to(r.inv[h : h + 1, :], (T, T))
        inv_col = jnp.transpose(inv_row)
        inv_col = jnp.concatenate([inv_col, inv_col], axis=1)
        agg = r.agg[h] + jnp.transpose(r.x[part, :]) * inv_row
        mixed = jnp.dot(
            jnp.transpose(agg), weight, precision=HIGHEST, preferred_element_type=F32
        )
        gelu, slope = gelu_pair(inv_col * mixed + bias)
        drop = r.drop[part, :].astype(F32) / 0.9
        hid_ref[part, :] = gelu * drop
        grad = inv_col * (r.cot[part, :] * drop * slope)
        ht_ref[h] = lax.dot_general(weight, grad, NT, precision=HIGHEST, preferred_element_type=F32)
        r.agg[h] = agg
        r.grad[h] = grad


def weight_update(r):
    total = jnp.zeros((T, 2 * T), F32)
    for h in range(2):
        total = total + jnp.dot(
            r.agg[h], r.grad[h], precision=HIGHEST, preferred_element_type=F32
        )
    for k in range(2):
        r.gw[k * 4 : (k + 1) * 4] = total[:, k * T : (k + 1) * T].reshape(4, 4, 8, T)


BLOCK_ORDER = (
    (0, 0), (0, 1), (0, 3), (1, 0), (0, 2), (2, 0), (1, 1), (1, 3),
    (3, 0), (1, 2), (2, 1), (2, 3), (2, 2), (3, 1), (3, 3), (3, 2),
)


def spread_gradients(p, r, ht_ref, parts_ref, gwo_ref, drains):
    row, col, zl, y, c = p.row, p.col, p.zl, p.y, p.c
    right, left, across = rem(y + 1, 4), rem(y + 3, 4), rem(y + 2, 4)
    core_dev = p.in_col(zl, y, 1 - c)
    right_dev, left_dev = p.in_col(zl, right, c), p.in_col(zl, left, c)
    up_dev = p.in_col(jnp.minimum(zl + 1, 3), y, c)
    down_dev = p.in_col(jnp.maximum(zl - 1, 0), y, c)
    r.g[zl, y, c] = ht_ref[...]

    def plane(k):
        return far_first(zl, 3 - k)

    def z_copy(z, up, h):
        slot = r.g.at[z, y, c, h]
        return link(slot, slot, r.gchain, (z, 0 if up else 1, h), up_dev if up else down_dev)

    end = (zl == 0) | (zl == 3)

    def end_copy(h):
        slot = r.g.at[zl, y, c, h]
        low = jnp.where(zl == 0, 1, 0)
        return link_from(
            slot, slot, r.gchain, (zl, low, h), (zl, 1 - low, h), p.in_col(3 - zl, y, c)
        )

    def near_copy(k, way, h):
        slot = r.g.at[plane(k), y, c, h]
        return link(slot, slot, r.gnear, (k, way, h), left_dev if way else right_dev)

    def far_copy(k, h):
        slot = r.g.at[plane(k), right if h else left, c, h]
        return link(slot, slot, r.gfar, (k, h), left_dev if h else right_dev)

    def core_copy(k, d):
        slot = r.g.at[plane(k), rem(y + d, 4), c]
        return link(slot, slot, r.gcore, (k, d), core_dev)

    def core_wait(k, d):
        arrival(r.g.at[plane(k), rem(y + d, 4), 1 - c], r.gcore, (k, d), core_dev)

    def near_wait(k, way, h):
        slot = r.g.at[plane(k), right if way else left, c, h]
        arrival(slot, r.gnear, (k, way, h), right_dev if way else left_dev)

    def z_arrive(k):
        z = plane(k)
        below = z < zl
        way = jnp.where(below, 0, 1)
        for h in range(2):
            arrival(r.g.at[z, y, c, h], r.gchain, (z, way, h), core_dev)

            @pl.when((zl - z == 1) & (zl < 3))
            def _():
                z_copy(z, True, h).start()

            @pl.when((z - zl == 1) & (zl > 0))
            def _():
                z_copy(z, False, h).start()

            near_copy(k, h, h).start()
        near_copy(k, 0, 1).start()
        near_copy(k, 1, 0).start()
        core_copy(k, 0).start()

    def y_arrive(k):
        near_wait(k, 0, 0)
        far_copy(k, 0).start()
        near_wait(k, 1, 1)
        far_copy(k, 1).start()
        near_wait(k, 0, 1)
        core_copy(k, 3).start()
        near_wait(k, 1, 0)
        core_copy(k, 1).start()

    def y_far(k):
        for h in range(2):
            arrival(
                r.g.at[plane(k), across, c, h], r.gfar, (k, h), right_dev if h else left_dev
            )
        core_copy(k, 2).start()

    def tile_row(k, d, cc, h):
        z, yy = plane(k), rem(y + d, 4)
        t = ((z * 4 + yy) * 2 + cc) * 2 + h
        adj = r.adj[t]
        back = jnp.dot(
            split(r.g[z, yy, cc, h], axis=1),
            jnp.concatenate([adj, adj], axis=0),
            preferred_element_type=F32,
        )
        for i in range(TPR):
            parts_ref[t, i] = back[:, i * T : (i + 1) * T]

    def use(g):
        return chosen(g, [b[0] for b in BLOCK_ORDER]), chosen(g, [b[1] for b in BLOCK_ORDER])

    zero = jnp.int32(0)
    for h in range(2):

        @pl.when(zl < 3)
        def _():
            z_copy(zl, True, h).start()

        @pl.when(zl > 0)
        def _():
            z_copy(zl, False, h).start()

        @pl.when(end)
        def _():
            end_copy(h).start()

        near_copy(zero, h, h).start()
    near_copy(zero, 0, 1).start()
    near_copy(zero, 1, 0).start()
    core_copy(zero, 0).start()

    member = rem(col, 8)

    def member_dev(o):
        return (row, zl * 8 + rem(member + o, 8))

    def plane_dev(o):
        return (row, rem(zl + o, 4) * 8 + member)

    def scatter_copy(o):
        return link(r.gw.at[rem(member + o, 8)], r.gin.at[o], r.gsem, o, member_dev(o))

    def reduce_copy(o):
        return link(r.gsum.at[rem(zl + o, 4)], r.gz.at[o], r.hsem, o, plane_dev(o))

    def share_copy(o):
        return link(r.mine, r.rin.at[row], r.wsem, o, (rem(row + o, ROWS), col))

    def plane_return(o):
        slot = r.full.at[member, zl]
        return link(slot, slot, r.isem, o, plane_dev(o))

    def member_return(o):
        slot = r.full.at[member]
        return link(slot, slot, r.bsem, o, member_dev(o))

    weight_update(r)
    for o in range(1, 8):
        scatter_copy(o).start()
    for drain_before in drains:
        drain_before()

    def reduce_members():
        total = r.gw[member]
        for o in range(1, 8):
            arrival(r.gin.at[o], r.gsem, o, member_dev(8 - o))
            total = total + r.gin[o]
        r.gsum[...] = total
        for o in range(1, 4):
            reduce_copy(o).start()

    def reduce_planes():
        total = r.gsum[zl]
        for o in range(1, 4):
            arrival(r.gz.at[o], r.hsem, o, plane_dev(4 - o))
            total = total + r.gz[o]
        r.mine[...] = total
        r.rin[row] = total
        each(1, ROWS, lambda o: share_copy(o).start())

    def reduce_row():
        def wait(o):
            peer = rem(row + ROWS - o, ROWS)
            arrival(r.rin.at[peer], r.wsem, o, (peer, col))

        each(1, ROWS, wait)
        total = r.rin[0]
        for i in range(1, ROWS):
            total = total + r.rin[i]
        r.full[member, zl] = total
        for o in range(1, 4):
            plane_return(o).start()

    def return_members():
        for o in range(1, 4):
            arrival(r.full.at[member, rem(zl + 4 - o, 4)], r.isem, o, plane_dev(4 - o))
        for o in range(1, 8):
            member_return(o).start()

    def drain_plane(k):
        z = plane(k)
        for d in range(4):
            core_copy(k, d).wait_send()
        for h in range(2):
            far_copy(k, h).wait_send()
            near_copy(k, 0, h).wait_send()
            near_copy(k, 1, h).wait_send()

            @pl.when(((z == zl) | (zl - z == 1)) & (zl < 3))
            def _():
                z_copy(z, True, h).wait_send()

            @pl.when(((z == zl) | (z - zl == 1)) & (zl > 0))
            def _():
                z_copy(z, False, h).wait_send()

            @pl.when((z == zl) & end)
            def _():
                end_copy(h).wait_send()

    def early_drain():
        each(0, 2, drain_plane)
        for o in range(1, 8):
            scatter_copy(o).wait_send()
        for o in range(1, 4):
            reduce_copy(o).wait_send()
        each(1, ROWS, lambda o: share_copy(o).wait_send())

    def events(g):
        for at, body in (
            (4, lambda: (y_far(zero), z_arrive(zero + 2))),
            (6, lambda: y_arrive(zero + 1)),
            (5, reduce_members),
            (7, reduce_planes),
            (8, lambda: z_arrive(zero + 3)),
            (9, lambda: (y_far(zero + 1), y_arrive(zero + 2))),
            (10, reduce_row),
            (12, lambda: (y_far(zero + 2), y_arrive(zero + 3))),
            (13, return_members),
            (14, early_drain),
            (15, lambda: y_far(zero + 3)),
        ):

            @pl.when(g == at)
            def _():
                body()

    def step(g, carry):
        events(g)
        k, d = use(g)
        kk, dd = use(g - 2)
        core_wait(kk, dd)
        for h in range(2):
            tile_row(k, d, c, h)
        for h in range(2):
            tile_row(kk, dd, 1 - c, h)
        return carry

    for h in range(2):
        tile_row(zero, zero, c, h)
    z_arrive(zero + 1)
    y_arrive(zero)
    for h in range(2):
        tile_row(zero, zero + 1, c, h)
    lax.fori_loop(2, 16, step, 0)

    def last(g):
        kk, dd = use(g)
        core_wait(kk, dd)
        for h in range(2):
            tile_row(kk, dd, 1 - c, h)

    each(14, 16, last)

    for o in range(1, 8):
        arrival(r.full.at[rem(member + 8 - o, 8)], r.bsem, o, member_dev(8 - o))
    for k in range(2):
        gwo_ref[:, k * T : (k + 1) * T] = r.full[k * 4 : (k + 1) * 4].reshape(T, T)

    def drain():
        each(2, 4, drain_plane)
        for o in range(1, 8):
            member_return(o).wait_send()
        for o in range(1, 4):
            plane_return(o).wait_send()

    return drain


SOURCES = ("cols", "x", "counts", "pos", "keep", "w", "b", "cot", "drop")
RESULTS = ("hid", "ht", "invo", "parts", "gwo")
BUFFERS = {
    "cols": ((TPR, TILE_ROWS), I32),
    "x": ((2 * T, T), F32),
    "counts": ((TPR, TILE_ROWS), I32),
    "pos": ((TILE_ROWS, SLOTS), I32),
    "keep": ((TILE_ROWS, SLOTS), I32),
    "w": ((T, 2 * T), F32),
    "b": ((1, 2 * T), F32),
    "cot": ((2 * T, 2 * T), F32),
    "drop": ((2 * T, 2 * T), I32),
    "code": ((TILE_ROWS, SLOTS), I32),
    "xg": ((ROWS, 2, T, T), F32),
    "deg": ((8, 8, T), F32),
    "degin": ((8, 8, T), F32),
    "degsum": ((8, T), F32),
    "degz": ((4, 8, T), F32),
    "inv": ((8, T), F32),
    "invg": ((ROWS, 8, T), F32),
    "adj": ((TILE_ROWS, T, TPR * T), BF16),
    "scaled": ((SRC_TILES, 2 * T, T), BF16),
    "pbuf": ((16, 2, T, T), F32),
    "cbuf": ((16, 2, T, T), F32),
    "q": ((16, 2, T, T), F32),
    "yfar": ((4, 2, T, T), F32),
    "yacc": ((4, 2, T, T), F32),
    "ynear": ((4, 2, 2, T, T), F32),
    "tot": ((4, 2, T, T), F32),
    "zin": ((4, 2, T, T), F32),
    "zmid": ((2, T, T), F32),
    "zout": ((2, T, T), F32),
    "agg": ((2, T, T), F32),
    "g": ((4, 4, 2, 2, T, T), F32),
    "grad": ((2, T, 2 * T), F32),
    "gw": ((8, 4, 8, T), F32),
    "gin": ((8, 4, 8, T), F32),
    "gsum": ((4, 8, T), F32),
    "gz": ((4, 8, T), F32),
    "rin": ((ROWS, 8, T), F32),
    "mine": ((8, T), F32),
    "full": ((8, 4, 8, T), F32),
}
LINKS = {
    "xpair": (2,),
    "xnear": (2, 2, 2),
    "xfar": (2, 2),
    "dsem": (8,),
    "esem": (4,),
    "vsem": (ROWS,),
    "fcore": (16,),
    "ffar": (4, 2),
    "fnear": (4, 2, 2),
    "fplane": (4, 2),
    "fend": (2,),
    "gchain": (4, 2, 2),
    "gnear": (4, 2, 2),
    "gfar": (4, 2),
    "gcore": (4, 4),
    "gsem": (8,),
    "hsem": (4,),
    "wsem": (ROWS,),
    "isem": (4,),
    "bsem": (8,),
}
LOADS = SOURCES


def layer_kernel(*refs):
    inputs = named(SOURCES, refs)
    outputs = named(RESULTS, refs[len(SOURCES) :])
    r = named(tuple(BUFFERS), refs[len(SOURCES) + len(RESULTS) : -1], tuple(LINKS))
    p = Place()
    loads = {
        name: pltpu.make_async_copy(getattr(inputs, name), getattr(r, name), refs[-1].at[i])
        for i, name in enumerate(LOADS)
    }
    for copy in loads.values():
        copy.start()
    barrier = pltpu.get_barrier_semaphore()
    for o in range(1, ROWS):
        signal(barrier, (rem(p.row + o, ROWS), p.col))
    for o in range(1, 8):
        signal(barrier, (p.row, p.zl * 8 + rem(rem(p.col, 8) + o, 8)))
    for o in range(1, 4):
        signal(barrier, (p.row, rem(p.zl + o, 4) * 8 + rem(p.col, 8)))
    for copy in loads.values():
        copy.wait()
    drain_gather = gather_features(p, r, lambda: pl.semaphore_wait(barrier, ROWS + 9))
    drain_forward = forward_sum(p, r, r.agg)
    node_update(r, outputs.hid, outputs.ht)
    outputs.invo[...] = r.inv[...]
    drain_spread = spread_gradients(
        p, r, outputs.ht, outputs.parts, outputs.gwo, (drain_gather, drain_forward)
    )
    drain_spread()


def layer_call(*args):
    return pl.pallas_call(
        layer_kernel,
        name="layer",
        out_shape=(
            shape(2 * T, 2 * T),
            shape(2, T, T),
            shape(8, T),
            shape(TILE_ROWS, TPR, T, T),
            shape(T, 2 * T),
        ),
        in_specs=[HBM] * 9,
        out_specs=(VMEM,) * 5,
        scratch_shapes=[
            (pltpu.SMEM if name == "cols" else pltpu.VMEM)(dims, dtype)
            for name, (dims, dtype) in BUFFERS.items()
        ]
        + sem_pairs(LINKS.values())
        + [pltpu.SemaphoreType.DMA((len(LOADS),))],
        compiler_params=pltpu.CompilerParams(
            collective_id=1, has_side_effects=True, vmem_limit_bytes=32 * MB
        ),
    )(*[in_hbm(arg) for arg in args])


def place_kernel(
    cols_hbm, parts_ref, hid_ref, gw_ref, out_ref, hid_out, gw_out, cols_ref, sems
):
    copy = pltpu.make_async_copy(cols_hbm, cols_ref, sems.at[0])
    hid_copy = pltpu.make_async_copy(hid_ref, hid_out, sems.at[1])
    gw_copy = pltpu.make_async_copy(gw_ref, gw_out, sems.at[2])
    copy.start()
    hid_copy.start()
    gw_copy.start()
    out_ref[...] = jnp.zeros_like(out_ref)
    copy.wait()

    def tile_row(t, carry):
        for k in range(TPR):
            out_ref[cols_ref[k, t]] += parts_ref[t, k]
        return carry

    lax.fori_loop(0, TILE_ROWS, tile_row, 0, unroll=2)
    hid_copy.wait()
    gw_copy.wait()


def place_call(cols, parts, hidden, grad_weight):
    return pl.pallas_call(
        place_kernel,
        name="place_tiles",
        out_shape=(
            shape(SRC_TILES, T, T),
            pltpu.HBM((2 * T, 2 * T), F32),
            pltpu.HBM((T, 2 * T), F32),
        ),
        in_specs=[HBM] + [VMEM] * 3,
        out_specs=(VMEM, HBM, HBM),
        scratch_shapes=[pltpu.SMEM((TPR, TILE_ROWS), I32), pltpu.SemaphoreType.DMA((3,))],
        compiler_params=pltpu.CompilerParams(vmem_limit_bytes=4 * MB),
    )(in_hbm(cols), parts, hidden, grad_weight)


def sum_row_kernel(*refs):
    q_ref, ht_ref, inv_ref, gf_ref = refs[:4]
    r = named(("xfar", "xacc", "xnear", "tot", "zin"), refs[4:], ("fsem", "nsem", "zsem"))
    p = Place()
    zh, x = p.zh, p.x
    right_dev, left_dev = p.in_row(zh, rem(x + 1, 4)), p.in_row(zh, rem(x + 3, 4))
    pair_dev = p.in_row(1 - zh, x)
    barrier = pltpu.get_barrier_semaphore()
    for dev in (right_dev, left_dev, pair_dev):
        signal(barrier, dev)
    pl.semaphore_wait(barrier, 3)
    base = ((1 - zh) * 4, zh * 4)

    def block(k, d):
        return base[k] + rem(x + d, 4)

    def far_copy(k, way):
        return link(
            q_ref.at[block(k, 2), way],
            r.xfar.at[k, way],
            r.fsem,
            (k, way),
            left_dev if way else right_dev,
        )

    def near_copy(k, way, h):
        src = r.xacc.at[k, way] if way == h else q_ref.at[block(k, 1 + 2 * way), h]
        return link(
            src, r.xnear.at[k, way, h], r.nsem, (k, way, h), left_dev if way else right_dev
        )

    def pair_copy(h):
        return link(r.tot.at[0, h], r.zin.at[h], r.zsem, h, pair_dev)

    def first(k):
        for way in range(2):
            far_copy(k, way).start()
        for way in range(2):
            near_copy(k, way, 1 - way).start()

    def second(k):
        for way, dev in ((0, left_dev), (1, right_dev)):
            arrival(r.xfar.at[k, way], r.fsem, (k, way), dev)
            r.xacc[k, way] = q_ref[block(k, 1 + 2 * way), way] + r.xfar[k, way]
            near_copy(k, way, way).start()

    def total(k, h):
        for way, dev in ((0, left_dev), (1, right_dev)):
            arrival(r.xnear.at[k, way, h], r.nsem, (k, way, h), dev)
        r.tot[k, h] = q_ref[block(k, 0), h] + (r.xnear[k, 0, h] + r.xnear[k, 1, h])

    first(0)
    second(0)
    first(1)
    for h in range(2):
        total(0, h)
        pair_copy(h).start()
    second(1)
    for h in range(2):
        total(1, h)
    for h in range(2):
        arrival(r.zin.at[h], r.zsem, h, pair_dev)
        back = (r.tot[1, h] + r.zin[h]) + ht_ref[h]
        gf_ref[h * T : (h + 1) * T, :] = jnp.transpose(
            back * jnp.broadcast_to(inv_ref[h : h + 1, :], (T, T))
        )
    for h in range(2):
        pair_copy(h).wait_send()
        for k in range(2):
            far_copy(k, h).wait_send()
            for way in range(2):
                near_copy(k, way, h).wait_send()


def sum_row_call(parts, ht, inv):
    return pl.pallas_call(
        sum_row_kernel,
        name="sum_over_row",
        out_shape=shape(2 * T, T),
        in_specs=[VMEM] * 3,
        out_specs=VMEM,
        scratch_shapes=[
            pltpu.VMEM((2, 2, T, T), F32),
            pltpu.VMEM((2, 2, T, T), F32),
            pltpu.VMEM((2, 2, 2, T, T), F32),
            pltpu.VMEM((2, 2, T, T), F32),
            pltpu.VMEM((2, T, T), F32),
        ]
        + sem_pairs(((2, 2), (2, 2, 2), (2,))),
        compiler_params=pltpu.CompilerParams(
            collective_id=2, has_side_effects=True, vmem_limit_bytes=6 * MB
        ),
    )(parts.reshape(ROWS, 2, T, T), ht, inv)


def shards(features, weight, bias, cot, drop, tile_cols, counts, pos, keep):
    cols = jnp.transpose(tile_cols[0, 0])
    hidden, ht, inv, parts, grad_weight = layer_call(
        cols,
        features,
        jnp.transpose(counts[0, 0]),
        pos[0, 0],
        keep[0, 0],
        weight,
        bias.reshape(1, 2 * T),
        cot,
        drop,
    )
    back, hidden, grad_weight = place_call(cols, parts, hidden, grad_weight)
    grad_features = sum_row_call(back, ht, inv)
    return hidden, grad_features, grad_weight


def solution(mesh):
    nodes = P(("row", "col"), None)
    block = P("row", "col", None, None)
    return jax.shard_map(
        shards,
        mesh=mesh,
        in_specs=(nodes, P(), P(), nodes, nodes, block, block, block, block),
        out_specs=(nodes, nodes, P()),
        check_vma=False,
    )
```

```python
from types import SimpleNamespace

import jax
import jax.numpy as jnp
from jax import lax
from jax.experimental import pallas as pl
from jax.experimental.pallas import tpu as pltpu
from jax.sharding import PartitionSpec as P

MESH = pl.DeviceIdType.MESH
HIGHEST = lax.Precision.HIGHEST
F32, BF16, I32 = jnp.float32, jnp.bfloat16, jnp.int32

T = 128
ROWS, COLS = 8, 32
TILE_ROWS, TPR, EPT = 64, 4, 64
SLOTS = TPR * EPT
SRC_TILES = 16
MB = 1 << 20
VMEM = pl.BlockSpec(memory_space=pltpu.VMEM)
HBM = pl.BlockSpec(memory_space=pltpu.HBM)
NT = (((1,), (1,)), ((), ()))


def in_hbm(array):
    return pltpu.with_memory_space_constraint(array, pltpu.HBM)


def rem(a, n):
    return lax.rem(a, jnp.int32(n))


def div(a, n):
    return lax.div(a, jnp.int32(n))


def shape(*dims, dtype=F32):
    return jax.ShapeDtypeStruct(dims, dtype)


def link_from(src, dst, sems, sent, received, dev):
    return pltpu.make_async_remote_copy(
        src_ref=src,
        dst_ref=dst,
        send_sem=sems.send.at[sent],
        recv_sem=sems.recv.at[received],
        device_id=dev,
        device_id_type=MESH,
    )


def link(src, dst, sems, where, dev):
    return link_from(src, dst, sems, where, where, dev)


def arrival(ref, sems, where, dev):
    link(ref, ref, sems, where, dev).wait_recv()


def signal(barrier, dev):
    pl.semaphore_signal(barrier, inc=1, device_id=dev, device_id_type=MESH)


def named(names, refs, pairs=()):
    out = SimpleNamespace(**dict(zip(names, refs)))
    rest = refs[len(names) :]
    for i, name in enumerate(pairs):
        setattr(out, name, SimpleNamespace(send=rest[2 * i], recv=rest[2 * i + 1]))
    return out


def sem_pairs(dims):
    return [pltpu.SemaphoreType.DMA(d) for d in dims for _ in range(2)]


def each(low, high, body):
    def run(o, carry):
        body(o)
        return carry

    lax.fori_loop(low, high, run, 0)


def slot_codes(counts, pos, keep):
    lane = lax.broadcasted_iota(I32, (TILE_ROWS, SLOTS), 1)
    counts = jnp.transpose(counts)
    limit = jnp.broadcast_to(counts[:, 0:1], (TILE_ROWS, SLOTS))
    for k in range(1, TPR):
        limit = jnp.where(
            lane >= k * EPT, jnp.broadcast_to(counts[:, k : k + 1], (TILE_ROWS, SLOTS)), limit
        )
    live = ((lane & (EPT - 1)) < limit) & (keep == 1)
    return jnp.where(live, pos >> 7, 4 * T)


def split(values, axis):
    high = values.astype(BF16)
    low = (values - high.astype(F32)).astype(BF16)
    return jnp.concatenate([high, low], axis=axis)


def hot_dst(code_row, side):
    return jnp.where(side == jnp.broadcast_to(code_row, (T, SLOTS)), 1.0, 0.0).astype(BF16)


def hot_src(pos_row, side, lane):
    code = (pos_row & (T - 1)) + ((lane >> 6) & 1) * T
    return jnp.where(side == jnp.broadcast_to(code, (2 * T, SLOTS)), 1.0, 0.0).astype(BF16)


def gelu_pair(values):
    half = 0.5 * (1.0 + lax.erf(values * 0.7071067811865476))
    slope = half + values * jnp.exp(-0.5 * values * values) * 0.3989422804014327
    return values * half, slope


def far_first(zl, k):
    near = jnp.where(zl >= 2, 3 - zl, zl)
    inner = jnp.where(k == 0, 3, jnp.where(k == 1, 0, 4 - k))
    plane = jnp.where(near == 0, 3 - k, inner)
    return jnp.where(zl >= 2, 3 - plane, plane)


def chosen(g, values):
    out = jnp.int32(values[0])
    for i in range(1, len(values)):
        out = jnp.where(g == i, values[i], out)
    return out


class Place:
    def __init__(self):
        self.row, self.col = lax.axis_index("row"), lax.axis_index("col")
        self.zh, self.x = div(self.row, 4), rem(self.row, 4)
        self.zl, self.y, self.c = div(self.col, 8), rem(div(self.col, 2), 4), rem(self.col, 2)

    def in_row(self, zh, x):
        return (zh * 4 + x, self.col)

    def in_col(self, zl, y, c):
        return (self.row, (zl * 4 + y) * 2 + c)


def gather_features(p, r, barrier_wait):
    row, col, zh, x = p.row, p.col, p.zh, p.x
    pair = 1 - zh
    right, left = rem(x + 1, 4), rem(x + 3, 4)
    right_dev, left_dev, pair_dev = p.in_row(zh, right), p.in_row(zh, left), p.in_row(pair, x)
    across_dev = p.in_row(zh, rem(x + 2, 4))
    for h in range(2):
        r.xg[row, h] = jnp.transpose(r.x[h * T : (h + 1) * T, :])
    r.code[...] = slot_codes(r.counts[...], r.pos[...], r.keep[...])
    def near_copy(k, zz, way, h):
        slot = r.xg.at[zz * 4 + x, h]
        return link(slot, slot, r.xnear, (k, way, h), left_dev if way else right_dev)

    def near_wait(k, zz, way, h):
        slot = r.xg.at[zz * 4 + (right if way else left), h]
        arrival(slot, r.xnear, (k, way, h), right_dev if way else left_dev)

    def far_copy(h):
        slot = r.xg.at[zh * 4 + (right if h else left), h]
        return link(slot, slot, r.xfar, (0, h), left_dev if h else right_dev)

    def across_copy(h):
        slot = r.xg.at[pair * 4 + x, h]
        return link(slot, slot, r.xfar, (1, h), across_dev)

    def pair_copy(h):
        return link(r.xg.at[row, h], r.xg.at[row, h], r.xpair, h, pair_dev)

    ones = jnp.ones((8, SLOTS), BF16)
    side = lax.broadcasted_iota(I32, (T, SLOTS), 0)
    wide = lax.broadcasted_iota(I32, (2 * T, SLOTS), 0)
    lane = lax.broadcasted_iota(I32, (1, SLOTS), 1)
    sub = lax.broadcasted_iota(I32, (8, T), 0)

    zl, member = p.zl, rem(col, 8)

    def count(m, carry):
        tile = jnp.zeros((8, T), F32)
        for i in range(8):
            t = 2 * ((i // 2) * 8 + m) + i % 2
            hot = hot_dst(r.code[pl.ds(t, 1), :], side)
            row_sums = lax.dot_general(ones, hot, NT, preferred_element_type=F32)
            tile = jnp.where(sub == i, row_sums, tile)
        r.deg[m] = tile
        return carry

    lax.fori_loop(0, 8, count, 0)
    barrier_wait()
    for h in range(2):
        pair_copy(h).start()
    for way, h in ((0, 0), (1, 1), (0, 1), (1, 0)):
        near_copy(0, zh, way, h).start()


    def member_copy(o):
        peer = rem(member + o, 8)
        return link(r.deg.at[peer], r.degin.at[o], r.dsem, o, (row, zl * 8 + peer))

    def member_wait(o):
        peer = rem(member + 8 - o, 8)
        arrival(r.degin.at[o], r.dsem, o, (row, zl * 8 + peer))

    def plane_copy(o):
        dev = (row, rem(zl + o, 4) * 8 + member)
        return link(r.degsum, r.degz.at[o], r.esem, o, dev)

    def plane_wait(o):
        arrival(r.degz.at[o], r.esem, o, (row, rem(zl + 4 - o, 4) * 8 + member))

    for o in range(1, 8):
        member_copy(o).start()

    def block(i, carry):
        for u in range(4):
            t = 4 * i + u
            dst = hot_dst(r.code[pl.ds(t, 1), :], side)
            src = hot_src(r.pos[pl.ds(t, 1), :], wide, lane)
            for q in range(2):
                part = slice(q * T, (q + 1) * T)
                r.adj[t, :, q * 2 * T : (q + 1) * 2 * T] = lax.dot_general(
                    dst[:, part], src[:, part], NT, preferred_element_type=F32
                ).astype(BF16)
        return carry

    def pass_on(h):
        arrival(r.xg.at[pair * 4 + x, h], r.xpair, h, pair_dev)
        across_copy(h).start()
        near_copy(1, pair, 0, h).start()
        near_copy(1, pair, 1, h).start()

    lax.fori_loop(0, 3, block, 0)
    total = r.deg[member]
    for o in range(1, 8):
        member_wait(o)
        total = total + r.degin[o]
    r.degsum[...] = total
    for o in range(1, 4):
        plane_copy(o).start()
    for h in range(2):
        near_wait(0, zh, h, h)
        far_copy(h).start()
    pass_on(0)
    mine = pl.ds(2 * zl, 2)
    total = r.degsum[mine, :]
    for o in range(1, 4):
        plane_wait(o)
        total = total + r.degz[o, mine, :]
    r.inv[...] = jnp.ones((8, T), F32)
    r.inv[0:2, :] = lax.rsqrt(1.0 + total)
    r.invg[row] = r.inv[...]

    def inv_copy(o):
        return link(r.inv, r.invg.at[row], r.vsem, o, (rem(row + o, ROWS), col))

    each(1, ROWS, lambda o: inv_copy(o).start())
    pass_on(1)
    lax.fori_loop(3, 16, block, 0)

    def inv_wait(o):
        peer = rem(row + ROWS - o, ROWS)
        arrival(r.invg.at[peer], r.vsem, o, (peer, col))

    each(1, ROWS, inv_wait)
    for h in range(2):
        near_wait(0, zh, 1 - h, h)
        slot = r.xg.at[zh * 4 + rem(x + 2, 4), h]
        arrival(slot, r.xfar, (0, h), right_dev if h else left_dev)
        near_wait(1, pair, 0, h)
        near_wait(1, pair, 1, h)
        arrival(r.xg.at[pair * 4 + rem(x + 2, 4), h], r.xfar, (1, h), across_dev)

    def drain():
        for h in range(2):
            pair_copy(h).wait_send()
            far_copy(h).wait_send()
            across_copy(h).wait_send()
            for k, zz in ((0, zh), (1, pair)):
                for way in range(2):
                    near_copy(k, zz, way, h).wait_send()
        each(1, ROWS, lambda o: inv_copy(o).wait_send())
        for o in range(1, 8):
            member_copy(o).wait_send()
        for o in range(1, 4):
            plane_copy(o).wait_send()

    return drain


SUM_ORDER = (
    (0, 0), (1, 0), (2, 0), (3, 0), (0, 1), (0, 2), (0, 3), (1, 1),
    (1, 2), (1, 3), (2, 1), (2, 2), (2, 3), (3, 1), (3, 2), (3, 3),
)
SUM_LAG = 2


def forward_sum(p, r, out_ref):
    row, zl, y, c = p.row, p.zl, p.y, p.c
    core_dev = p.in_col(zl, y, 1 - c)
    right_dev, left_dev = p.in_col(zl, rem(y + 1, 4), c), p.in_col(zl, rem(y + 3, 4), c)
    for u in range(SRC_TILES):
        i, h = u // 2, u % 2
        r.scaled[u] = split(
            r.xg[i, h] * jnp.broadcast_to(r.invg[i, h : h + 1, :], (T, T)), axis=0
        )
    q = r.q

    def tile_row(t):
        panel = jnp.concatenate([r.scaled[r.cols[k, t]] for k in range(TPR)], axis=1)
        both = lax.dot_general(panel, r.adj[t], NT, preferred_element_type=F32)
        return both[:T] + both[T:]

    def core_copy(g):
        return link(r.pbuf.at[g], r.cbuf.at[g], r.fcore, g, core_dev)

    def far_copy(k, way):
        return link(
            q.at[4 * k, way],
            r.yfar.at[k, way],
            r.ffar,
            (k, way),
            left_dev if way else right_dev,
        )

    def near_copy(k, way, h):
        src = r.yacc.at[k, way] if way == h else q.at[4 * k + 1 + way, h]
        return link(
            src, r.ynear.at[k, way, h], r.fnear, (k, way, h), left_dev if way else right_dev
        )

    inner = (zl == 1) | (zl == 2)
    inner_plane = jnp.where(zl <= 1, 1, 2)

    def plane_copy(k, h):
        slot = r.zin.at[zl, h]
        dev = p.in_col(far_first(zl, k), y, c)
        return link_from(r.tot.at[k, h], slot, r.fplane, (k, h), (zl, h), dev)

    def joint_copy(h):
        dev = p.in_col(far_first(zl, 0), y, c)
        return link_from(r.zout.at[h], r.zin.at[zl, h], r.fplane, (0, h), (zl, h), dev)

    def end_copy(h):
        return link(r.tot.at[0, h], r.zmid.at[h], r.fend, h, p.in_col(inner_plane, y, c))

    def finish(k, j):
        g = 4 * k + j
        core_copy(g).wait_recv()
        q[g] = q[g] + r.cbuf[g]

        @pl.when(j == 0)
        def _():
            far_copy(k, 0).start()
            far_copy(k, 1).start()

    def accumulate(k):
        for way, dev in ((0, left_dev), (1, right_dev)):
            arrival(r.yfar.at[k, way], r.ffar, (k, way), dev)
            r.yacc[k, way] = q[4 * k + 1 + way, way] + r.yfar[k, way]
            near_copy(k, way, way).start()
        for way in range(2):
            near_copy(k, way, 1 - way).start()

    def plane_sum(k, h):
        arrival(r.ynear.at[k, 0, h], r.fnear, (k, 0, h), left_dev)
        arrival(r.ynear.at[k, 1, h], r.fnear, (k, 1, h), right_dev)
        return q[4 * k + 3, h] + (r.ynear[k, 0, h] + r.ynear[k, 1, h])

    def place_in(i):
        return chosen(i, [b[0] for b in SUM_ORDER]), chosen(i, [b[1] for b in SUM_ORDER])

    def step(i, carry):
        k, j = place_in(i)
        g = 4 * k + j
        d = chosen(j, (2, 1, 3, 0))
        first = (far_first(zl, k) * 4 + rem(y + d, 4)) * 4
        for h in range(2):
            r.pbuf[g, h] = tile_row(first + 2 * (1 - c) + h)
        for h in range(2):
            q[g, h] = tile_row(first + 2 * c + h)
        core_copy(g).start()
        ready_k, ready_j = place_in(i - SUM_LAG)

        @pl.when(i >= SUM_LAG)
        def _():
            finish(ready_k, ready_j)

        @pl.when((i >= SUM_LAG) & (ready_j == 3))
        def _():
            accumulate(ready_k)

        return carry

    lax.fori_loop(0, 16, step, 0)

    def rest(i):
        k, j = place_in(i)
        finish(k, j)

    each(16 - SUM_LAG, 16, rest)
    accumulate(jnp.int32(3))
    for k in range(3):
        for h in range(2):
            r.tot[k, h] = plane_sum(k, h)
            if k > 0:
                plane_copy(k, h).start()
            else:

                @pl.when(jnp.logical_not(inner))
                def _():
                    end_copy(h).start()

        if k == 1:

            @pl.when(inner)
            def _():
                for h in range(2):
                    arrival(r.zmid.at[h], r.fend, h, core_dev)
                    r.zout[h] = r.tot[0, h] + r.zmid[h]
                    joint_copy(h).start()

    for h in range(2):
        out_ref[h] = plane_sum(3, h)
        for s in range(4):

            @pl.when((zl != s) & (zl + s != 3) | ((zl == 1) & (s == 2)) | ((zl == 2) & (s == 1)))
            def _():
                arrival(r.zin.at[s, h], r.fplane, (s, h), core_dev)
                out_ref[h] = out_ref[h] + r.zin[s, h]

    def drain_plane(k):
        for way in range(2):
            far_copy(k, way).wait_send()
            for h in range(2):
                near_copy(k, way, h).wait_send()
        for j in range(4):
            core_copy(4 * k + j).wait_send()

    def drain():
        each(0, 4, drain_plane)
        for h in range(2):
            for k in (1, 2):
                plane_copy(k, h).wait_send()

            @pl.when(inner)
            def _():
                joint_copy(h).wait_send()

            @pl.when(jnp.logical_not(inner))
            def _():
                end_copy(h).wait_send()

    return drain


def node_update(r, hid_ref, ht_ref):
    weight = r.w[...]
    bias = jnp.broadcast_to(r.b[...], (T, 2 * T))
    for h in range(2):
        part = slice(h * T, (h + 1) * T)
        inv_row = jnp.broadcast_to(r.inv[h : h + 1, :], (T, T))
        inv_col = jnp.transpose(inv_row)
        inv_col = jnp.concatenate([inv_col, inv_col], axis=1)
        agg = r.agg[h] + jnp.transpose(r.x[part, :]) * inv_row
        mixed = jnp.dot(
            jnp.transpose(agg), weight, precision=HIGHEST, preferred_element_type=F32
        )
        gelu, slope = gelu_pair(inv_col * mixed + bias)
        drop = r.drop[part, :].astype(F32) / 0.9
        hid_ref[part, :] = gelu * drop
        grad = inv_col * (r.cot[part, :] * drop * slope)
        ht_ref[h] = lax.dot_general(weight, grad, NT, precision=HIGHEST, preferred_element_type=F32)
        r.agg[h] = agg
        r.grad[h] = grad


def weight_update(r):
    total = jnp.zeros((T, 2 * T), F32)
    for h in range(2):
        total = total + jnp.dot(
            r.agg[h], r.grad[h], precision=HIGHEST, preferred_element_type=F32
        )
    for k in range(2):
        r.gw[k * 4 : (k + 1) * 4] = total[:, k * T : (k + 1) * T].reshape(4, 4, 8, T)


BLOCK_ORDER = (
    (0, 0), (0, 1), (0, 3), (1, 0), (0, 2), (2, 0), (1, 1), (1, 3),
    (3, 0), (1, 2), (2, 1), (2, 3), (2, 2), (3, 1), (3, 3), (3, 2),
)


def spread_gradients(p, r, ht_ref, parts_ref, gwo_ref, drains):
    row, col, zl, y, c = p.row, p.col, p.zl, p.y, p.c
    right, left, across = rem(y + 1, 4), rem(y + 3, 4), rem(y + 2, 4)
    core_dev = p.in_col(zl, y, 1 - c)
    right_dev, left_dev = p.in_col(zl, right, c), p.in_col(zl, left, c)
    up_dev = p.in_col(jnp.minimum(zl + 1, 3), y, c)
    down_dev = p.in_col(jnp.maximum(zl - 1, 0), y, c)
    r.g[zl, y, c] = ht_ref[...]

    def plane(k):
        return far_first(zl, 3 - k)

    def z_copy(z, up, h):
        slot = r.g.at[z, y, c, h]
        return link(slot, slot, r.gchain, (z, 0 if up else 1, h), up_dev if up else down_dev)

    end = (zl == 0) | (zl == 3)

    def end_copy(h):
        slot = r.g.at[zl, y, c, h]
        low = jnp.where(zl == 0, 1, 0)
        return link_from(
            slot, slot, r.gchain, (zl, low, h), (zl, 1 - low, h), p.in_col(3 - zl, y, c)
        )

    def near_copy(k, way, h):
        slot = r.g.at[plane(k), y, c, h]
        return link(slot, slot, r.gnear, (k, way, h), left_dev if way else right_dev)

    def far_copy(k, h):
        slot = r.g.at[plane(k), right if h else left, c, h]
        return link(slot, slot, r.gfar, (k, h), left_dev if h else right_dev)

    def core_copy(k, d):
        slot = r.g.at[plane(k), rem(y + d, 4), c]
        return link(slot, slot, r.gcore, (k, d), core_dev)

    def core_wait(k, d):
        arrival(r.g.at[plane(k), rem(y + d, 4), 1 - c], r.gcore, (k, d), core_dev)

    def near_wait(k, way, h):
        slot = r.g.at[plane(k), right if way else left, c, h]
        arrival(slot, r.gnear, (k, way, h), right_dev if way else left_dev)

    def z_arrive(k):
        z = plane(k)
        below = z < zl
        way = jnp.where(below, 0, 1)
        for h in range(2):
            arrival(r.g.at[z, y, c, h], r.gchain, (z, way, h), core_dev)

            @pl.when((zl - z == 1) & (zl < 3))
            def _():
                z_copy(z, True, h).start()

            @pl.when((z - zl == 1) & (zl > 0))
            def _():
                z_copy(z, False, h).start()

            near_copy(k, h, h).start()
        near_copy(k, 0, 1).start()
        near_copy(k, 1, 0).start()
        core_copy(k, 0).start()

    def y_arrive(k):
        near_wait(k, 0, 0)
        far_copy(k, 0).start()
        near_wait(k, 1, 1)
        far_copy(k, 1).start()
        near_wait(k, 0, 1)
        core_copy(k, 3).start()
        near_wait(k, 1, 0)
        core_copy(k, 1).start()

    def y_far(k):
        for h in range(2):
            arrival(
                r.g.at[plane(k), across, c, h], r.gfar, (k, h), right_dev if h else left_dev
            )
        core_copy(k, 2).start()

    def tile_row(k, d, cc, h):
        z, yy = plane(k), rem(y + d, 4)
        t = ((z * 4 + yy) * 2 + cc) * 2 + h
        adj = r.adj[t]
        back = jnp.dot(
            split(r.g[z, yy, cc, h], axis=1),
            jnp.concatenate([adj, adj], axis=0),
            preferred_element_type=F32,
        )
        for i in range(TPR):
            parts_ref[t, i] = back[:, i * T : (i + 1) * T]

    def use(g):
        return chosen(g, [b[0] for b in BLOCK_ORDER]), chosen(g, [b[1] for b in BLOCK_ORDER])

    zero = jnp.int32(0)
    for h in range(2):

        @pl.when(zl < 3)
        def _():
            z_copy(zl, True, h).start()

        @pl.when(zl > 0)
        def _():
            z_copy(zl, False, h).start()

        @pl.when(end)
        def _():
            end_copy(h).start()

        near_copy(zero, h, h).start()
    near_copy(zero, 0, 1).start()
    near_copy(zero, 1, 0).start()
    core_copy(zero, 0).start()

    member = rem(col, 8)

    def member_dev(o):
        return (row, zl * 8 + rem(member + o, 8))

    def plane_dev(o):
        return (row, rem(zl + o, 4) * 8 + member)

    def scatter_copy(o):
        return link(r.gw.at[rem(member + o, 8)], r.gin.at[o], r.gsem, o, member_dev(o))

    def reduce_copy(o):
        return link(r.gsum.at[rem(zl + o, 4)], r.gz.at[o], r.hsem, o, plane_dev(o))

    def share_copy(o):
        return link(r.mine, r.rin.at[row], r.wsem, o, (rem(row + o, ROWS), col))

    def plane_return(o):
        slot = r.full.at[member, zl]
        return link(slot, slot, r.isem, o, plane_dev(o))

    def member_return(o):
        slot = r.full.at[member]
        return link(slot, slot, r.bsem, o, member_dev(o))

    weight_update(r)
    for o in range(1, 8):
        scatter_copy(o).start()
    for drain_before in drains:
        drain_before()

    def reduce_members():
        total = r.gw[member]
        for o in range(1, 8):
            arrival(r.gin.at[o], r.gsem, o, member_dev(8 - o))
            total = total + r.gin[o]
        r.gsum[...] = total
        for o in range(1, 4):
            reduce_copy(o).start()

    def reduce_planes():
        total = r.gsum[zl]
        for o in range(1, 4):
            arrival(r.gz.at[o], r.hsem, o, plane_dev(4 - o))
            total = total + r.gz[o]
        r.mine[...] = total
        r.rin[row] = total
        each(1, ROWS, lambda o: share_copy(o).start())

    def reduce_row():
        def wait(o):
            peer = rem(row + ROWS - o, ROWS)
            arrival(r.rin.at[peer], r.wsem, o, (peer, col))

        each(1, ROWS, wait)
        total = r.rin[0]
        for i in range(1, ROWS):
            total = total + r.rin[i]
        r.full[member, zl] = total
        for o in range(1, 4):
            plane_return(o).start()

    def return_members():
        for o in range(1, 4):
            arrival(r.full.at[member, rem(zl + 4 - o, 4)], r.isem, o, plane_dev(4 - o))
        for o in range(1, 8):
            member_return(o).start()

    def drain_plane(k):
        z = plane(k)
        for d in range(4):
            core_copy(k, d).wait_send()
        for h in range(2):
            far_copy(k, h).wait_send()
            near_copy(k, 0, h).wait_send()
            near_copy(k, 1, h).wait_send()

            @pl.when(((z == zl) | (zl - z == 1)) & (zl < 3))
            def _():
                z_copy(z, True, h).wait_send()

            @pl.when(((z == zl) | (z - zl == 1)) & (zl > 0))
            def _():
                z_copy(z, False, h).wait_send()

            @pl.when((z == zl) & end)
            def _():
                end_copy(h).wait_send()

    def early_drain():
        each(0, 2, drain_plane)
        for o in range(1, 8):
            scatter_copy(o).wait_send()
        for o in range(1, 4):
            reduce_copy(o).wait_send()
        each(1, ROWS, lambda o: share_copy(o).wait_send())

    def events(g):
        for at, body in (
            (4, lambda: (y_far(zero), z_arrive(zero + 2))),
            (6, lambda: y_arrive(zero + 1)),
            (5, reduce_members),
            (7, reduce_planes),
            (8, lambda: z_arrive(zero + 3)),
            (9, lambda: (y_far(zero + 1), y_arrive(zero + 2))),
            (10, reduce_row),
            (12, lambda: (y_far(zero + 2), y_arrive(zero + 3))),
            (13, return_members),
            (14, early_drain),
            (15, lambda: y_far(zero + 3)),
        ):

            @pl.when(g == at)
            def _():
                body()

    def step(g, carry):
        events(g)
        k, d = use(g)
        kk, dd = use(g - 2)
        core_wait(kk, dd)
        for h in range(2):
            tile_row(k, d, c, h)
        for h in range(2):
            tile_row(kk, dd, 1 - c, h)
        return carry

    for h in range(2):
        tile_row(zero, zero, c, h)
    z_arrive(zero + 1)
    y_arrive(zero)
    for h in range(2):
        tile_row(zero, zero + 1, c, h)
    lax.fori_loop(2, 16, step, 0)

    def last(g):
        kk, dd = use(g)
        core_wait(kk, dd)
        for h in range(2):
            tile_row(kk, dd, 1 - c, h)

    each(14, 16, last)

    for o in range(1, 8):
        arrival(r.full.at[rem(member + 8 - o, 8)], r.bsem, o, member_dev(8 - o))
    for k in range(2):
        gwo_ref[:, k * T : (k + 1) * T] = r.full[k * 4 : (k + 1) * 4].reshape(T, T)

    def drain():
        each(2, 4, drain_plane)
        for o in range(1, 8):
            member_return(o).wait_send()
        for o in range(1, 4):
            plane_return(o).wait_send()

    return drain


SOURCES = ("cols", "x", "counts", "pos", "keep", "w", "b", "cot", "drop")
RESULTS = ("hid", "ht", "invo", "parts", "gwo")
BUFFERS = {
    "cols": ((TPR, TILE_ROWS), I32),
    "x": ((2 * T, T), F32),
    "counts": ((TPR, TILE_ROWS), I32),
    "pos": ((TILE_ROWS, SLOTS), I32),
    "keep": ((TILE_ROWS, SLOTS), I32),
    "w": ((T, 2 * T), F32),
    "b": ((1, 2 * T), F32),
    "cot": ((2 * T, 2 * T), F32),
    "drop": ((2 * T, 2 * T), I32),
    "code": ((TILE_ROWS, SLOTS), I32),
    "xg": ((ROWS, 2, T, T), F32),
    "deg": ((8, 8, T), F32),
    "degin": ((8, 8, T), F32),
    "degsum": ((8, T), F32),
    "degz": ((4, 8, T), F32),
    "inv": ((8, T), F32),
    "invg": ((ROWS, 8, T), F32),
    "adj": ((TILE_ROWS, T, TPR * T), BF16),
    "scaled": ((SRC_TILES, 2 * T, T), BF16),
    "pbuf": ((16, 2, T, T), F32),
    "cbuf": ((16, 2, T, T), F32),
    "q": ((16, 2, T, T), F32),
    "yfar": ((4, 2, T, T), F32),
    "yacc": ((4, 2, T, T), F32),
    "ynear": ((4, 2, 2, T, T), F32),
    "tot": ((4, 2, T, T), F32),
    "zin": ((4, 2, T, T), F32),
    "zmid": ((2, T, T), F32),
    "zout": ((2, T, T), F32),
    "agg": ((2, T, T), F32),
    "g": ((4, 4, 2, 2, T, T), F32),
    "grad": ((2, T, 2 * T), F32),
    "gw": ((8, 4, 8, T), F32),
    "gin": ((8, 4, 8, T), F32),
    "gsum": ((4, 8, T), F32),
    "gz": ((4, 8, T), F32),
    "rin": ((ROWS, 8, T), F32),
    "mine": ((8, T), F32),
    "full": ((8, 4, 8, T), F32),
}
LINKS = {
    "xpair": (2,),
    "xnear": (2, 2, 2),
    "xfar": (2, 2),
    "dsem": (8,),
    "esem": (4,),
    "vsem": (ROWS,),
    "fcore": (16,),
    "ffar": (4, 2),
    "fnear": (4, 2, 2),
    "fplane": (4, 2),
    "fend": (2,),
    "gchain": (4, 2, 2),
    "gnear": (4, 2, 2),
    "gfar": (4, 2),
    "gcore": (4, 4),
    "gsem": (8,),
    "hsem": (4,),
    "wsem": (ROWS,),
    "isem": (4,),
    "bsem": (8,),
}
LOADS = SOURCES


def layer_kernel(*refs):
    inputs = named(SOURCES, refs)
    outputs = named(RESULTS, refs[len(SOURCES) :])
    r = named(tuple(BUFFERS), refs[len(SOURCES) + len(RESULTS) : -1], tuple(LINKS))
    p = Place()
    loads = {
        name: pltpu.make_async_copy(getattr(inputs, name), getattr(r, name), refs[-1].at[i])
        for i, name in enumerate(LOADS)
    }
    for copy in loads.values():
        copy.start()
    barrier = pltpu.get_barrier_semaphore()
    for o in range(1, ROWS):
        signal(barrier, (rem(p.row + o, ROWS), p.col))
    for o in range(1, 8):
        signal(barrier, (p.row, p.zl * 8 + rem(rem(p.col, 8) + o, 8)))
    for o in range(1, 4):
        signal(barrier, (p.row, rem(p.zl + o, 4) * 8 + rem(p.col, 8)))
    for copy in loads.values():
        copy.wait()
    drain_gather = gather_features(p, r, lambda: pl.semaphore_wait(barrier, ROWS + 9))
    drain_forward = forward_sum(p, r, r.agg)
    node_update(r, outputs.hid, outputs.ht)
    outputs.invo[...] = r.inv[...]
    drain_spread = spread_gradients(
        p, r, outputs.ht, outputs.parts, outputs.gwo, (drain_gather, drain_forward)
    )
    drain_spread()


def layer_call(*args):
    return pl.pallas_call(
        layer_kernel,
        name="layer",
        out_shape=(
            shape(2 * T, 2 * T),
            shape(2, T, T),
            shape(8, T),
            shape(TILE_ROWS, TPR, T, T),
            shape(T, 2 * T),
        ),
        in_specs=[HBM] * 9,
        out_specs=(VMEM,) * 5,
        scratch_shapes=[
            (pltpu.SMEM if name == "cols" else pltpu.VMEM)(dims, dtype)
            for name, (dims, dtype) in BUFFERS.items()
        ]
        + sem_pairs(LINKS.values())
        + [pltpu.SemaphoreType.DMA((len(LOADS),))],
        compiler_params=pltpu.CompilerParams(
            collective_id=1, has_side_effects=True, vmem_limit_bytes=32 * MB
        ),
    )(*[in_hbm(arg) for arg in args])


def place_kernel(
    cols_hbm, parts_ref, hid_ref, gw_ref, out_ref, hid_out, gw_out, cols_ref, sems
):
    copy = pltpu.make_async_copy(cols_hbm, cols_ref, sems.at[0])
    hid_copy = pltpu.make_async_copy(hid_ref, hid_out, sems.at[1])
    gw_copy = pltpu.make_async_copy(gw_ref, gw_out, sems.at[2])
    copy.start()
    hid_copy.start()
    gw_copy.start()
    out_ref[...] = jnp.zeros_like(out_ref)
    copy.wait()

    def tile_row(t, carry):
        for k in range(TPR):
            out_ref[cols_ref[k, t]] += parts_ref[t, k]
        return carry

    lax.fori_loop(0, TILE_ROWS, tile_row, 0, unroll=2)
    hid_copy.wait()
    gw_copy.wait()


def place_call(cols, parts, hidden, grad_weight):
    return pl.pallas_call(
        place_kernel,
        name="place_tiles",
        out_shape=(
            shape(SRC_TILES, T, T),
            pltpu.HBM((2 * T, 2 * T), F32),
            pltpu.HBM((T, 2 * T), F32),
        ),
        in_specs=[HBM] + [VMEM] * 3,
        out_specs=(VMEM, HBM, HBM),
        scratch_shapes=[pltpu.SMEM((TPR, TILE_ROWS), I32), pltpu.SemaphoreType.DMA((3,))],
        compiler_params=pltpu.CompilerParams(vmem_limit_bytes=4 * MB),
    )(in_hbm(cols), parts, hidden, grad_weight)


def sum_row_kernel(*refs):
    q_ref, ht_ref, inv_ref, gf_ref = refs[:4]
    r = named(("xfar", "xacc", "xnear", "tot", "zin"), refs[4:], ("fsem", "nsem", "zsem"))
    p = Place()
    zh, x = p.zh, p.x
    right_dev, left_dev = p.in_row(zh, rem(x + 1, 4)), p.in_row(zh, rem(x + 3, 4))
    pair_dev = p.in_row(1 - zh, x)
    barrier = pltpu.get_barrier_semaphore()
    for dev in (right_dev, left_dev, pair_dev):
        signal(barrier, dev)
    pl.semaphore_wait(barrier, 3)
    base = ((1 - zh) * 4, zh * 4)

    def block(k, d):
        return base[k] + rem(x + d, 4)

    def far_copy(k, way):
        return link(
            q_ref.at[block(k, 2), way],
            r.xfar.at[k, way],
            r.fsem,
            (k, way),
            left_dev if way else right_dev,
        )

    def near_copy(k, way, h):
        src = r.xacc.at[k, way] if way == h else q_ref.at[block(k, 1 + 2 * way), h]
        return link(
            src, r.xnear.at[k, way, h], r.nsem, (k, way, h), left_dev if way else right_dev
        )

    def pair_copy(h):
        return link(r.tot.at[0, h], r.zin.at[h], r.zsem, h, pair_dev)

    def first(k):
        for way in range(2):
            far_copy(k, way).start()
        for way in range(2):
            near_copy(k, way, 1 - way).start()

    def second(k):
        for way, dev in ((0, left_dev), (1, right_dev)):
            arrival(r.xfar.at[k, way], r.fsem, (k, way), dev)
            r.xacc[k, way] = q_ref[block(k, 1 + 2 * way), way] + r.xfar[k, way]
            near_copy(k, way, way).start()

    def total(k, h):
        for way, dev in ((0, left_dev), (1, right_dev)):
            arrival(r.xnear.at[k, way, h], r.nsem, (k, way, h), dev)
        r.tot[k, h] = q_ref[block(k, 0), h] + (r.xnear[k, 0, h] + r.xnear[k, 1, h])

    first(0)
    second(0)
    first(1)
    for h in range(2):
        total(0, h)
        pair_copy(h).start()
    second(1)
    for h in range(2):
        total(1, h)
    for h in range(2):
        arrival(r.zin.at[h], r.zsem, h, pair_dev)
        back = (r.tot[1, h] + r.zin[h]) + ht_ref[h]
        gf_ref[h * T : (h + 1) * T, :] = jnp.transpose(
            back * jnp.broadcast_to(inv_ref[h : h + 1, :], (T, T))
        )
    for h in range(2):
        pair_copy(h).wait_send()
        for k in range(2):
            far_copy(k, h).wait_send()
            for way in range(2):
                near_copy(k, way, h).wait_send()


def sum_row_call(parts, ht, inv):
    return pl.pallas_call(
        sum_row_kernel,
        name="sum_over_row",
        out_shape=shape(2 * T, T),
        in_specs=[VMEM] * 3,
        out_specs=VMEM,
        scratch_shapes=[
            pltpu.VMEM((2, 2, T, T), F32),
            pltpu.VMEM((2, 2, T, T), F32),
            pltpu.VMEM((2, 2, 2, T, T), F32),
            pltpu.VMEM((2, 2, T, T), F32),
            pltpu.VMEM((2, T, T), F32),
        ]
        + sem_pairs(((2, 2), (2, 2, 2), (2,))),
        compiler_params=pltpu.CompilerParams(
            collective_id=2, has_side_effects=True, vmem_limit_bytes=6 * MB
        ),
    )(parts.reshape(ROWS, 2, T, T), ht, inv)


def shards(features, weight, bias, cot, drop, tile_cols, counts, pos, keep):
    cols = jnp.transpose(tile_cols[0, 0])
    hidden, ht, inv, parts, grad_weight = layer_call(
        cols,
        features,
        jnp.transpose(counts[0, 0]),
        pos[0, 0],
        keep[0, 0],
        weight,
        bias.reshape(1, 2 * T),
        cot,
        drop,
    )
    back, hidden, grad_weight = place_call(cols, parts, hidden, grad_weight)
    grad_features = sum_row_call(back, ht, inv)
    return hidden, grad_features, grad_weight


def solution(mesh):
    nodes = P(("row", "col"), None)
    block = P("row", "col", None, None)
    return jax.shard_map(
        shards,
        mesh=mesh,
        in_specs=(nodes, P(), P(), nodes, nodes, block, block, block, block),
        out_specs=(nodes, nodes, P()),
        check_vma=False,
    )
```
